32 devices in a mesh: dp: 4 (over x, core), seq: 8 (over z, y).
Axes of the slice: x: 2, y: 2, z: 4, core: 2. Of those that a mesh axis runs over, the one named last changes fastest.
Arguments:
- tokens: bfloat16 [1, 4, 1024, 2048], P(None, 'dp', 'seq'), may hold values from -6 to 6
- segment_ids: int32 [1, 4, 1024], P(None, 'dp', 'seq'), may hold values from 0 to 1, as said below
- out_grad: bfloat16 [1, 4, 1024, 2048], P(None, 'dp', 'seq'), may hold values from -6 to 6
- gain_attn: float32 [2048], replicated, may hold values from 0.5 to 1.5
- gain_mlp: float32 [2048], replicated, may hold values from 0.5 to 1.5
- w_query: bfloat16 [2048, 2048], P(None, 'dp'), may hold values from -0.125 to 0.125
- w_key: bfloat16 [2048, 256], replicated, may hold values from -0.125 to 0.125
- w_value: bfloat16 [2048, 256], replicated, may hold values from -0.125 to 0.125
- w_out: bfloat16 [2048, 2048], P('dp'), may hold values from -0.5 to 0.5
- w_gate: bfloat16 [2048, 16384], P(None, 'dp'), may hold values from -0.125 to 0.125
- w_up: bfloat16 [2048, 16384], P(None, 'dp'), may hold values from -0.125 to 0.125
- w_down: bfloat16 [16384, 2048], P('dp'), may hold values from -0.046875 to 0.046875
- query_adapt: bfloat16 [2048, 256], replicated, may hold values from -0.125 to 0.125
- query_expand: bfloat16 [256, 2048], P(None, 'dp'), may hold values from -0.375 to 0.375
- key_adapt: bfloat16 [2048, 256], replicated, may hold values from -0.125 to 0.125
- key_expand: bfloat16 [256, 256], replicated, may hold values from -0.375 to 0.375
- value_adapt: bfloat16 [2048, 256], replicated, may hold values from -0.125 to 0.125
- value_expand: bfloat16 [256, 256], replicated, may hold values from -0.375 to 0.375
- out_adapt: bfloat16 [2048, 256], P('dp'), may hold values from -0.5 to 0.5
- out_expand: bfloat16 [256, 2048], replicated, may hold values from -0.375 to 0.375
- gate_adapt: bfloat16 [2048, 256], replicated, may hold values from -0.125 to 0.125
- gate_expand: bfloat16 [256, 16384], P(None, 'dp'), may hold values from -0.375 to 0.375
- up_adapt: bfloat16 [2048, 256], replicated, may hold values from -0.125 to 0.125
- up_expand: bfloat16 [256, 16384], P(None, 'dp'), may hold values from -0.375 to 0.375
- down_adapt: bfloat16 [16384, 256], P('dp'), may hold values from -0.046875 to 0.046875
- down_expand: bfloat16 [256, 2048], replicated, may hold values from -0.375 to 0.375
Outputs:
- layer_out: bfloat16 [1, 4, 1024, 2048], P(None, 'dp', 'seq')
- tokens_grad: bfloat16 [1, 4, 1024, 2048], P(None, 'dp', 'seq')
- grad_gain_attn: float32 [2048], P(('dp', 'seq'))
- grad_gain_mlp: float32 [2048], P(('dp', 'seq'))
- grad_w_query: float32 [2048, 2048], P('seq', 'dp')
- grad_w_key: float32 [2048, 256], P(('dp', 'seq'))
- grad_w_value: float32 [2048, 256], P(('dp', 'seq'))
- grad_w_out: float32 [2048, 2048], P('dp', 'seq')
- grad_w_gate: float32 [2048, 16384], P('seq', 'dp')
- grad_w_up: float32 [2048, 16384], P('seq', 'dp')
- grad_w_down: float32 [16384, 2048], P('dp', 'seq')
- grad_query_adapt: float32 [2048, 256], P(('dp', 'seq'))
- grad_query_expand: float32 [256, 2048], P('seq', 'dp')
- grad_key_adapt: float32 [2048, 256], P(('dp', 'seq'))
- grad_key_expand: float32 [256, 256], P(('dp', 'seq'))
- grad_value_adapt: float32 [2048, 256], P(('dp', 'seq'))
- grad_value_expand: float32 [256, 256], P(('dp', 'seq'))
- grad_out_adapt: float32 [2048, 256], P('dp', 'seq')
- grad_out_expand: float32 [256, 2048], P(('dp', 'seq'))
- grad_gate_adapt: float32 [2048, 256], P(('dp', 'seq'))
- grad_gate_expand: float32 [256, 16384], P('seq', 'dp')
- grad_up_adapt: float32 [2048, 256], P(('dp', 'seq'))
- grad_up_expand: float32 [256, 16384], P('seq', 'dp')
- grad_down_adapt: float32 [16384, 256], P('dp', 'seq')
- grad_down_expand: float32 [256, 2048], P(('dp', 'seq'))
The draws below stay inside these ranges and needn't reach their ends.
Inputs may be any that keep to these rules, and one draw needn't show every extreme that they name: `segment_ids`: every sequence holds two documents: document 0 ends within the first 128 tokens, at a place drawn from the seed, and document 1 runs from there to the sequence's end.
All inputs are finite; a program needn't handle non-finite values.
Results may differ from the reference program's by a relative error of at most 0.028.
Values may be sent and summed in bfloat16 or wider, within the bound.
A program may use at most 384 MiB of HBM per device.

```python
import jax
import jax.numpy as jnp
from jax import lax

D = 2048
H = 8
HD = 256
FF = 16384
RANK = 256
MB = 1
SEQ_LEN = 1024
TOK_DEV = 128
SEQS_MB = 4


def draw_segment_ids(key, part):
    folded = jax.random.fold_in(key, 7)
    cuts = jax.random.randint(folded, (MB, SEQS_MB, 1), 1, TOK_DEV + 1)
    places = jnp.arange(SEQ_LEN, dtype=jnp.int32)[None, None, :]
    return (places >= cuts).astype(jnp.int32)


def levels(stream_key, shape, shards, least, top_value):
    gain, own = 1.0, jax.random.fold_in(stream_key, 6)
    for axis_at, shards_of in shards:
        draws = jnp.exp(jax.random.uniform(jax.random.fold_in(own, axis_at), (shards_of,), jnp.float32, least / len(shards), top_value / len(shards)))
        gain = gain * jnp.repeat(draws, shape[axis_at] // shards_of).reshape([-1 if axis == axis_at else 1 for axis in range(len(shape))])
    return gain


def scatter_about(key, shape, width, bound, pieces=(), held_as=jnp.bfloat16):
    gain = levels(key, shape, pieces, -0.22, 0.18) if pieces else 1.0
    array = jax.random.normal(key, shape, jnp.float32) * width * gain
    return jnp.minimum(jnp.maximum(array, -bound), bound).astype(held_as)


def setup_inputs(seed: int = 0) -> dict:
    key_of = jax.random.split(jax.random.key(seed), 27)
    return {
        "tokens": scatter_about(key_of[0], (MB, SEQS_MB, SEQ_LEN, D), 1.0, 6.0, ((1, 4), (2, 8))),
        "segment_ids": draw_segment_ids(jax.random.fold_in(key_of[26], 71), 0),
        "out_grad": scatter_about(key_of[2], (MB, SEQS_MB, SEQ_LEN, D), 1.0, 6.0, ((1, 4), (2, 8))),
        "gain_attn": jnp.clip(1.0 + 0.1 * jax.random.normal(key_of[3], (D,), jnp.float32), 0.5, 1.5),
        "gain_mlp": jnp.clip(1.0 + 0.1 * jax.random.normal(key_of[4], (D,), jnp.float32), 0.5, 1.5),
        "w_query": scatter_about(key_of[5], (D, H * HD), D ** -0.5, 0.125, ((1, 4),)),
        "w_key": scatter_about(key_of[6], (D, HD), D ** -0.5, 0.125),
        "w_value": scatter_about(key_of[7], (D, HD), D ** -0.5, 0.125),
        "w_out": scatter_about(key_of[8], (H * HD, D), (H * HD // 16) ** -0.5, 0.5, ((0, 4),)),
        "w_gate": scatter_about(key_of[9], (D, FF), D ** -0.5, 0.125, ((1, 4),)),
        "w_up": scatter_about(key_of[10], (D, FF), D ** -0.5, 0.125, ((1, 4),)),
        "w_down": scatter_about(key_of[11], (FF, D), FF ** -0.5, 0.046875, ((0, 4),)),
        "query_adapt": scatter_about(key_of[12], (D, RANK), D ** -0.5, 0.125),
        "query_expand": scatter_about(key_of[13], (RANK, H * HD), RANK ** -0.5, 0.375, ((1, 4),)),
        "key_adapt": scatter_about(key_of[14], (D, RANK), D ** -0.5, 0.125),
        "key_expand": scatter_about(key_of[15], (RANK, HD), RANK ** -0.5, 0.375),
        "value_adapt": scatter_about(key_of[16], (D, RANK), D ** -0.5, 0.125),
        "value_expand": scatter_about(key_of[17], (RANK, HD), RANK ** -0.5, 0.375),
        "out_adapt": scatter_about(key_of[18], (H * HD, RANK), (H * HD // 16) ** -0.5, 0.5, ((0, 4),)),
        "out_expand": scatter_about(key_of[19], (RANK, D), RANK ** -0.5, 0.375),
        "gate_adapt": scatter_about(key_of[20], (D, RANK), D ** -0.5, 0.125),
        "gate_expand": scatter_about(key_of[21], (RANK, FF), RANK ** -0.5, 0.375, ((1, 4),)),
        "up_adapt": scatter_about(key_of[22], (D, RANK), D ** -0.5, 0.125),
        "up_expand": scatter_about(key_of[23], (RANK, FF), RANK ** -0.5, 0.375, ((1, 4),)),
        "down_adapt": scatter_about(key_of[24], (FF, RANK), FF ** -0.5, 0.046875, ((0, 4),)),
        "down_expand": scatter_about(key_of[25], (RANK, D), RANK ** -0.5, 0.375),
    }


EPSILON = 1e-06
ROTARY_BASE = 10000.0
MASKED = -1e+30

@jax.custom_vjp
def low(v):
    return lax.optimization_barrier(v.astype(jnp.bfloat16)).astype(jnp.float32)

@jax.custom_vjp
def low_back(v):
    return v

def low_keep(v):
    return (low(v), None)

def low_pass(kept, grad):
    return (grad,)

def back_keep(v):
    return (v, None)

def back_low(kept, grad):
    return (low(grad),)
low.defvjp(low_keep, low_pass)
low_back.defvjp(back_keep, back_low)

def matmul(left, right):
    return jnp.dot(left, right, precision=lax.Precision.HIGHEST, preferred_element_type=jnp.float32)

def rotary(positions, size):
    half_size = size // 2
    frequency = ROTARY_BASE ** (-(jnp.arange(half_size, dtype=jnp.float32) * 2.0) / size)
    angles = positions.astype(jnp.float32)[:, None] * frequency[None, :]
    return (jnp.cos(angles), jnp.sin(angles))

def rotate(values, cosine_table, sine_table):
    half_size = values.shape[-1] // 2
    first_half = values[..., :half_size]
    second_half = values[..., half_size:]
    return jnp.concatenate([first_half * cosine_table - second_half * sine_table, second_half * cosine_table + first_half * sine_table], axis=-1)

def normalize(values, gain_vector):
    inverse_rms = lax.rsqrt(lax.optimization_barrier(jnp.mean(values * values, axis=-1, keepdims=True)) + EPSILON)
    return values * inverse_rms * gain_vector

def block_forward(token_rows, segments, weights):
    gain_attn, gain_mlp, w_query, w_key, w_value, w_out, w_gate, w_up, w_down, query_adapt, query_expand, key_adapt, key_expand, value_adapt, value_expand, out_adapt, out_expand, gate_adapt, gate_expand, up_adapt, up_expand, down_adapt, down_expand = weights
    length = token_rows.shape[0]
    positions = jnp.arange(length, dtype=jnp.int32)
    cosine_table, sine_table = rotary(positions, HD)
    scale_qk = HD ** (-0.5)
    normed_attn = low(normalize(token_rows, gain_attn))
    query_low = low_back(low(matmul(normed_attn, query_adapt)))
    key_low = low_back(low(matmul(normed_attn, key_adapt)))
    value_low = low_back(low(matmul(normed_attn, value_adapt)))
    queries = low_back(matmul(normed_attn, w_query) + matmul(query_low, query_expand))
    key_pre = low_back(matmul(normed_attn, w_key) + matmul(key_low, key_expand))
    value_pre = low_back(matmul(normed_attn, w_value) + matmul(value_low, value_expand))
    query_rot = low(rotate(queries.reshape(length, H, HD), cosine_table[:, None, :], sine_table[:, None, :]))
    key_rot = low(rotate(key_pre, cosine_table, sine_table))
    value_rows = low(value_pre)
    raw_scores = low_back(jnp.einsum('thd,jd->htj', query_rot, key_rot, precision=lax.Precision.HIGHEST) * scale_qk)
    allowed = (positions[None, :] <= positions[:, None]) & (segments[:, None] == segments[None, :])
    scores = jnp.where(allowed[None, :, :], raw_scores, MASKED)
    log_total = jax.nn.logsumexp(scores, axis=-1, keepdims=True)
    prob_low = low(jnp.exp(scores - log_total))
    heads_mixed = jnp.einsum('htj,jd->thd', prob_low, value_rows, precision=lax.Precision.HIGHEST)
    heads_out = low_back(low(heads_mixed.reshape(length, H * HD)))
    out_low = low_back(low(matmul(heads_out, out_adapt)))
    branch = low_back(matmul(heads_out, w_out) + matmul(out_low, out_expand))
    middle = token_rows + branch
    normed_mlp = low(normalize(middle, gain_mlp))
    gate_low = low_back(low(matmul(normed_mlp, gate_adapt)))
    up_low = low_back(low(matmul(normed_mlp, up_adapt)))
    gating = low_back(matmul(normed_mlp, w_gate) + matmul(gate_low, gate_expand))
    lifting = low_back(matmul(normed_mlp, w_up) + matmul(up_low, up_expand))
    mixture = low_back(low(jax.nn.gelu(gating, approximate=True) * lifting))
    down_low = low_back(low(matmul(mixture, down_adapt)))
    branch_mlp = low_back(matmul(mixture, w_down) + matmul(down_low, down_expand))
    return middle + branch_mlp

def reference(tokens, segment_ids, out_grad, gain_attn, gain_mlp, w_query, w_key, w_value, w_out, w_gate, w_up, w_down, query_adapt, query_expand, key_adapt, key_expand, value_adapt, value_expand, out_adapt, out_expand, gate_adapt, gate_expand, up_adapt, up_expand, down_adapt, down_expand):
    weights = tuple((weight.astype(jnp.float32) for weight in (gain_attn, gain_mlp, w_query, w_key, w_value, w_out, w_gate, w_up, w_down, query_adapt, query_expand, key_adapt, key_expand, value_adapt, value_expand, out_adapt, out_expand, gate_adapt, gate_expand, up_adapt, up_expand, down_adapt, down_expand)))
    sequences = tokens.reshape(MB * SEQS_MB, SEQ_LEN, D).astype(jnp.float32)
    documents = segment_ids.reshape(MB * SEQS_MB, SEQ_LEN).astype(jnp.int32)
    cotangents = out_grad.reshape(MB * SEQS_MB, SEQ_LEN, D).astype(jnp.float32)
    initial = tuple((jnp.zeros(weight.shape, jnp.float32) for weight in weights))

    def one_sequence(totals, inputs_row):
        sequence_rows, document_row, cotangent_rows = inputs_row
        result_rows, backward = jax.vjp(lambda rows_in, weights_in: block_forward(rows_in, document_row, weights_in), sequence_rows, weights)
        grad_rows, grad_weights = backward(cotangent_rows)
        totals = tuple((total_now + grad_now for total_now, grad_now in zip(totals, grad_weights)))
        return (totals, (result_rows.astype(jnp.bfloat16), grad_rows.astype(jnp.bfloat16)))
    totals, (results, grad_tokens) = lax.scan(one_sequence, initial, (sequences, documents, cotangents))
    return (results.reshape(tokens.shape), grad_tokens.reshape(tokens.shape), totals[0], totals[1], totals[2], totals[3], totals[4], totals[5], totals[6], totals[7], totals[8], totals[9], totals[10], totals[11], totals[12], totals[13], totals[14], totals[15], totals[16], totals[17], totals[18], totals[19], totals[20], totals[21], totals[22])
```

```python
import itertools
import math

import jax
import jax.numpy as jnp
from jax import lax
from jax.experimental import pallas as pl
from jax.experimental.pallas import tpu as pltpu
from jax.sharding import PartitionSpec as P

HD = 256
EPSILON = 1e-06
ROTARY_BASE = 10000.0
MASKED = -1e30

MESH = pl.DeviceIdType.MESH
BF16 = jnp.bfloat16
F32 = jnp.float32


class Topo:
    def __init__(self, n_dp, n_seq):
        self.n_dp, self.n_seq = n_dp, n_seq
        self.size = {"c": 2, "x": n_dp // 2, "b": n_seq // 4, "l": 2, "h": 2}

    def here(self):
        dp, seq = lax.axis_index("dp"), lax.axis_index("seq")
        nb = self.size["b"]
        outer = lax.div(seq, nb)
        return {
            "c": lax.rem(dp, 2),
            "x": lax.div(dp, 2),
            "b": lax.rem(seq, nb),
            "l": lax.rem(outer, 2),
            "h": lax.div(outer, 2),
        }

    def moved(self, at, dims, offsets, sign=1):
        new = dict(at)
        for dim, offset in zip(dims, offsets):
            n = self.size[dim]
            if offset:
                new[dim] = lax.rem(at[dim] + (offset if sign > 0 else n - offset), n)
        return new

    def seq_of(self, at):
        return (at["h"] * 2 + at["l"]) * self.size["b"] + at["b"]

    def device(self, at):
        return (at["x"] * 2 + at["c"], self.seq_of(at))

    def index(self, at, group):
        dp, seq = self.device(at)
        if group == "all":
            return dp * self.n_seq + seq
        if group == "half":
            nb = self.size["b"]
            return dp * (2 * nb) + at["l"] * nb + at["b"]
        if group == "dp":
            return dp
        if group == "seq":
            return seq
        if group == "quad":
            return at["l"] * self.size["b"] + at["b"]
        raise ValueError(group)

    def group_size(self, group):
        nb = self.size["b"]
        return {
            "all": self.n_dp * self.n_seq,
            "half": self.n_dp * 2 * nb,
            "dp": self.n_dp,
            "seq": self.n_seq,
            "quad": 2 * nb,
        }[group]


GROUP_DIMS = {"all": "cxblh", "half": "cxbl", "dp": "cx", "seq": "blh", "quad": "bl"}


def remote(src, dst, send_sem, recv_sem, device):
    return pltpu.make_async_remote_copy(
        src_ref=src,
        dst_ref=dst,
        send_sem=send_sem,
        recv_sem=recv_sem,
        device_id=device,
        device_id_type=MESH,
    )


class Gather:
    def __init__(self, topo, group, x, parts):
        self.topo, self.group, self.parts = topo, group, parts
        self.inputs = [x]
        rows, cols = x.shape
        self.outputs = [jax.ShapeDtypeStruct((topo.group_size(group), rows, cols), x.dtype)]
        self.out_specs = [pl.BlockSpec(memory_space=pl.ANY)]
        self.in_specs = [pl.BlockSpec(memory_space=pl.ANY)]
        n = topo.group_size(group)
        self.scratch = [
            pltpu.SemaphoreType.DMA((len(parts), n)),
            pltpu.SemaphoreType.DMA((len(parts), n)),
            pltpu.SemaphoreType.DMA(()),
        ]

    def peers(self):
        return {
            ((dim, d),) for dim in GROUP_DIMS[self.group] for d in range(1, self.topo.size[dim])
        }

    def run(self, ins, outs, scratch):
        topo = self.topo
        (x_ref,), (out_ref,) = ins, outs
        send_sem, recv_sem, own_sem = scratch
        at = topo.here()
        own = pltpu.make_async_copy(x_ref, out_ref.at[topo.index(at, self.group)], own_sem)
        own.start()
        started = []

        def key_index(order, key):
            k = 0
            for dim, o in zip(order, key):
                k = k * topo.size[dim] + o
            return k

        def copy(part, order, row, rows, key, stage, d):
            origin = topo.moved(at, order, key, -1)
            slot = topo.index(origin, self.group)
            new_key = tuple(d if i == stage else o for i, o in enumerate(key))
            src = (
                x_ref.at[pl.ds(row, rows)]
                if not any(key)
                else out_ref.at[slot, pl.ds(row, rows)]
            )
            k = key_index(order, new_key)
            target = topo.device(topo.moved(at, [order[stage]], [d]))
            return remote(
                src,
                out_ref.at[slot, pl.ds(row, rows)],
                send_sem.at[part, k],
                recv_sem.at[part, k],
                target,
            )

        work = []
        for part, (row, rows, order) in enumerate(self.parts):
            sizes = [topo.size[dim] for dim in order]
            keys = list(itertools.product(*[range(s) for s in sizes]))
            last = {k: max([i for i, o in enumerate(k) if o], default=-1) for k in keys}
            hops = {k: sum(1 for o in k if o) for k in keys}
            for k in keys:
                work.append((hops[k], last[k], part, row, rows, order, k))
        work.sort(key=lambda w: (w[0], w[1], w[2]))
        for hops, last, part, row, rows, order, key in work:
            if hops:
                slot = topo.index(topo.moved(at, order, key, -1), self.group)
                k = key_index(order, key)
                dst = out_ref.at[slot, pl.ds(row, rows)]
                remote(dst, dst, send_sem.at[part, k], recv_sem.at[part, k], topo.device(at)).wait_recv()
            for stage in range(last + 1, len(order)):
                for d in range(1, topo.size[order[stage]]):
                    cp = copy(part, order, row, rows, key, stage, d)
                    cp.start()
                    started.append(cp)
            yield
        for cp in started:
            cp.wait_send()
        own.wait()


class Scatter:
    def __init__(self, topo, group, x, parts, out_dtype=None):
        self.topo, self.group, self.parts = topo, group, parts
        self.inputs = [x]
        n, rows, cols = x.shape
        assert n == topo.group_size(group), (n, group)
        self.outputs = [jax.ShapeDtypeStruct((rows, cols), out_dtype or F32)]
        self.in_specs = [pl.BlockSpec(memory_space=pl.ANY)]
        self.out_specs = [pl.BlockSpec(memory_space=pltpu.VMEM)]
        self.scratch = []
        for row, nrows, order in parts:
            sizes = [topo.size[dim] for dim in order]
            keep = math.prod(sizes[1:])
            self.scratch.append(pltpu.VMEM((keep, nrows, cols), x.dtype))
            self.scratch.append(pltpu.SemaphoreType.DMA((keep,)))
            for k, s in enumerate(sizes):
                rest = math.prod(sizes[k + 1 :])
                self.scratch.append(pltpu.VMEM((max(s - 1, 1), rest, nrows, cols), x.dtype))
                self.scratch.append(pltpu.SemaphoreType.DMA((max(s - 1, 1), rest)))
                self.scratch.append(pltpu.SemaphoreType.DMA((max(s - 1, 1), rest)))

    def peers(self):
        return {
            ((dim, d),) for dim in GROUP_DIMS[self.group] for d in range(1, self.topo.size[dim])
        }

    def run(self, ins, outs, scratch):
        topo = self.topo
        (x_ref,), (out_ref,) = ins, outs
        at = topo.here()
        scratch = list(scratch)
        started, jobs = [], []
        for part, (row, nrows, order) in enumerate(self.parts):
            sizes = [topo.size[dim] for dim in order]
            acc, own_sem = scratch.pop(0), scratch.pop(0)
            bufs = [(scratch.pop(0), scratch.pop(0), scratch.pop(0)) for _ in sizes]

            def flat(key, start, sizes=sizes):
                k = 0
                for o, s in zip(key[start:], sizes[start:]):
                    k = k * s + o
                return k

            keys = list(itertools.product(*[range(s) for s in sizes]))
            first = {k: min([i for i, o in enumerate(k) if o], default=len(sizes)) for k in keys}
            keys.sort(key=lambda k: (first[k], [0 if o else 1 for o in k]))
            for key in keys:
                jobs.append((first[key], part, row, nrows, order, sizes, acc, own_sem, bufs, flat, key))
        jobs.sort(key=lambda j: j[0])

        def out_copy(job, src, key, stage):
            _, part, row, nrows, order, sizes, acc, own_sem, bufs, flat, _ = job
            buf, send_sem, recv_sem = bufs[stage]
            d = key[stage]
            k = flat(key, stage + 1)
            target = topo.device(topo.moved(at, [order[stage]], [d]))
            return remote(src, buf.at[d - 1, k], send_sem.at[d - 1, k], recv_sem.at[d - 1, k], target)

        for job in jobs:
            first, part, row, nrows, order, sizes, acc, own_sem, bufs, flat, key = job
            block = topo.index(topo.moved(at, order, key), self.group)
            if first == 0:
                cp = out_copy(job, x_ref.at[block, pl.ds(row, nrows)], key, 0)
                cp.start()
                started.append(cp)
        yield
        for job in jobs:
            first, part, row, nrows, order, sizes, acc, own_sem, bufs, flat, key = job
            if first > 0:
                block = topo.index(topo.moved(at, order, key), self.group)
                k = flat(key, 1)
                pltpu.make_async_copy(
                    x_ref.at[block, pl.ds(row, nrows)], acc.at[k], own_sem.at[k]
                ).start()
        yield
        for job in jobs:
            first, part, row, nrows, order, sizes, acc, own_sem, bufs, flat, key = job
            if first == 0:
                continue
            kk = flat(key, 1)
            block = topo.index(topo.moved(at, order, key), self.group)
            pltpu.make_async_copy(
                x_ref.at[block, pl.ds(row, nrows)], acc.at[kk], own_sem.at[kk]
            ).wait()
            terms = []
            for stage in range(first):
                buf, send_sem, recv_sem = bufs[stage]
                k = flat(key, stage + 1)
                for d in range(1, sizes[stage]):
                    ref = buf.at[d - 1, k]
                    remote(ref, ref, send_sem.at[d - 1, k], recv_sem.at[d - 1, k], topo.device(at)).wait_recv()
                    terms.append((buf, d - 1, k))
            step = 16 if nrows % 16 == 0 else 8
            final = first == len(sizes)

            def add(r, _, terms=terms, acc=acc, kk=kk, final=final, row=row, step=step):
                r0 = pl.multiple_of(r * step, step)
                total = acc[kk, pl.ds(r0, step), :].astype(F32)
                for buf, d, k in terms:
                    total = total + buf[d, k, pl.ds(r0, step), :].astype(F32)
                if final:
                    out_ref[pl.ds(row + r0, step), :] = total.astype(out_ref.dtype)
                else:
                    acc[kk, pl.ds(r0, step), :] = total.astype(acc.dtype)
                return 0

            lax.fori_loop(0, nrows // step, add, 0)
            if not final:
                cp = out_copy(job, acc.at[kk], key, first)
                cp.start()
                started.append(cp)
            yield
        for cp in started:
            cp.wait_send()


class Exchange:
    def __init__(self, topo, group, x):
        self.topo, self.group = topo, group
        self.inputs = [x]
        n = x.shape[0]
        assert n == topo.group_size(group)
        self.outputs = [jax.ShapeDtypeStruct(x.shape, x.dtype)]
        self.in_specs = [pl.BlockSpec(memory_space=pl.ANY)]
        self.out_specs = [pl.BlockSpec(memory_space=pl.ANY)]
        self.scratch = [
            pltpu.SemaphoreType.DMA((n,)),
            pltpu.SemaphoreType.DMA((n,)),
            pltpu.SemaphoreType.DMA(()),
        ]

    def offsets(self):
        dims = GROUP_DIMS[self.group]
        return dims, [
            o for o in itertools.product(*[range(self.topo.size[d]) for d in dims]) if any(o)
        ]

    def peers(self):
        dims, offsets = self.offsets()
        return {tuple((dim, o) for dim, o in zip(dims, off) if o) for off in offsets}

    def run(self, ins, outs, scratch):
        topo = self.topo
        (x_ref,), (out_ref,) = ins, outs
        send_sem, recv_sem, own_sem = scratch
        at = topo.here()
        me = topo.index(at, self.group)
        own = pltpu.make_async_copy(x_ref.at[me], out_ref.at[me], own_sem)
        own.start()
        dims, offsets = self.offsets()
        started = []
        for i, off in enumerate(offsets):
            there = topo.moved(at, dims, off)
            cp = remote(
                x_ref.at[topo.index(there, self.group)],
                out_ref.at[me],
                send_sem.at[i],
                recv_sem.at[i],
                topo.device(there),
            )
            cp.start()
            started.append(cp)
        yield
        for i, off in enumerate(offsets):
            ref = out_ref.at[topo.index(topo.moved(at, dims, off, -1), self.group)]
            remote(ref, ref, send_sem.at[i], recv_sem.at[i], topo.device(at)).wait_recv()
            yield
        for cp in started:
            cp.wait_send()
        own.wait()


class Finish:
    def __init__(self, topo, x, y):
        self.topo = topo
        self.inputs = [x, y]
        self.outputs = [
            jax.ShapeDtypeStruct(x.shape, x.dtype),
            jax.ShapeDtypeStruct(y.shape, y.dtype),
        ]
        self.in_specs = [pl.BlockSpec(memory_space=pl.ANY)] * 2
        self.out_specs = [pl.BlockSpec(memory_space=pl.ANY)] * 2
        self.inner = Exchange(topo, "seq", y)
        self.scratch = self.inner.scratch + [
            pltpu.SemaphoreType.DMA(()),
            pltpu.SemaphoreType.DMA(()),
            pltpu.SemaphoreType.DMA(()),
        ]

    def peers(self):
        return self.inner.peers()

    def route(self):
        topo = self.topo
        dp, seq = lax.axis_index("dp"), lax.axis_index("seq")
        n = seq * topo.n_dp + dp
        target = (lax.div(n, topo.n_seq), lax.rem(n, topo.n_seq))
        m = dp * topo.n_seq + seq
        source = (lax.rem(m, topo.n_dp), lax.div(m, topo.n_dp))
        stays = (target[0] == dp) & (target[1] == seq)
        return target, source, stays

    def greet(self, barrier):
        target, source, stays = self.route()

        @pl.when(jnp.logical_not(stays))
        def _():
            pl.semaphore_signal(barrier, inc=1, device_id=source, device_id_type=MESH)

        return jnp.where(stays, 0, 1)

    def run(self, ins, outs, scratch):
        (x_ref, y_ref), (x_out, y_out) = ins, outs
        send_sem, recv_sem, own_sem = scratch[3:]
        target, source, stays = self.route()
        cp = remote(x_ref, x_out, send_sem, recv_sem, target)
        own = pltpu.make_async_copy(x_ref, x_out, own_sem)

        @pl.when(stays)
        def _():
            own.start()

        @pl.when(jnp.logical_not(stays))
        def _():
            cp.start()

        yield from self.inner.run([y_ref], [y_out], scratch[:3])

        @pl.when(stays)
        def _():
            own.wait()

        @pl.when(jnp.logical_not(stays))
        def _():
            cp.wait()


def communicate(topo, name, collective_id, *ops):
    n_in = [len(op.inputs) for op in ops]
    n_out = [len(op.outputs) for op in ops]
    n_scratch = [len(op.scratch) for op in ops]

    def kernel(*refs):
        refs = list(refs)
        take = lambda counts: [[refs.pop(0) for _ in range(k)] for k in counts]
        ins, outs, scratch = take(n_in), take(n_out), take(n_scratch)
        at = topo.here()
        peers = sorted(set().union(*[op.peers() for op in ops]))
        barrier = pltpu.get_barrier_semaphore()
        for peer in peers:
            there = topo.device(topo.moved(at, [p[0] for p in peer], [p[1] for p in peer]))
            pl.semaphore_signal(barrier, inc=1, device_id=there, device_id_type=MESH)
        greeted = len(peers)
        for op in ops:
            if hasattr(op, "greet"):
                greeted = greeted + op.greet(barrier)
        pl.semaphore_wait(barrier, greeted)
        running = [op.run(i, o, s) for op, i, o, s in zip(ops, ins, outs, scratch)]
        while running:
            for step in list(running):
                try:
                    next(step)
                except StopIteration:
                    running.remove(step)

    results = pl.pallas_call(
        kernel,
        name=name,
        out_shape=[s for op in ops for s in op.outputs],
        in_specs=[s for op in ops for s in op.in_specs],
        out_specs=[s for op in ops for s in op.out_specs],
        scratch_shapes=[s for op in ops for s in op.scratch],
        compiler_params=pltpu.CompilerParams(
            collective_id=collective_id, has_side_effects=True, vmem_limit_bytes=58 << 20
        ),
    )(*[x for op in ops for x in op.inputs])
    results = list(results)
    return [[results.pop(0) for _ in range(k)] for k in n_out]


def row_parts(rows, orders, weights, step=16):
    parts, row, total = [], 0, sum(weights)
    for i, (order, weight) in enumerate(zip(orders, weights)):
        n = rows - row if i == len(orders) - 1 else min(rows - row, int(round(rows * weight / total / step)) * step)
        if n:
            parts.append((row, n, order))
            row += n
    return parts


def matmul(left, right):
    return jnp.dot(left, right, preferred_element_type=jnp.float32)


def contract(form, left, right):
    return jnp.einsum(form, left, right, preferred_element_type=jnp.float32)


def rotary(positions, size):
    half_size = size // 2
    frequency = ROTARY_BASE ** (-(jnp.arange(half_size, dtype=jnp.float32) * 2.0) / size)
    angles = positions.astype(jnp.float32)[:, None] * frequency[None, :]
    return (jnp.cos(angles), jnp.sin(angles))


def rotate(values, cosine_table, sine_table):
    half_size = values.shape[-1] // 2
    first_half = values[..., :half_size]
    second_half = values[..., half_size:]
    return jnp.concatenate(
        [
            first_half * cosine_table - second_half * sine_table,
            second_half * cosine_table + first_half * sine_table,
        ],
        axis=-1,
    )


def normalize(values, gain_vector):
    inverse_rms = lax.rsqrt(jnp.mean(values * values, axis=-1, keepdims=True) + EPSILON)
    unit_rows = values * inverse_rms
    return (unit_rows * gain_vector, unit_rows, inverse_rms)


def norm_backward(grad_normed, unit_rows, inverse_rms, gain_vector):
    gain_term = jnp.sum(grad_normed * unit_rows, axis=0)
    grad_unit = grad_normed * gain_vector
    inner = jnp.mean(grad_unit * unit_rows, axis=-1, keepdims=True)
    return (gain_term, inverse_rms * (grad_unit - unit_rows * inner))


def dot_t(left, right):
    return lax.dot_general(left, right, (((1,), (1,)), ((), ())), preferred_element_type=F32)


def t_dot(left, right):
    return lax.dot_general(left, right, (((0,), (0,)), ((), ())), preferred_element_type=F32)


GELU_C = math.sqrt(2.0 / math.pi)


def gelu_parts(v):
    square = v * v
    t = jnp.tanh(GELU_C * (v + 0.044715 * v * square))
    half_up = 0.5 * (1.0 + t)
    slope = half_up + 0.5 * v * (1.0 - t * t) * (GELU_C * (1.0 + 3.0 * 0.044715 * square))
    return v * half_up, slope


def feed_forward(topo, normed_all, grad_all, w_gate, w_up, w_down, low_gu, low_d, high):
    tokens, width = normed_all.shape
    units = w_gate.shape[1]
    ranks = low_d.shape[0]
    quad = topo.group_size("quad")
    half_width = width // 2
    d_rows, r_rows = half_width // quad, ranks // quad
    tile = 512
    run = (topo.n_seq // 2) * 128 // tile
    own = tokens // tile // 2
    block = 256

    def chunk(t, high_ref):
        mine = t < own
        k = jnp.where(mine, t, t - own)
        side = jnp.where(mine, high_ref[0], 1 - high_ref[0])
        return lax.div(k, run) * 2 * run + side * run + lax.rem(k, run)

    def kernel(
        high_ref, n_ref, g_ref, wg_ref, wu_ref, wd_ref, lgu_ref, ld_ref,
        down_ref, gn_ref, dg_ref, du_ref, dd_ref,
        acc_g, acc_u, acc_d, mix_s, gg_s, gu_s,
    ):
        t = pl.program_id(0)

        @pl.when(t == 0)
        def _():
            acc_g[...] = jnp.zeros_like(acc_g)
            acc_u[...] = jnp.zeros_like(acc_u)
            acc_d[...] = jnp.zeros_like(acc_d)

        low = matmul(n_ref[...], lgu_ref[...])
        low_g = low[:, :ranks].astype(BF16)
        low_u = low[:, ranks:].astype(BF16)
        low_b = dot_t(g_ref[...], ld_ref[...]).astype(BF16)

        def one(i, _):
            cols = pl.ds(pl.multiple_of(i * block, block), block)
            gate = matmul(n_ref[...], wg_ref[:, cols])
            up = matmul(n_ref[...], wu_ref[:, cols])
            act, slope = gelu_parts(gate)
            gm = dot_t(g_ref[...], wd_ref[cols, :])
            mix_s[:, cols] = (act * up).astype(BF16)
            gg_s[:, cols] = (gm * up * slope).astype(BF16)
            gu_s[:, cols] = (gm * act).astype(BF16)
            return 0

        lax.fori_loop(0, units // block, one, 0)

        @pl.when(t < own)
        def _():
            def two(i, _):
                cols = pl.ds(pl.multiple_of(i * block, block), block)
                down_ref[:, cols] = matmul(mix_s[...], wd_ref[:, cols]).astype(BF16)
                gn_ref[:, cols] = (
                    dot_t(gg_s[...], wg_ref[cols, :]) + dot_t(gu_s[...], wu_ref[cols, :])
                ).astype(BF16)
                return 0

            lax.fori_loop(0, width // block, two, 0)

        for acc, low_rows, grads in ((acc_g, low_g, gg_s), (acc_u, low_u, gu_s), (acc_d, low_b, mix_s)):
            acc[half_width:, :] += t_dot(low_rows, grads[...])

        def three(i, _):
            rows = pl.ds(pl.multiple_of(i * block, block), block)
            cols = pl.ds(pl.multiple_of(high_ref[0] * half_width + i * block, block), block)
            acc_g[rows, :] += t_dot(n_ref[:, cols], gg_s[...])
            acc_u[rows, :] += t_dot(n_ref[:, cols], gu_s[...])
            acc_d[rows, :] += t_dot(g_ref[:, cols], mix_s[...])
            return 0

        lax.fori_loop(0, half_width // block, three, 0)

        @pl.when(t == pl.num_programs(0) - 1)
        def _():
            for acc, out in ((acc_g, dg_ref), (acc_u, du_ref), (acc_d, dd_ref)):
                for q in range(quad):
                    out[q, :d_rows, :] = acc[q * d_rows : (q + 1) * d_rows, :].astype(BF16)
                    out[q, d_rows:, :] = acc[
                        half_width + q * r_rows : half_width + (q + 1) * r_rows, :
                    ].astype(BF16)

    whole = lambda t, h: (0, 0)
    once = pl.Buffered(1)
    grads = jax.ShapeDtypeStruct((quad, d_rows + r_rows, units), BF16)
    grad_spec = pl.BlockSpec((quad, d_rows + r_rows, units), lambda t, h: (0, 0, 0), pipeline_mode=once)
    part = jax.ShapeDtypeStruct((tokens // 2, width), BF16)
    part_spec = pl.BlockSpec((tile, width), lambda t, h: (jnp.minimum(t, own - 1), 0))
    row_spec = pl.BlockSpec((tile, width), lambda t, h: (chunk(t, h), 0))
    flops = 2 * tokens * units * width * 9
    return pl.pallas_call(
        kernel,
        name="feed_forward",
        grid_spec=pltpu.PrefetchScalarGridSpec(
            num_scalar_prefetch=1,
            grid=(2 * own,),
            in_specs=[
                row_spec,
                row_spec,
                pl.BlockSpec((width, units), whole, pipeline_mode=once),
                pl.BlockSpec((width, units), whole, pipeline_mode=once),
                pl.BlockSpec((units, width), whole, pipeline_mode=once),
                pl.BlockSpec((width, 2 * ranks), whole, pipeline_mode=once),
                pl.BlockSpec((ranks, width), whole, pipeline_mode=once),
            ],
            out_specs=[part_spec, part_spec, grad_spec, grad_spec, grad_spec],
            scratch_shapes=[
                pltpu.VMEM((half_width + ranks, units), F32),
                pltpu.VMEM((half_width + ranks, units), F32),
                pltpu.VMEM((half_width + ranks, units), F32),
                pltpu.VMEM((tile, units), BF16),
                pltpu.VMEM((tile, units), BF16),
                pltpu.VMEM((tile, units), BF16),
            ],
        ),
        out_shape=[part, part, grads, grads, grads],
        compiler_params=pltpu.CompilerParams(vmem_limit_bytes=60 << 20),
        cost_estimate=pl.CostEstimate(flops=flops, bytes_accessed=4 * tokens * width, transcendentals=0),
    )(high, normed_all, grad_all, w_gate, w_up, w_down, low_gu, low_d)


def local(
    topo,
    tokens, segment_ids, out_grad, gain_attn, gain_mlp, w_query, w_key, w_value, w_out, w_gate, w_up, w_down,
    query_adapt, query_expand, key_adapt, key_expand, value_adapt, value_expand, out_adapt, out_expand,
    gate_adapt, gate_expand, up_adapt, up_expand, down_adapt, down_expand,
):
    rows, width = tokens.shape[2], tokens.shape[3]
    groups, n_seq = topo.n_dp, topo.n_seq
    length = rows * n_seq
    heads_dev = w_query.shape[1] // HD
    head_cols = heads_dev * HD
    rank = query_adapt.shape[1]
    scale_qk = HD ** (-0.5)
    quad = topo.group_size("quad")
    units = w_gate.shape[1] // quad
    seq = lax.axis_index("seq")
    dp = lax.axis_index("dp")
    high = lax.div(seq, quad)
    member = lax.rem(seq, quad)

    def merged(weight, adapt, expand):
        return (weight.astype(F32) + matmul(adapt, expand)).astype(BF16)

    def unit_cols(a):
        return lax.dynamic_slice_in_dim(a, member * units, units, 1)

    def unit_rows(a):
        return lax.dynamic_slice_in_dim(a, member * units, units, 0)

    wq = merged(w_query, query_adapt, query_expand)
    wk = merged(w_key, key_adapt, key_expand)
    wv = merged(w_value, value_adapt, value_expand)
    wo = merged(w_out, out_adapt, out_expand)
    wg = merged(unit_cols(w_gate), gate_adapt, unit_cols(gate_expand))
    wu = merged(unit_cols(w_up), up_adapt, unit_cols(up_expand))
    wd = merged(unit_rows(w_down), unit_rows(down_adapt), down_expand)
    half_rank = rank // 2
    my_ranks = lambda a, axis: lax.dynamic_slice_in_dim(a, high * half_rank, half_rank, axis)
    low_gu = jnp.concatenate([my_ranks(gate_adapt, 1), my_ranks(up_adapt, 1)], axis=1)
    low_d = my_ranks(down_expand, 0)

    token_rows = tokens[0, 0].astype(F32)
    grad_rows_in = out_grad[0, 0]
    normed, unit_attn, rms_attn = normalize(token_rows, gain_attn)
    normed_attn = normed.astype(BF16)
    positions = seq * rows + jnp.arange(rows, dtype=jnp.int32)
    cosine_table, sine_table = rotary(positions, HD)
    cosine_heads, sine_heads = cosine_table[:, None, :], sine_table[:, None, :]
    key_rot = rotate(matmul(normed_attn, wk), cosine_table, sine_table).astype(BF16)
    value_rows = matmul(normed_attn, wv).astype(BF16)
    key_value = jnp.concatenate([key_rot, value_rows], axis=1)
    seg_rows = jnp.zeros((16, rows), F32).at[0].set(segment_ids[0, 0].astype(F32))

    zyx, xzy = "lhbxc", "xlhbc"
    (normed_all,), (kv_all,), (seg_all,), (grad_all,) = communicate(
        topo, "gather_attention", 0,
        Gather(topo, "dp", normed_attn, [(0, rows, "xc")]),
        Gather(topo, "all", key_value, row_parts(rows, (zyx, xzy), (7, 4))),
        Gather(topo, "all", seg_rows, [(0, 16, zyx)]),
        Gather(topo, "all", grad_rows_in, row_parts(rows, (zyx, xzy), (7, 4))),
    )
    kv_all = kv_all.reshape(groups, length, 2 * HD)
    keys_all, values_all = kv_all[..., :HD], kv_all[..., HD:]
    segments = seg_all[:, 0, :].reshape(groups, length)
    own_segments = lax.dynamic_slice_in_dim(segments, seq * rows, rows, 1)
    key_positions = jnp.arange(length, dtype=jnp.int32)
    causal = (key_positions[None, :] <= positions[:, None])[None, :, :]
    allowed = (causal & (own_segments[:, :, None] == segments[:, None, :]))[:, None, :, :]

    queries = matmul(normed_all.reshape(groups * rows, width), wq)
    query_rot = rotate(queries.reshape(groups, rows, heads_dev, HD), cosine_heads, sine_heads).astype(BF16)
    scores = jnp.where(allowed, contract("sthd,sjd->shtj", query_rot, keys_all) * scale_qk, MASKED)
    row_top = jnp.max(scores, axis=-1, keepdims=True)
    log_total = row_top + jnp.log(jnp.sum(jnp.exp(scores - row_top), axis=-1, keepdims=True))
    prob_low = jnp.exp(scores - log_total).astype(BF16)
    heads_out = (
        contract("shtj,sjd->sthd", prob_low, values_all).reshape(groups * rows, head_cols).astype(BF16)
    )
    out_part = matmul(heads_out, wo).astype(BF16).reshape(groups, rows, width)
    (out_sum,), = communicate(
        topo, "sum_attention", 1, Scatter(topo, "dp", out_part, [(0, rows, "cx")])
    )
    middle = token_rows + out_sum
    normed, unit_mlp, rms_mlp = normalize(middle, gain_mlp)
    normed_mlp = normed.astype(BF16)
    (mlp_all,), = communicate(
        topo, "gather_mlp", 2, Gather(topo, "all", normed_mlp, row_parts(rows, (zyx, xzy), (7, 4)))
    )
    flat = lambda a: a.reshape(-1, width)
    down_part, gn_part, dg, du, dd = feed_forward(
        topo, flat(mlp_all), flat(grad_all), wg, wu, wd, low_gu, low_d, high.reshape(1)
    )
    half = topo.group_size("half")
    blocks = lambda a: a.reshape(half, rows, width)
    thirds = row_parts(rows, ("cxbl", "cblx", "clxb"), (1, 1, 1))
    down_op = Scatter(topo, "half", blocks(down_part), thirds)
    gn_op = Scatter(topo, "half", blocks(gn_part), thirds)
    if half > 16:
        (gn_sum,), = communicate(topo, "sum_mlp", 3, gn_op)
        (down_sum,), = communicate(topo, "sum_down", 10, down_op)
    else:
        (down_sum,), (gn_sum,) = communicate(topo, "sum_mlp", 3, down_op, gn_op)
    result_rows = (middle + down_sum).astype(BF16)
    gain_mlp_term, grad_from_mlp = norm_backward(gn_sum, unit_mlp, rms_mlp, gain_mlp)
    grad_middle = grad_rows_in.astype(F32) + grad_from_mlp
    grad_branch_attn = grad_middle.astype(BF16)
    (grad_attn_all,), (dg,), (du,), (dd,) = communicate(
        topo, "gather_back", 4,
        Gather(topo, "dp", grad_branch_attn, [(0, rows, "xc")]),
        Exchange(topo, "quad", dg),
        Exchange(topo, "quad", du),
        Exchange(topo, "quad", dd),
    )
    grad_attn_all = grad_attn_all.reshape(groups * rows, width)
    grad_heads = dot_t(grad_attn_all, wo).astype(BF16)
    grad_heads_split = grad_heads.reshape(groups, rows, heads_dev, HD)
    scores_again = jnp.where(allowed, contract("sthd,sjd->shtj", query_rot, keys_all) * scale_qk, MASKED)
    probabilities = jnp.exp(scores_again - log_total)
    grad_values_part = contract("shtj,sthd->sjd", probabilities.astype(BF16), grad_heads_split)
    grad_probs = contract("sthd,sjd->shtj", grad_heads_split, values_all)
    delta_rows = jnp.sum(probabilities * grad_probs, axis=-1, keepdims=True)
    grad_scores = (probabilities * (grad_probs - delta_rows)).astype(BF16)
    grad_query_rot = contract("shtj,sjd->sthd", grad_scores, keys_all) * scale_qk
    grad_keys_part = contract("shtj,sthd->sjd", grad_scores, query_rot) * scale_qk
    grad_query = (
        rotate(grad_query_rot, cosine_heads, -sine_heads).reshape(groups * rows, head_cols).astype(BF16)
    )
    gn_attn_part = dot_t(grad_query, wq).astype(BF16).reshape(groups, rows, width)
    grad_kv_part = jnp.concatenate([grad_keys_part, grad_values_part], axis=-1).astype(BF16)
    (gn_attn_sum,), (grad_kv_sum,) = communicate(
        topo, "sum_back", 5,
        Scatter(topo, "dp", gn_attn_part, [(0, rows, "cx")]),
        Scatter(
            topo, "all", grad_kv_part.reshape(groups * n_seq, rows, 2 * HD),
            row_parts(rows, ("cxblh", "cblhx"), (1, 1)),
        ),
    )
    grad_key = rotate(grad_kv_sum[:, :HD], cosine_table, -sine_table).astype(BF16)
    grad_value = grad_kv_sum[:, HD:].astype(BF16)
    grad_normed_attn = gn_attn_sum + dot_t(grad_key, wk) + dot_t(grad_value, wv)
    gain_attn_term, grad_from_attn = norm_backward(grad_normed_attn, unit_attn, rms_attn, gain_attn)
    grad_rows = (grad_middle + grad_from_attn).astype(BF16)

    (grad_kv_group,), = communicate(
        topo, "gather_kv", 6,
        Gather(topo, "dp", jnp.concatenate([grad_key, grad_value], axis=1), [(0, rows, "xc")]),
    )
    grad_kv_group = grad_kv_group.reshape(groups * rows, 2 * HD)
    normed_group = normed_all.reshape(groups * rows, width)
    query_low = matmul(normed_group, query_adapt).astype(BF16)
    grad_out_low = dot_t(grad_attn_all, out_expand).astype(BF16)
    d_rows, r_rows = width // n_seq, rank // n_seq
    per_dev_d, per_dev_r = d_rows // groups, r_rows // groups
    cols = lax.dynamic_slice_in_dim(normed_group, dp * (width // groups), width // groups, 1)
    my_kv_ranks = lambda a: lax.dynamic_slice_in_dim(a, dp * (rank // groups), rank // groups, 1)
    key_low = matmul(normed_group, my_kv_ranks(key_adapt)).astype(BF16)
    value_low = matmul(normed_group, my_kv_ranks(value_adapt)).astype(BF16)
    kv_weight = t_dot(cols, grad_kv_group)
    kv_expand = jnp.concatenate(
        [t_dot(key_low, grad_kv_group[:, :HD]), t_dot(value_low, grad_kv_group[:, HD:])], axis=1
    )
    by_seq = lambda a: a.reshape(n_seq, -1, a.shape[-1])
    widen = lambda a: jnp.pad(a, ((0, 0), (0, 0), (0, 2 * HD - a.shape[-1])))
    fold = lambda a: a if a.shape[-1] == 2 * HD else widen(a)
    gains = jnp.stack([gain_attn_term, gain_mlp_term]).reshape(2, n_seq, d_rows).transpose(1, 0, 2)
    gains = jnp.pad(gains, ((0, 0), (0, 6), (0, 2 * HD - d_rows)))
    pieces = [
        fold(by_seq(t_dot(normed_group, grad_query))),
        fold(by_seq(t_dot(query_low, grad_query))),
        fold(by_seq(t_dot(grad_attn_all, heads_out))),
        fold(by_seq(t_dot(grad_out_low, heads_out))),
        by_seq(kv_weight),
        by_seq(kv_expand),
        gains,
    ]
    sizes = [p.shape[1] for p in pieces]
    fill = -sum(sizes) % 16
    stacked = jnp.concatenate(
        [p.astype(BF16) for p in pieces] + [jnp.zeros((n_seq, fill, 2 * HD), BF16)], axis=1
    )
    (weights,), = communicate(
        topo, "sum_weights", 7,
        Scatter(topo, "seq", stacked, row_parts(stacked.shape[1], ("blh", "lhb"), (9, 4))),
    )
    starts = [sum(sizes[:i]) for i in range(len(sizes))]
    grad_wq, grad_qe, grad_wo, grad_oa, grad_wkv, grad_kve, gains = [
        weights[a : a + s] for a, s in zip(starts, sizes)
    ]
    grad_wq, grad_qe = grad_wq[:, :head_cols], grad_qe[:, :head_cols]
    grad_wo, grad_oa = grad_wo[:, :head_cols].T, grad_oa[:, :head_cols].T

    def unfold(a):
        full = a.astype(F32).transpose(1, 0, 2).reshape(d_rows + r_rows, quad * units)
        return full[:d_rows], full[d_rows:]

    grad_wg, grad_ge = unfold(dg)
    grad_wu, grad_ue = unfold(du)
    grad_wd_t, grad_da_t = unfold(dd)
    grad_wd, grad_da = grad_wd_t.T, grad_da_t.T

    adapt = jnp.stack(
        [
            dot_t(grad_wg.astype(BF16), gate_expand),
            dot_t(grad_wu.astype(BF16), up_expand),
            dot_t(grad_wq.astype(BF16), query_expand),
        ]
    )
    expand = jnp.stack(
        [
            matmul(down_adapt.T, grad_wd.astype(BF16)),
            matmul(out_adapt.T, grad_wo.astype(BF16)),
        ]
    )
    adapt = adapt.reshape(3, groups, per_dev_d, rank).transpose(1, 0, 2, 3).reshape(groups, -1, rank)
    expand = expand.reshape(2, groups, rank // groups, d_rows).transpose(1, 0, 2, 3).reshape(groups, -1, d_rows)
    expand = jnp.pad(expand, ((0, 0), (0, 0), (0, rank - d_rows)))
    small_gains = jnp.pad(
        gains[:, :d_rows].reshape(8, groups, per_dev_d).transpose(1, 0, 2), ((0, 0), (0, 8), (0, rank - per_dev_d))
    )
    small = jnp.concatenate([adapt, small_gains, expand], axis=1).astype(BF16)
    n_adapt = 3 * per_dev_d
    (small_sum,), = communicate(
        topo, "sum_small", 8, Scatter(topo, "dp", small, [(0, small.shape[1], "cx")])
    )
    per_seq = rank // groups // n_seq
    across = small_sum[n_adapt + 16 :, :d_rows].reshape(2, n_seq, per_seq, d_rows).transpose(1, 0, 2, 3)
    across = across.reshape(n_seq, 2 * per_seq, d_rows)
    (own_adapt, own_expand), = communicate(
        topo, "finish", 9, Finish(topo, small_sum[: n_adapt + 16], across)
    )
    grad_ga, grad_ua, grad_qa = own_adapt[:n_adapt].reshape(3, per_dev_d, rank)
    grad_gain_attn = own_adapt[n_adapt, :per_dev_d]
    grad_gain_mlp = own_adapt[n_adapt + 1, :per_dev_d]
    own_expand = own_expand.reshape(n_seq, 2, per_seq, d_rows).transpose(1, 2, 0, 3).reshape(2, per_seq, width)
    grad_de, grad_oe = own_expand[0], own_expand[1]
    grad_wk, grad_wv = grad_wkv[:, :HD], grad_wkv[:, HD:]
    grad_ka = dot_t(grad_wk.astype(BF16), key_expand)
    grad_va = dot_t(grad_wv.astype(BF16), value_expand)
    grad_ke, grad_ve = grad_kve[:, :HD], grad_kve[:, HD:]
    return (
        result_rows[None, None], grad_rows[None, None],
        grad_gain_attn, grad_gain_mlp,
        grad_wq, grad_wk, grad_wv, grad_wo, grad_wg, grad_wu, grad_wd,
        grad_qa, grad_qe, grad_ka, grad_ke, grad_va, grad_ve, grad_oa, grad_oe,
        grad_ga, grad_ge, grad_ua, grad_ue, grad_da, grad_de,
    )


def solution(mesh):
    topo = Topo(mesh.shape["dp"], mesh.shape["seq"])
    both = ("dp", "seq")
    in_specs = (
        P(None, "dp", "seq", None), P(None, "dp", "seq"), P(None, "dp", "seq", None),
        P(), P(), P(None, "dp"), P(), P(), P("dp", None), P(None, "dp"), P(None, "dp"), P("dp", None),
        P(), P(None, "dp"), P(), P(), P(), P(), P("dp", None), P(),
        P(), P(None, "dp"), P(), P(None, "dp"), P("dp", None), P(),
    )
    out_specs = (
        P(None, "dp", "seq", None), P(None, "dp", "seq", None), P(both), P(both),
        P("seq", "dp"), P(both, None), P(both, None), P("dp", "seq"), P("seq", "dp"), P("seq", "dp"), P("dp", "seq"),
        P(both, None), P("seq", "dp"), P(both, None), P(both, None), P(both, None), P(both, None),
        P("dp", "seq"), P(both, None), P(both, None), P("seq", "dp"), P(both, None), P("seq", "dp"),
        P("dp", "seq"), P(both, None),
    )
    return jax.shard_map(
        lambda *args: local(topo, *args), mesh=mesh, in_specs=in_specs, out_specs=out_specs, check_vma=False
    )
```

```python
import itertools
import math

import jax
import jax.numpy as jnp
from jax import lax
from jax.experimental import pallas as pl
from jax.experimental.pallas import tpu as pltpu
from jax.sharding import PartitionSpec as P

HD = 256
EPSILON = 1e-06
ROTARY_BASE = 10000.0
MASKED = -1e30

MESH = pl.DeviceIdType.MESH
BF16 = jnp.bfloat16
F32 = jnp.float32


class Topo:
    def __init__(self, n_dp, n_seq):
        self.n_dp, self.n_seq = n_dp, n_seq
        self.size = {"c": 2, "x": n_dp // 2, "b": n_seq // 4, "l": 2, "h": 2}

    def here(self):
        dp, seq = lax.axis_index("dp"), lax.axis_index("seq")
        nb = self.size["b"]
        outer = lax.div(seq, nb)
        return {
            "c": lax.rem(dp, 2),
            "x": lax.div(dp, 2),
            "b": lax.rem(seq, nb),
            "l": lax.rem(outer, 2),
            "h": lax.div(outer, 2),
        }

    def moved(self, at, dims, offsets, sign=1):
        new = dict(at)
        for dim, offset in zip(dims, offsets):
            n = self.size[dim]
            if offset:
                new[dim] = lax.rem(at[dim] + (offset if sign > 0 else n - offset), n)
        return new

    def seq_of(self, at):
        return (at["h"] * 2 + at["l"]) * self.size["b"] + at["b"]

    def device(self, at):
        return (at["x"] * 2 + at["c"], self.seq_of(at))

    def index(self, at, group):
        dp, seq = self.device(at)
        if group == "all":
            return dp * self.n_seq + seq
        if group == "half":
            nb = self.size["b"]
            return dp * (2 * nb) + at["l"] * nb + at["b"]
        if group == "dp":
            return dp
        if group == "seq":
            return seq
        if group == "quad":
            return at["l"] * self.size["b"] + at["b"]
        raise ValueError(group)

    def group_size(self, group):
        nb = self.size["b"]
        return {
            "all": self.n_dp * self.n_seq,
            "half": self.n_dp * 2 * nb,
            "dp": self.n_dp,
            "seq": self.n_seq,
            "quad": 2 * nb,
        }[group]


GROUP_DIMS = {"all": "cxblh", "half": "cxbl", "dp": "cx", "seq": "blh", "quad": "bl"}


def remote(src, dst, send_sem, recv_sem, device):
    return pltpu.make_async_remote_copy(
        src_ref=src,
        dst_ref=dst,
        send_sem=send_sem,
        recv_sem=recv_sem,
        device_id=device,
        device_id_type=MESH,
    )


class Gather:
    def __init__(self, topo, group, x, parts, beyond=None, need=None):
        self.topo, self.group, self.parts, self.beyond = topo, group, parts, beyond
        self.slots = "half" if beyond else group
        self.need = need or (lambda dims, key: 0)
        self.inputs = [x]
        rows, cols = x.shape
        self.outputs = [jax.ShapeDtypeStruct((topo.group_size(self.slots), rows, cols), x.dtype)]
        self.out_specs = [pl.BlockSpec(memory_space=pl.ANY)]
        self.in_specs = [pl.BlockSpec(memory_space=pl.ANY)]
        n = topo.group_size(group)
        self.scratch = [
            pltpu.SemaphoreType.DMA((len(parts), n)),
            pltpu.SemaphoreType.DMA((len(parts), n)),
            pltpu.SemaphoreType.DMA(()),
        ]

    def peers(self):
        return {
            ((dim, d),) for dim in GROUP_DIMS[self.group] for d in range(1, self.topo.size[dim])
        }

    def work(self):
        work = []
        for part, (row, rows, order) in enumerate(self.parts):
            for key in itertools.product(*[range(self.topo.size[dim]) for dim in order]):
                if not any(key) or self.keeps(order, key):
                    hops = sum(1 for o in key if o)
                    last = max([i for i, o in enumerate(key) if o], default=-1)
                    work.append((self.need(order, key), hops, last, part, key))
        work.sort()
        return [(w[3], w[4]) for w in work]

    def keeps(self, order, key):
        return not self.beyond or key[order.index(self.beyond)] != 0

    def run(self, ins, outs, scratch):
        topo = self.topo
        (x_ref,), (out_ref,) = ins, outs
        send_sem, recv_sem, own_sem = scratch
        at = topo.here()
        own = None
        if not self.beyond:
            own = pltpu.make_async_copy(x_ref, out_ref.at[topo.index(at, self.slots)], own_sem)
            own.start()
        started = []

        def key_index(order, key):
            k = 0
            for dim, o in zip(order, key):
                k = k * topo.size[dim] + o
            return k

        def copy(part, order, row, rows, key, stage, d):
            origin = topo.moved(at, order, key, -1)
            slot = topo.index(origin, self.slots)
            new_key = tuple(d if i == stage else o for i, o in enumerate(key))
            src = (
                x_ref.at[pl.ds(row, rows)]
                if not any(key)
                else out_ref.at[slot, pl.ds(row, rows)]
            )
            k = key_index(order, new_key)
            target = topo.device(topo.moved(at, [order[stage]], [d]))
            return remote(
                src,
                out_ref.at[slot, pl.ds(row, rows)],
                send_sem.at[part, k],
                recv_sem.at[part, k],
                target,
            )

        for part, key in self.work():
            row, rows, order = self.parts[part]
            if any(key):
                slot = topo.index(topo.moved(at, order, key, -1), self.slots)
                k = key_index(order, key)
                dst = out_ref.at[slot, pl.ds(row, rows)]
                remote(dst, dst, send_sem.at[part, k], recv_sem.at[part, k], topo.device(at)).wait_recv()
            last = max([i for i, o in enumerate(key) if o], default=-1)
            sends = []
            for stage in range(last + 1, len(order)):
                for d in range(1, topo.size[order[stage]]):
                    new_key = tuple(d if i == stage else o for i, o in enumerate(key))
                    if self.keeps(order, new_key):
                        sends.append((self.need(order, new_key), stage, d))
            for _, stage, d in sorted(sends):
                cp = copy(part, order, row, rows, key, stage, d)
                cp.start()
                started.append(cp)
            yield
        for cp in started:
            cp.wait_send()
        if own is not None:
            own.wait()


class Scatter:
    def __init__(self, topo, group, x, parts, out_dtype=None):
        self.topo, self.group, self.parts = topo, group, parts
        self.inputs = [x]
        n, rows, cols = x.shape
        assert n == topo.group_size(group), (n, group)
        self.outputs = [jax.ShapeDtypeStruct((rows, cols), out_dtype or F32)]
        self.in_specs = [pl.BlockSpec(memory_space=pl.ANY)]
        self.out_specs = [pl.BlockSpec(memory_space=pltpu.VMEM)]
        self.scratch = []
        for row, nrows, order in parts:
            sizes = [topo.size[dim] for dim in order]
            keep = math.prod(sizes[1:])
            self.scratch.append(pltpu.VMEM((keep, nrows, cols), x.dtype))
            self.scratch.append(pltpu.SemaphoreType.DMA((keep,)))
            for k, s in enumerate(sizes):
                rest = math.prod(sizes[k + 1 :])
                self.scratch.append(pltpu.VMEM((max(s - 1, 1), rest, nrows, cols), x.dtype))
                self.scratch.append(pltpu.SemaphoreType.DMA((max(s - 1, 1), rest)))
                self.scratch.append(pltpu.SemaphoreType.DMA((max(s - 1, 1), rest)))

    def peers(self):
        return {
            ((dim, d),) for dim in GROUP_DIMS[self.group] for d in range(1, self.topo.size[dim])
        }

    def run(self, ins, outs, scratch):
        topo = self.topo
        (x_ref,), (out_ref,) = ins, outs
        at = topo.here()
        scratch = list(scratch)
        started, jobs = [], []
        for part, (row, nrows, order) in enumerate(self.parts):
            sizes = [topo.size[dim] for dim in order]
            acc, own_sem = scratch.pop(0), scratch.pop(0)
            bufs = [(scratch.pop(0), scratch.pop(0), scratch.pop(0)) for _ in sizes]

            def flat(key, start, sizes=sizes):
                k = 0
                for o, s in zip(key[start:], sizes[start:]):
                    k = k * s + o
                return k

            keys = list(itertools.product(*[range(s) for s in sizes]))
            first = {k: min([i for i, o in enumerate(k) if o], default=len(sizes)) for k in keys}
            keys.sort(key=lambda k: (first[k], [0 if o else 1 for o in k]))
            for key in keys:
                jobs.append((first[key], part, row, nrows, order, sizes, acc, own_sem, bufs, flat, key))
        jobs.sort(key=lambda j: j[0])

        def out_copy(job, src, key, stage):
            _, part, row, nrows, order, sizes, acc, own_sem, bufs, flat, _ = job
            buf, send_sem, recv_sem = bufs[stage]
            d = key[stage]
            k = flat(key, stage + 1)
            target = topo.device(topo.moved(at, [order[stage]], [d]))
            return remote(src, buf.at[d - 1, k], send_sem.at[d - 1, k], recv_sem.at[d - 1, k], target)

        for job in jobs:
            first, part, row, nrows, order, sizes, acc, own_sem, bufs, flat, key = job
            block = topo.index(topo.moved(at, order, key), self.group)
            if first == 0:
                cp = out_copy(job, x_ref.at[block, pl.ds(row, nrows)], key, 0)
                cp.start()
                started.append(cp)
        yield
        for job in jobs:
            first, part, row, nrows, order, sizes, acc, own_sem, bufs, flat, key = job
            if first > 0:
                block = topo.index(topo.moved(at, order, key), self.group)
                k = flat(key, 1)
                pltpu.make_async_copy(
                    x_ref.at[block, pl.ds(row, nrows)], acc.at[k], own_sem.at[k]
                ).start()
        yield
        for job in jobs:
            first, part, row, nrows, order, sizes, acc, own_sem, bufs, flat, key = job
            if first == 0:
                continue
            kk = flat(key, 1)
            block = topo.index(topo.moved(at, order, key), self.group)
            pltpu.make_async_copy(
                x_ref.at[block, pl.ds(row, nrows)], acc.at[kk], own_sem.at[kk]
            ).wait()
            terms = []
            for stage in range(first):
                buf, send_sem, recv_sem = bufs[stage]
                k = flat(key, stage + 1)
                for d in range(1, sizes[stage]):
                    ref = buf.at[d - 1, k]
                    remote(ref, ref, send_sem.at[d - 1, k], recv_sem.at[d - 1, k], topo.device(at)).wait_recv()
                    terms.append((buf, d - 1, k))
            step = 16 if nrows % 16 == 0 else 8
            final = first == len(sizes)

            def add(r, _, terms=terms, acc=acc, kk=kk, final=final, row=row, step=step):
                r0 = pl.multiple_of(r * step, step)
                total = acc[kk, pl.ds(r0, step), :].astype(F32)
                for buf, d, k in terms:
                    total = total + buf[d, k, pl.ds(r0, step), :].astype(F32)
                if final:
                    out_ref[pl.ds(row + r0, step), :] = total.astype(out_ref.dtype)
                else:
                    acc[kk, pl.ds(r0, step), :] = total.astype(acc.dtype)
                return 0

            lax.fori_loop(0, nrows // step, add, 0)
            if not final:
                cp = out_copy(job, acc.at[kk], key, first)
                cp.start()
                started.append(cp)
            yield
        for cp in started:
            cp.wait_send()


class SlimScatter:
    def __init__(self, topo, group, shape, dtype, parts):
        self.topo, self.group, self.parts = topo, group, parts
        n, rows, cols = shape
        self.dtype = dtype
        self.outputs = [jax.ShapeDtypeStruct((rows, cols), F32)]
        self.out_specs = [pl.BlockSpec(memory_space=pltpu.VMEM)]
        self.scratch = []
        terms = 1 + sum(topo.size[d] - 1 for d in GROUP_DIMS[group])
        most = max(p[1] for p in parts)
        self.terms, self.most, self.cols = terms, most, cols
        for row, nrows, order in parts:
            sizes = [topo.size[dim] for dim in order]
            for k, s in enumerate(sizes):
                rest = math.prod(sizes[k + 1 :])
                m = max(s - 1, 1)
                self.outputs.append(jax.ShapeDtypeStruct((m, rest, nrows, cols), dtype))
                self.out_specs.append(pl.BlockSpec(memory_space=pl.ANY))
                self.scratch.append(pltpu.SemaphoreType.DMA((m, rest)))
                self.scratch.append(pltpu.SemaphoreType.DMA((m, rest)))

    RING = 4

    def shared_scratch(self):
        return [
            pltpu.VMEM((2, self.terms, self.most, self.cols), self.dtype),
            pltpu.SemaphoreType.DMA((2, self.terms)),
            pltpu.VMEM((self.RING, self.most, self.cols), self.dtype),
        ]

    def peers(self):
        return {
            ((dim, d),) for dim in GROUP_DIMS[self.group] for d in range(1, self.topo.size[dim])
        }

    def run(self, x_ref, outs, scratch, shared):
        topo = self.topo
        outs, scratch = list(outs), list(scratch)
        out_ref = outs.pop(0)
        stage_buf, stage_sem, ring = shared
        at = topo.here()
        jobs, started = [], []
        for part, (row, nrows, order) in enumerate(self.parts):
            sizes = [topo.size[dim] for dim in order]
            bufs = [(outs.pop(0), scratch.pop(0), scratch.pop(0)) for _ in sizes]
            keys = list(itertools.product(*[range(s) for s in sizes]))
            first = {k: min([i for i, o in enumerate(k) if o], default=len(sizes)) for k in keys}
            keys.sort(key=lambda k: (first[k], [0 if o else 1 for o in k]))
            for rank, key in enumerate(keys):
                jobs.append((first[key], rank, part, row, nrows, order, sizes, bufs, key))
        jobs.sort(key=lambda j: (j[0], j[1], j[2]))

        def flat(key, start, sizes):
            k = 0
            for o, s in zip(key[start:], sizes[start:]):
                k = k * s + o
            return k

        def out_copy(job, src):
            stage, _, part, row, nrows, order, sizes, bufs, key = job
            buf, send_sem, recv_sem = bufs[stage]
            d, k = key[stage], flat(key, stage + 1, sizes)
            target = topo.device(topo.moved(at, [order[stage]], [d]))
            return remote(src, buf.at[d - 1, k], send_sem.at[d - 1, k], recv_sem.at[d - 1, k], target)

        def block(job):
            _, _, part, row, nrows, order, sizes, bufs, key = job
            return x_ref.at[topo.index(topo.moved(at, order, key), self.group), pl.ds(row, nrows)]

        for job in jobs:
            if job[0] == 0:
                cp = out_copy(job, block(job))
                cp.start()
                started.append(cp)
        yield
        jobs = [job for job in jobs if job[0] > 0]

        def loads(job, slot, arrived):
            first, _, part, row, nrows, order, sizes, bufs, key = job
            copies = []
            i = 0
            sources = [block(job)]
            for stage in range(first):
                buf, send_sem, recv_sem = bufs[stage]
                k = flat(key, stage + 1, sizes)
                for d in range(1, sizes[stage]):
                    ref = buf.at[d - 1, k]
                    if not arrived:
                        remote(ref, ref, send_sem.at[d - 1, k], recv_sem.at[d - 1, k], topo.device(at)).wait_recv()
                    sources.append(ref)
            for i, ref in enumerate(sources):
                copies.append(
                    pltpu.make_async_copy(ref, stage_buf.at[slot, i, pl.ds(0, nrows)], stage_sem.at[slot, i])
                )
            return copies

        in_ring = [None] * self.RING
        sent = 0
        for cp in loads(jobs[0], 0, False):
            cp.start()
        yield
        for n, job in enumerate(jobs):
            first, _, part, row, nrows, order, sizes, bufs, key = job
            slot = n % 2
            copies = loads(job, slot, True)
            for cp in copies:
                cp.wait()
            final = first == len(sizes)
            if not final:
                place = sent % self.RING
                if in_ring[place] is not None:
                    in_ring[place].wait_send()
            step = 16 if nrows % 16 == 0 else 8

            def add(r, _, slot=slot, count=len(copies), final=final, row=row, step=step):
                r0 = pl.multiple_of(r * step, step)
                total = stage_buf[slot, 0, pl.ds(r0, step), :].astype(F32)
                for i in range(1, count):
                    total = total + stage_buf[slot, i, pl.ds(r0, step), :].astype(F32)
                if final:
                    out_ref[pl.ds(row + r0, step), :] = total
                else:
                    ring[place, pl.ds(r0, step), :] = total.astype(ring.dtype)
                return 0

            lax.fori_loop(0, nrows // step, add, 0)
            if not final:
                cp = out_copy(job, ring.at[place, pl.ds(0, nrows)])
                cp.start()
                in_ring[place] = cp
                sent += 1
            if n + 1 < len(jobs):
                for cp in loads(jobs[n + 1], 1 - slot, False):
                    cp.start()
            yield
        for cp in started:
            cp.wait_send()
        for cp in in_ring:
            if cp is not None:
                cp.wait_send()


class Exchange:
    def __init__(self, topo, group, x):
        self.topo, self.group = topo, group
        self.inputs = [x]
        n = x.shape[0]
        assert n == topo.group_size(group)
        self.outputs = [jax.ShapeDtypeStruct(x.shape, x.dtype)]
        self.in_specs = [pl.BlockSpec(memory_space=pl.ANY)]
        self.out_specs = [pl.BlockSpec(memory_space=pl.ANY)]
        self.scratch = [
            pltpu.SemaphoreType.DMA((n,)),
            pltpu.SemaphoreType.DMA((n,)),
            pltpu.SemaphoreType.DMA(()),
        ]

    def offsets(self):
        dims = GROUP_DIMS[self.group]
        return dims, [
            o for o in itertools.product(*[range(self.topo.size[d]) for d in dims]) if any(o)
        ]

    def peers(self):
        dims, offsets = self.offsets()
        return {tuple((dim, o) for dim, o in zip(dims, off) if o) for off in offsets}

    def run(self, ins, outs, scratch):
        topo = self.topo
        (x_ref,), (out_ref,) = ins, outs
        send_sem, recv_sem, own_sem = scratch
        at = topo.here()
        me = topo.index(at, self.group)
        own = pltpu.make_async_copy(x_ref.at[me], out_ref.at[me], own_sem)
        own.start()
        dims, offsets = self.offsets()
        started = []
        for i, off in enumerate(offsets):
            there = topo.moved(at, dims, off)
            cp = remote(
                x_ref.at[topo.index(there, self.group)],
                out_ref.at[me],
                send_sem.at[i],
                recv_sem.at[i],
                topo.device(there),
            )
            cp.start()
            started.append(cp)
        yield
        for i, off in enumerate(offsets):
            ref = out_ref.at[topo.index(topo.moved(at, dims, off, -1), self.group)]
            remote(ref, ref, send_sem.at[i], recv_sem.at[i], topo.device(at)).wait_recv()
            yield
        for cp in started:
            cp.wait_send()
        own.wait()


class Finish:
    def __init__(self, topo, x, y):
        self.topo = topo
        self.inputs = [x, y]
        self.outputs = [
            jax.ShapeDtypeStruct(x.shape, x.dtype),
            jax.ShapeDtypeStruct(y.shape, y.dtype),
        ]
        self.in_specs = [pl.BlockSpec(memory_space=pl.ANY)] * 2
        self.out_specs = [pl.BlockSpec(memory_space=pl.ANY)] * 2
        self.inner = Exchange(topo, "seq", y)
        self.scratch = self.inner.scratch + [
            pltpu.SemaphoreType.DMA(()),
            pltpu.SemaphoreType.DMA(()),
            pltpu.SemaphoreType.DMA(()),
        ]

    def peers(self):
        return self.inner.peers()

    def route(self):
        topo = self.topo
        dp, seq = lax.axis_index("dp"), lax.axis_index("seq")
        n = seq * topo.n_dp + dp
        target = (lax.div(n, topo.n_seq), lax.rem(n, topo.n_seq))
        m = dp * topo.n_seq + seq
        source = (lax.rem(m, topo.n_dp), lax.div(m, topo.n_dp))
        stays = (target[0] == dp) & (target[1] == seq)
        return target, source, stays

    def greet(self, barrier):
        target, source, stays = self.route()

        @pl.when(jnp.logical_not(stays))
        def _():
            pl.semaphore_signal(barrier, inc=1, device_id=source, device_id_type=MESH)

        return jnp.where(stays, 0, 1)

    def run(self, ins, outs, scratch):
        (x_ref, y_ref), (x_out, y_out) = ins, outs
        send_sem, recv_sem, own_sem = scratch[3:]
        target, source, stays = self.route()
        cp = remote(x_ref, x_out, send_sem, recv_sem, target)
        own = pltpu.make_async_copy(x_ref, x_out, own_sem)

        @pl.when(stays)
        def _():
            own.start()

        @pl.when(jnp.logical_not(stays))
        def _():
            cp.start()

        yield from self.inner.run([y_ref], [y_out], scratch[:3])

        @pl.when(stays)
        def _():
            own.wait()

        @pl.when(jnp.logical_not(stays))
        def _():
            cp.wait()


def communicate(topo, name, collective_id, *ops):
    n_in = [len(op.inputs) for op in ops]
    n_out = [len(op.outputs) for op in ops]
    n_scratch = [len(op.scratch) for op in ops]

    def kernel(*refs):
        refs = list(refs)
        take = lambda counts: [[refs.pop(0) for _ in range(k)] for k in counts]
        ins, outs, scratch = take(n_in), take(n_out), take(n_scratch)
        at = topo.here()
        peers = sorted(set().union(*[op.peers() for op in ops]))
        barrier = pltpu.get_barrier_semaphore()
        for peer in peers:
            there = topo.device(topo.moved(at, [p[0] for p in peer], [p[1] for p in peer]))
            pl.semaphore_signal(barrier, inc=1, device_id=there, device_id_type=MESH)
        greeted = len(peers)
        for op in ops:
            if hasattr(op, "greet"):
                greeted = greeted + op.greet(barrier)
        pl.semaphore_wait(barrier, greeted)
        running = [op.run(i, o, s) for op, i, o, s in zip(ops, ins, outs, scratch)]
        while running:
            for step in list(running):
                try:
                    next(step)
                except StopIteration:
                    running.remove(step)

    results = pl.pallas_call(
        kernel,
        name=name,
        out_shape=[s for op in ops for s in op.outputs],
        in_specs=[s for op in ops for s in op.in_specs],
        out_specs=[s for op in ops for s in op.out_specs],
        scratch_shapes=[s for op in ops for s in op.scratch],
        compiler_params=pltpu.CompilerParams(
            collective_id=collective_id, has_side_effects=True, vmem_limit_bytes=58 << 20
        ),
    )(*[x for op in ops for x in op.inputs])
    results = list(results)
    return [[results.pop(0) for _ in range(k)] for k in n_out]


def row_parts(rows, orders, weights, step=16):
    parts, row, total = [], 0, sum(weights)
    for i, (order, weight) in enumerate(zip(orders, weights)):
        n = rows - row if i == len(orders) - 1 else min(rows - row, int(round(rows * weight / total / step)) * step)
        if n:
            parts.append((row, n, order))
            row += n
    return parts


def matmul(left, right):
    return jnp.dot(left, right, preferred_element_type=jnp.float32)


def contract(form, left, right):
    return jnp.einsum(form, left, right, preferred_element_type=jnp.float32)


def rotary(positions, size):
    half_size = size // 2
    frequency = ROTARY_BASE ** (-(jnp.arange(half_size, dtype=jnp.float32) * 2.0) / size)
    angles = positions.astype(jnp.float32)[:, None] * frequency[None, :]
    return (jnp.cos(angles), jnp.sin(angles))


def rotate(values, cosine_table, sine_table):
    half_size = values.shape[-1] // 2
    first_half = values[..., :half_size]
    second_half = values[..., half_size:]
    return jnp.concatenate(
        [
            first_half * cosine_table - second_half * sine_table,
            second_half * cosine_table + first_half * sine_table,
        ],
        axis=-1,
    )


def normalize(values, gain_vector):
    inverse_rms = lax.rsqrt(jnp.mean(values * values, axis=-1, keepdims=True) + EPSILON)
    unit_rows = values * inverse_rms
    return (unit_rows * gain_vector, unit_rows, inverse_rms)


def norm_backward(grad_normed, unit_rows, inverse_rms, gain_vector):
    gain_term = jnp.sum(grad_normed * unit_rows, axis=0)
    grad_unit = grad_normed * gain_vector
    inner = jnp.mean(grad_unit * unit_rows, axis=-1, keepdims=True)
    return (gain_term, inverse_rms * (grad_unit - unit_rows * inner))


def dot_t(left, right):
    return lax.dot_general(left, right, (((1,), (1,)), ((), ())), preferred_element_type=F32)


def t_dot(left, right):
    return lax.dot_general(left, right, (((0,), (0,)), ((), ())), preferred_element_type=F32)


GELU_C = math.sqrt(2.0 / math.pi)


def gelu_parts(v):
    square = v * v
    t = jnp.tanh(GELU_C * (v + 0.044715 * v * square))
    half_up = 0.5 * (1.0 + t)
    slope = half_up + 0.5 * v * (1.0 - t * t) * (GELU_C * (1.0 + 3.0 * 0.044715 * square))
    return v * half_up, slope


def feed_forward(
    topo, collective_id, normed, grads, grads_half,
    w_gate, w_up, w_down, gate_adapt, gate_expand, up_adapt, up_expand, down_adapt, down_expand,
):
    rows, width = normed.shape
    quad = topo.group_size("quad")
    half = topo.group_size("half")
    units = w_gate.shape[1] // quad
    rank = gate_adapt.shape[1]
    ranks = rank // 2
    half_width = width // 2
    d_rows, r_rows = half_width // quad, ranks // quad
    per_chunk = 512 // rows
    tile = 512
    block = 256

    dims = "hxclb"
    keys = list(itertools.product(*[range(topo.size[d]) for d in dims]))
    chunks = [keys[i : i + per_chunk] for i in range(0, len(keys), per_chunk)]
    own = len(chunks) // 2
    chunk_of = {key: i for i, keys_of in enumerate(chunks) for key in keys_of}

    def need(order, key):
        at_dim = dict(zip(order, key))
        return chunk_of[tuple(at_dim[d] for d in dims)]

    gather_n = Gather(topo, "all", normed, row_parts(rows, ("lhbxc", "xlhbc"), (7, 4)), need=need)
    gather_g = Gather(
        topo, "all", grads, row_parts(rows, ("hxlbc", "hlbxc", "hbxlc"), (1, 1, 1)), beyond="h", need=need
    )
    thirds = row_parts(rows, ("cxbl", "cblx", "clxb"), (1, 1, 1))
    sum_n = SlimScatter(topo, "half", (half, rows, width), BF16, thirds)
    sum_d = SlimScatter(topo, "half", (half, rows, width), BF16, thirds)
    comm = [gather_n, gather_g, sum_n, sum_d]

    inputs = [
        normed, grads, grads_half, w_gate, w_up, w_down,
        gate_adapt, gate_expand, up_adapt, up_expand, down_adapt, down_expand,
    ]
    part = jax.ShapeDtypeStruct((half, rows, width), BF16)
    grad = jax.ShapeDtypeStruct((quad, d_rows + r_rows, units), BF16)
    any_spec = pl.BlockSpec(memory_space=pl.ANY)
    out_shape = [part, part, grad, grad, grad]
    out_specs = [any_spec] * 5
    scratch = [
        pltpu.VMEM((width, units), BF16), pltpu.VMEM((width, units), BF16), pltpu.VMEM((units, width), BF16),
        pltpu.VMEM((width, rank), BF16), pltpu.VMEM((rank, units), BF16),
        pltpu.VMEM((width, rank), BF16), pltpu.VMEM((rank, units), BF16),
        pltpu.VMEM((units, rank), BF16), pltpu.VMEM((rank, width), BF16),
        pltpu.VMEM((half_width + ranks, units), F32),
        pltpu.VMEM((half_width + ranks, units), F32),
        pltpu.VMEM((half_width + ranks, units), F32),
        pltpu.VMEM((3, tile, units), BF16),
        pltpu.VMEM((2, tile, width), BF16), pltpu.VMEM((2, tile, width), BF16),
        pltpu.VMEM((tile, width), BF16), pltpu.VMEM((tile, width), BF16),
        pltpu.SemaphoreType.DMA((9,)),
        pltpu.SemaphoreType.DMA((2, 2, per_chunk)),
        pltpu.SemaphoreType.DMA((2, per_chunk)),
        pltpu.SemaphoreType.DMA((3,)),
    ]
    n_own = len(scratch)
    shared = sum_n.shared_scratch()
    scratch = scratch + shared
    for op in comm:
        out_shape = out_shape + op.outputs
        out_specs = out_specs + op.out_specs
        scratch = scratch + op.scratch

    def kernel(*refs):
        refs = list(refs)
        (
            n_hbm, g_hbm, g_half, wg_hbm, wu_hbm, wd_hbm, ga_hbm, ge_hbm, ua_hbm, ue_hbm, da_hbm, de_hbm,
        ) = [refs.pop(0) for _ in inputs]
        down_part, gn_part, dg_out, du_out, dd_out = [refs.pop(0) for _ in range(5)]
        op_outs = [[refs.pop(0) for _ in op.outputs] for op in comm]
        (
            wg, wu, wd, ga, ge, ua, ue, da, de, acc_g, acc_u, acc_d, acts, n_buf, g_buf, down_st, gn_st,
            w_sem, load_sem, store_sem, grad_sem,
        ) = [refs.pop(0) for _ in range(n_own)]
        shared_refs = [refs.pop(0) for _ in shared]
        op_scratch = [[refs.pop(0) for _ in op.scratch] for op in comm]
        mix_s, gg_s, gu_s = acts.at[0], acts.at[1], acts.at[2]
        at = topo.here()
        high = at["h"]
        member = topo.index(at, "quad")
        unit_at = pl.multiple_of(member * units, units)

        w_copies = [
            pltpu.make_async_copy(src, dst, w_sem.at[i])
            for i, (src, dst) in enumerate(
                (
                    (de_hbm, de),
                    (da_hbm.at[pl.ds(unit_at, units), :], da),
                    (wd_hbm.at[pl.ds(unit_at, units), :], wd),
                    (ga_hbm, ga),
                    (ge_hbm.at[:, pl.ds(unit_at, units)], ge),
                    (wg_hbm.at[:, pl.ds(unit_at, units)], wg),
                    (ua_hbm, ua),
                    (ue_hbm.at[:, pl.ds(unit_at, units)], ue),
                    (wu_hbm.at[:, pl.ds(unit_at, units)], wu),
                )
            )
        ]
        for cp in w_copies:
            cp.start()

        peers = sorted(set().union(*[op.peers() for op in comm]))
        barrier = pltpu.get_barrier_semaphore()
        for peer in peers:
            there = topo.device(topo.moved(at, [p[0] for p in peer], [p[1] for p in peer]))
            pl.semaphore_signal(barrier, inc=1, device_id=there, device_id_type=MESH)
        pl.semaphore_wait(barrier, len(peers))

        steps_n = gather_n.run([n_hbm], op_outs[0], op_scratch[0])
        steps_g = gather_g.run([g_hbm], op_outs[1], op_scratch[1])
        order_n = [need(gather_n.parts[p][2], k) for p, k in gather_n.work()]
        order_g = [need(gather_g.parts[p][2], k) if any(k) else own for p, k in gather_g.work()]
        arrivals = sorted(
            [(c, i / len(order_n), 0) for i, c in enumerate(order_n)]
            + [(c, i / len(order_g), 1) for i, c in enumerate(order_g)],
            key=lambda w: w[0],
        )
        first_g = [w for w in arrivals if w[2] == 1][:len(gather_g.parts)]
        for w in first_g:
            arrivals.remove(w)
        per_part = len(gather_n.parts)
        arrivals = arrivals[:per_part] + first_g + arrivals[per_part:]
        done = [0]

        def advance(count=None, upto=None):
            while done[0] < len(arrivals):
                if count is not None:
                    if count == 0:
                        return
                    count -= 1
                elif not any(w[0] <= upto for w in arrivals[done[0]:]):
                    return
                next((steps_n, steps_g)[arrivals[done[0]][2]], None)
                done[0] += 1

        acc_g[...] = jnp.zeros_like(acc_g)
        acc_u[...] = jnp.zeros_like(acc_u)
        acc_d[...] = jnp.zeros_like(acc_d)
        advance(count=per_part + len(first_g))

        def merge_rows(weight, adapt, expand, total):
            def one(i, _):
                r = pl.ds(pl.multiple_of(i * block, block), block)
                weight[r, :] = (weight[r, :].astype(F32) + matmul(adapt[r, :], expand[...])).astype(BF16)
                return 0

            lax.fori_loop(0, total // block, one, 0)

        for cp in w_copies[:3]:
            cp.wait()
        merge_rows(wd, da, de, units)
        for cp in w_copies[3:6]:
            cp.wait()
        merge_rows(wg, ga, ge, width)
        for cp in w_copies[6:]:
            cp.wait()
        merge_rows(wu, ua, ue, width)

        def chunk_copies(c, slot):
            copies = []
            for i, key in enumerate(chunks[c]):
                origin = topo.moved(at, dims, key, -1)
                r = pl.ds(i * rows, rows)
                in_half = topo.index(origin, "half")
                g_src = g_half if key[0] == 0 else op_outs[1][0]
                n_src = op_outs[0][0].at[topo.index(origin, "all")] if any(key) else n_hbm
                copies.append(pltpu.make_async_copy(n_src, n_buf.at[slot, r], load_sem.at[slot, 0, i]))
                copies.append(
                    pltpu.make_async_copy(g_src.at[in_half], g_buf.at[slot, r], load_sem.at[slot, 1, i])
                )
            return copies

        def store_copies(c):
            copies = []
            for i, key in enumerate(chunks[c]):
                slot = topo.index(topo.moved(at, dims, key, -1), "half")
                r = pl.ds(i * rows, rows)
                copies.append(pltpu.make_async_copy(down_st.at[r], down_part.at[slot], store_sem.at[0, i]))
                copies.append(pltpu.make_async_copy(gn_st.at[r], gn_part.at[slot], store_sem.at[1, i]))
            return copies

        sums = []

        def sum_steps(count):
            for _ in range(count):
                if not sums:
                    return
                try:
                    next(sums[0])
                except StopIteration:
                    sums.pop(0)

        advance(upto=0)
        for cp in chunk_copies(0, 0):
            cp.start()
        low_cols = pl.ds(pl.multiple_of(high * ranks, ranks), ranks)
        half_at = high * half_width

        def poll(c):
            if c < own:
                advance(count=POLL)
            else:
                sum_steps(SUM_POLL)

        for c in range(len(chunks)):
            slot = c % 2
            nb, gb = n_buf.at[slot], g_buf.at[slot]
            for cp in chunk_copies(c, slot):
                cp.wait()
            low_g = matmul(nb[...], ga[:, low_cols]).astype(BF16)
            low_u = matmul(nb[...], ua[:, low_cols]).astype(BF16)
            low_b = dot_t(gb[...], de[low_cols, :]).astype(BF16)

            def one(i, _, nb=nb, gb=gb):
                cols = pl.ds(pl.multiple_of(i * block, block), block)
                gate = matmul(nb[...], wg[:, cols])
                up = matmul(nb[...], wu[:, cols])
                act, slope = gelu_parts(gate)
                gm = dot_t(gb[...], wd[cols, :])
                mix_s[:, cols] = (act * up).astype(BF16)
                gg_s[:, cols] = (gm * up * slope).astype(BF16)
                gu_s[:, cols] = (gm * act).astype(BF16)
                return 0

            lax.fori_loop(0, units // block, one, 0)
            poll(c)
            if c < own:
                if c > 0:
                    for cp in store_copies(c - 1):
                        cp.wait()

                def two(i, _):
                    cols = pl.ds(pl.multiple_of(i * block, block), block)
                    down_st[:, cols] = matmul(mix_s[...], wd[:, cols]).astype(BF16)
                    gn_st[:, cols] = (dot_t(gg_s[...], wg[cols, :]) + dot_t(gu_s[...], wu[cols, :])).astype(BF16)
                    return 0

                lax.fori_loop(0, width // block, two, 0)
                for cp in store_copies(c):
                    cp.start()
            for acc, low_rows, grads_s in ((acc_g, low_g, gg_s), (acc_u, low_u, gu_s), (acc_d, low_b, mix_s)):
                acc[half_width:, :] += t_dot(low_rows, grads_s[...])
            if c + 1 < len(chunks):
                advance(upto=c + 1)
                for cp in chunk_copies(c + 1, 1 - slot):
                    cp.start()

            def three(i, _, nb=nb, gb=gb):
                r = pl.ds(pl.multiple_of(i * block, block), block)
                cols = pl.ds(pl.multiple_of(half_at + i * block, block), block)
                acc_g[r, :] += t_dot(nb[:, cols], gg_s[...])
                acc_u[r, :] += t_dot(nb[:, cols], gu_s[...])
                acc_d[r, :] += t_dot(gb[:, cols], mix_s[...])
                return 0

            lax.fori_loop(0, half_width // block, three, 0)
            if c == own - 1:
                for cp in store_copies(c):
                    cp.wait()
                sums.append(sum_n.run(gn_part, op_outs[2], op_scratch[2], shared_refs))
                sums.append(sum_d.run(down_part, op_outs[3], op_scratch[3], shared_refs))
            poll(c)

        pending = []
        for q in range(quad):
            for k, (acc, out) in enumerate(((acc_g, dg_out), (acc_u, du_out), (acc_d, dd_out))):
                if len(pending) >= 3:
                    pending.pop(0).wait()
                acts[k, :d_rows, :] = acc[q * d_rows : (q + 1) * d_rows, :].astype(BF16)
                acts[k, d_rows : d_rows + r_rows, :] = acc[
                    half_width + q * r_rows : half_width + (q + 1) * r_rows, :
                ].astype(BF16)
                cp = pltpu.make_async_copy(acts.at[k, pl.ds(0, d_rows + r_rows)], out.at[q], grad_sem.at[k])
                cp.start()
                pending.append(cp)
        for cp in pending:
            cp.wait()
        sum_steps(10000)
        for _ in steps_n:
            pass
        for _ in steps_g:
            pass

    flops = 2 * rows * topo.n_dp * topo.n_seq * units * width * 9
    results = pl.pallas_call(
        kernel,
        name="feed_forward",
        out_shape=out_shape,
        in_specs=[any_spec] * len(inputs),
        out_specs=out_specs,
        scratch_shapes=scratch,
        compiler_params=pltpu.CompilerParams(
            collective_id=collective_id, has_side_effects=True, vmem_limit_bytes=60 << 20
        ),
        cost_estimate=pl.CostEstimate(flops=flops, bytes_accessed=1 << 27, transcendentals=0),
    )(*inputs)
    dg, du, dd = results[2:5]
    skip = 5 + len(gather_n.outputs) + len(gather_g.outputs)
    return results[skip + len(sum_n.outputs)], results[skip], dg, du, dd


POLL = 6
SUM_POLL = 12


def local(
    topo,
    tokens, segment_ids, out_grad, gain_attn, gain_mlp, w_query, w_key, w_value, w_out, w_gate, w_up, w_down,
    query_adapt, query_expand, key_adapt, key_expand, value_adapt, value_expand, out_adapt, out_expand,
    gate_adapt, gate_expand, up_adapt, up_expand, down_adapt, down_expand,
):
    rows, width = tokens.shape[2], tokens.shape[3]
    groups, n_seq = topo.n_dp, topo.n_seq
    length = rows * n_seq
    heads_dev = w_query.shape[1] // HD
    head_cols = heads_dev * HD
    rank = query_adapt.shape[1]
    scale_qk = HD ** (-0.5)
    quad = topo.group_size("quad")
    units = w_gate.shape[1] // quad
    seq = lax.axis_index("seq")
    dp = lax.axis_index("dp")

    def merged(weight, adapt, expand):
        return (weight.astype(F32) + matmul(adapt, expand)).astype(BF16)

    wq = merged(w_query, query_adapt, query_expand)
    wk = merged(w_key, key_adapt, key_expand)
    wv = merged(w_value, value_adapt, value_expand)
    wo = merged(w_out, out_adapt, out_expand)
    token_rows = tokens[0, 0].astype(F32)
    grad_rows_in = out_grad[0, 0]
    normed, unit_attn, rms_attn = normalize(token_rows, gain_attn)
    normed_attn = normed.astype(BF16)
    positions = seq * rows + jnp.arange(rows, dtype=jnp.int32)
    cosine_table, sine_table = rotary(positions, HD)
    cosine_heads, sine_heads = cosine_table[:, None, :], sine_table[:, None, :]
    key_rot = rotate(matmul(normed_attn, wk), cosine_table, sine_table).astype(BF16)
    value_rows = matmul(normed_attn, wv).astype(BF16)
    key_value = jnp.concatenate([key_rot, value_rows], axis=1)
    seg_rows = jnp.zeros((16, rows), F32).at[0].set(segment_ids[0, 0].astype(F32))

    zyx, xzy = "lhbxc", "xlhbc"
    (normed_all,), (kv_all,), (seg_all,), (grad_half,) = communicate(
        topo, "gather_attention", 0,
        Gather(topo, "dp", normed_attn, [(0, rows, "xc")]),
        Gather(topo, "all", key_value, row_parts(rows, (zyx, xzy), (7, 4))),
        Gather(topo, "all", seg_rows, [(0, 16, zyx)]),
        Gather(topo, "half", grad_rows_in, row_parts(rows, ("xlbc", "lbxc", "bxlc"), (1, 1, 1))),
    )
    kv_all = kv_all.reshape(groups, length, 2 * HD)
    keys_all, values_all = kv_all[..., :HD], kv_all[..., HD:]
    segments = seg_all[:, 0, :].reshape(groups, length)
    own_segments = lax.dynamic_slice_in_dim(segments, seq * rows, rows, 1)
    key_positions = jnp.arange(length, dtype=jnp.int32)
    causal = (key_positions[None, :] <= positions[:, None])[None, :, :]
    allowed = (causal & (own_segments[:, :, None] == segments[:, None, :]))[:, None, :, :]

    queries = matmul(normed_all.reshape(groups * rows, width), wq)
    query_rot = rotate(queries.reshape(groups, rows, heads_dev, HD), cosine_heads, sine_heads).astype(BF16)
    scores = jnp.where(allowed, contract("sthd,sjd->shtj", query_rot, keys_all) * scale_qk, MASKED)
    row_top = jnp.max(scores, axis=-1, keepdims=True)
    log_total = row_top + jnp.log(jnp.sum(jnp.exp(scores - row_top), axis=-1, keepdims=True))
    prob_low = jnp.exp(scores - log_total).astype(BF16)
    heads_out = (
        contract("shtj,sjd->sthd", prob_low, values_all).reshape(groups * rows, head_cols).astype(BF16)
    )
    out_part = matmul(heads_out, wo).astype(BF16).reshape(groups, rows, width)
    (out_sum,), = communicate(
        topo, "sum_attention", 1, Scatter(topo, "dp", out_part, [(0, rows, "cx")])
    )
    middle = token_rows + out_sum
    normed, unit_mlp, rms_mlp = normalize(middle, gain_mlp)
    normed_mlp = normed.astype(BF16)
    down_sum, gn_sum, dg, du, dd = feed_forward(
        topo, 2, normed_mlp, grad_rows_in, grad_half,
        w_gate, w_up, w_down, gate_adapt, gate_expand, up_adapt, up_expand, down_adapt, down_expand,
    )
    result_rows = (middle + down_sum).astype(BF16)
    gain_mlp_term, grad_from_mlp = norm_backward(gn_sum, unit_mlp, rms_mlp, gain_mlp)
    grad_middle = grad_rows_in.astype(F32) + grad_from_mlp
    grad_branch_attn = grad_middle.astype(BF16)
    (grad_attn_all,), (dg,), (du,), (dd,) = communicate(
        topo, "gather_back", 4,
        Gather(topo, "dp", grad_branch_attn, [(0, rows, "xc")]),
        Exchange(topo, "quad", dg),
        Exchange(topo, "quad", du),
        Exchange(topo, "quad", dd),
    )
    grad_attn_all = grad_attn_all.reshape(groups * rows, width)
    grad_heads = dot_t(grad_attn_all, wo).astype(BF16)
    grad_heads_split = grad_heads.reshape(groups, rows, heads_dev, HD)
    scores_again = jnp.where(allowed, contract("sthd,sjd->shtj", query_rot, keys_all) * scale_qk, MASKED)
    probabilities = jnp.exp(scores_again - log_total)
    grad_values_part = contract("shtj,sthd->sjd", probabilities.astype(BF16), grad_heads_split)
    grad_probs = contract("sthd,sjd->shtj", grad_heads_split, values_all)
    delta_rows = jnp.sum(probabilities * grad_probs, axis=-1, keepdims=True)
    grad_scores = (probabilities * (grad_probs - delta_rows)).astype(BF16)
    grad_query_rot = contract("shtj,sjd->sthd", grad_scores, keys_all) * scale_qk
    grad_keys_part = contract("shtj,sthd->sjd", grad_scores, query_rot) * scale_qk
    grad_query = (
        rotate(grad_query_rot, cosine_heads, -sine_heads).reshape(groups * rows, head_cols).astype(BF16)
    )
    gn_attn_part = dot_t(grad_query, wq).astype(BF16).reshape(groups, rows, width)
    grad_kv_part = jnp.concatenate([grad_keys_part, grad_values_part], axis=-1).astype(BF16)
    (gn_attn_sum,), (grad_kv_sum,) = communicate(
        topo, "sum_back", 5,
        Scatter(topo, "dp", gn_attn_part, [(0, rows, "cx")]),
        Scatter(
            topo, "all", grad_kv_part.reshape(groups * n_seq, rows, 2 * HD),
            row_parts(rows, ("cxblh", "cblhx"), (1, 1)),
        ),
    )
    grad_key = rotate(grad_kv_sum[:, :HD], cosine_table, -sine_table).astype(BF16)
    grad_value = grad_kv_sum[:, HD:].astype(BF16)
    grad_normed_attn = gn_attn_sum + dot_t(grad_key, wk) + dot_t(grad_value, wv)
    gain_attn_term, grad_from_attn = norm_backward(grad_normed_attn, unit_attn, rms_attn, gain_attn)
    grad_rows = (grad_middle + grad_from_attn).astype(BF16)

    (grad_kv_group,), = communicate(
        topo, "gather_kv", 6,
        Gather(topo, "dp", jnp.concatenate([grad_key, grad_value], axis=1), [(0, rows, "xc")]),
    )
    grad_kv_group = grad_kv_group.reshape(groups * rows, 2 * HD)
    normed_group = normed_all.reshape(groups * rows, width)
    query_low = matmul(normed_group, query_adapt).astype(BF16)
    grad_out_low = dot_t(grad_attn_all, out_expand).astype(BF16)
    d_rows, r_rows = width // n_seq, rank // n_seq
    per_dev_d, per_dev_r = d_rows // groups, r_rows // groups
    cols = lax.dynamic_slice_in_dim(normed_group, dp * (width // groups), width // groups, 1)
    my_kv_ranks = lambda a: lax.dynamic_slice_in_dim(a, dp * (rank // groups), rank // groups, 1)
    key_low = matmul(normed_group, my_kv_ranks(key_adapt)).astype(BF16)
    value_low = matmul(normed_group, my_kv_ranks(value_adapt)).astype(BF16)
    kv_weight = t_dot(cols, grad_kv_group)
    kv_expand = jnp.concatenate(
        [t_dot(key_low, grad_kv_group[:, :HD]), t_dot(value_low, grad_kv_group[:, HD:])], axis=1
    )
    by_seq = lambda a: a.reshape(n_seq, -1, a.shape[-1])
    widen = lambda a: jnp.pad(a, ((0, 0), (0, 0), (0, 2 * HD - a.shape[-1])))
    fold = lambda a: a if a.shape[-1] == 2 * HD else widen(a)
    gains = jnp.stack([gain_attn_term, gain_mlp_term]).reshape(2, n_seq, d_rows).transpose(1, 0, 2)
    gains = jnp.pad(gains, ((0, 0), (0, 6), (0, 2 * HD - d_rows)))
    pieces = [
        fold(by_seq(t_dot(normed_group, grad_query))),
        fold(by_seq(t_dot(query_low, grad_query))),
        fold(by_seq(t_dot(grad_attn_all, heads_out))),
        fold(by_seq(t_dot(grad_out_low, heads_out))),
        by_seq(kv_weight),
        by_seq(kv_expand),
        gains,
    ]
    sizes = [p.shape[1] for p in pieces]
    fill = -sum(sizes) % 16
    stacked = jnp.concatenate(
        [p.astype(BF16) for p in pieces] + [jnp.zeros((n_seq, fill, 2 * HD), BF16)], axis=1
    )
    (weights,), = communicate(
        topo, "sum_weights", 7,
        Scatter(topo, "seq", stacked, row_parts(stacked.shape[1], ("blh", "lhb"), (9, 4))),
    )
    starts = [sum(sizes[:i]) for i in range(len(sizes))]
    grad_wq, grad_qe, grad_wo, grad_oa, grad_wkv, grad_kve, gains = [
        weights[a : a + s] for a, s in zip(starts, sizes)
    ]
    grad_wq, grad_qe = grad_wq[:, :head_cols], grad_qe[:, :head_cols]
    grad_wo, grad_oa = grad_wo[:, :head_cols].T, grad_oa[:, :head_cols].T

    def unfold(a):
        full = a.astype(F32).transpose(1, 0, 2).reshape(d_rows + r_rows, quad * units)
        return full[:d_rows], full[d_rows:]

    grad_wg, grad_ge = unfold(dg)
    grad_wu, grad_ue = unfold(du)
    grad_wd_t, grad_da_t = unfold(dd)
    grad_wd, grad_da = grad_wd_t.T, grad_da_t.T

    adapt = jnp.stack(
        [
            dot_t(grad_wg.astype(BF16), gate_expand),
            dot_t(grad_wu.astype(BF16), up_expand),
            dot_t(grad_wq.astype(BF16), query_expand),
        ]
    )
    expand = jnp.stack(
        [
            matmul(down_adapt.T, grad_wd.astype(BF16)),
            matmul(out_adapt.T, grad_wo.astype(BF16)),
        ]
    )
    adapt = adapt.reshape(3, groups, per_dev_d, rank).transpose(1, 0, 2, 3).reshape(groups, -1, rank)
    expand = expand.reshape(2, groups, rank // groups, d_rows).transpose(1, 0, 2, 3).reshape(groups, -1, d_rows)
    expand = jnp.pad(expand, ((0, 0), (0, 0), (0, rank - d_rows)))
    small_gains = jnp.pad(
        gains[:, :d_rows].reshape(8, groups, per_dev_d).transpose(1, 0, 2), ((0, 0), (0, 8), (0, rank - per_dev_d))
    )
    small = jnp.concatenate([adapt, small_gains, expand], axis=1).astype(BF16)
    n_adapt = 3 * per_dev_d
    (small_sum,), = communicate(
        topo, "sum_small", 8, Scatter(topo, "dp", small, [(0, small.shape[1], "cx")])
    )
    per_seq = rank // groups // n_seq
    across = small_sum[n_adapt + 16 :, :d_rows].reshape(2, n_seq, per_seq, d_rows).transpose(1, 0, 2, 3)
    across = across.reshape(n_seq, 2 * per_seq, d_rows)
    (own_adapt, own_expand), = communicate(
        topo, "finish", 9, Finish(topo, small_sum[: n_adapt + 16], across)
    )
    grad_ga, grad_ua, grad_qa = own_adapt[:n_adapt].reshape(3, per_dev_d, rank)
    grad_gain_attn = own_adapt[n_adapt, :per_dev_d]
    grad_gain_mlp = own_adapt[n_adapt + 1, :per_dev_d]
    own_expand = own_expand.reshape(n_seq, 2, per_seq, d_rows).transpose(1, 2, 0, 3).reshape(2, per_seq, width)
    grad_de, grad_oe = own_expand[0], own_expand[1]
    grad_wk, grad_wv = grad_wkv[:, :HD], grad_wkv[:, HD:]
    grad_ka = dot_t(grad_wk.astype(BF16), key_expand)
    grad_va = dot_t(grad_wv.astype(BF16), value_expand)
    grad_ke, grad_ve = grad_kve[:, :HD], grad_kve[:, HD:]
    return (
        result_rows[None, None], grad_rows[None, None],
        grad_gain_attn, grad_gain_mlp,
        grad_wq, grad_wk, grad_wv, grad_wo, grad_wg, grad_wu, grad_wd,
        grad_qa, grad_qe, grad_ka, grad_ke, grad_va, grad_ve, grad_oa, grad_oe,
        grad_ga, grad_ge, grad_ua, grad_ue, grad_da, grad_de,
    )


def solution(mesh):
    topo = Topo(mesh.shape["dp"], mesh.shape["seq"])
    both = ("dp", "seq")
    in_specs = (
        P(None, "dp", "seq", None), P(None, "dp", "seq"), P(None, "dp", "seq", None),
        P(), P(), P(None, "dp"), P(), P(), P("dp", None), P(None, "dp"), P(None, "dp"), P("dp", None),
        P(), P(None, "dp"), P(), P(), P(), P(), P("dp", None), P(),
        P(), P(None, "dp"), P(), P(None, "dp"), P("dp", None), P(),
    )
    out_specs = (
        P(None, "dp", "seq", None), P(None, "dp", "seq", None), P(both), P(both),
        P("seq", "dp"), P(both, None), P(both, None), P("dp", "seq"), P("seq", "dp"), P("seq", "dp"), P("dp", "seq"),
        P(both, None), P("seq", "dp"), P(both, None), P(both, None), P(both, None), P(both, None),
        P("dp", "seq"), P(both, None), P(both, None), P("seq", "dp"), P(both, None), P("seq", "dp"),
        P("dp", "seq"), P(both, None),
    )
    return jax.shard_map(
        lambda *args: local(topo, *args), mesh=mesh, in_specs=in_specs, out_specs=out_specs, check_vma=False
    )
```

```python
import itertools
import math

import jax
import jax.numpy as jnp
from jax import lax
from jax.experimental import pallas as pl
from jax.experimental.pallas import tpu as pltpu
from jax.sharding import PartitionSpec as P

HD = 256
EPSILON = 1e-06
ROTARY_BASE = 10000.0
MASKED = -1e30

MESH = pl.DeviceIdType.MESH
BF16 = jnp.bfloat16
F32 = jnp.float32


class Topo:
    def __init__(self, n_dp, n_seq):
        self.n_dp, self.n_seq = n_dp, n_seq
        self.size = {"c": 2, "x": n_dp // 2, "b": n_seq // 4, "l": 2, "h": 2}

    def here(self):
        dp, seq = lax.axis_index("dp"), lax.axis_index("seq")
        nb = self.size["b"]
        outer = lax.div(seq, nb)
        return {
            "c": lax.rem(dp, 2),
            "x": lax.div(dp, 2),
            "b": lax.rem(seq, nb),
            "l": lax.rem(outer, 2),
            "h": lax.div(outer, 2),
        }

    def moved(self, at, dims, offsets, sign=1):
        new = dict(at)
        for dim, offset in zip(dims, offsets):
            n = self.size[dim]
            if not (isinstance(offset, int) and offset == 0):
                new[dim] = lax.rem(at[dim] + (offset if sign > 0 else n - offset), n)
        return new

    def seq_of(self, at):
        return (at["h"] * 2 + at["l"]) * self.size["b"] + at["b"]

    def device(self, at):
        return (at["x"] * 2 + at["c"], self.seq_of(at))

    def index(self, at, group):
        dp, seq = self.device(at)
        if group == "all":
            return dp * self.n_seq + seq
        if group == "half":
            nb = self.size["b"]
            return dp * (2 * nb) + at["l"] * nb + at["b"]
        if group == "dp":
            return dp
        if group == "seq":
            return seq
        if group == "quad":
            return at["l"] * self.size["b"] + at["b"]
        raise ValueError(group)

    def group_size(self, group):
        nb = self.size["b"]
        return {
            "all": self.n_dp * self.n_seq,
            "half": self.n_dp * 2 * nb,
            "dp": self.n_dp,
            "seq": self.n_seq,
            "quad": 2 * nb,
        }[group]


GROUP_DIMS = {"all": "cxblh", "half": "cxbl", "dp": "cx", "seq": "blh", "quad": "bl"}


def remote(src, dst, send_sem, recv_sem, device):
    return pltpu.make_async_remote_copy(
        src_ref=src,
        dst_ref=dst,
        send_sem=send_sem,
        recv_sem=recv_sem,
        device_id=device,
        device_id_type=MESH,
    )


def peers_of(topo, group):
    return {((dim, d),) for dim in GROUP_DIMS[group] for d in range(1, topo.size[dim])}


def digits(key, sizes):
    k = 0
    for o, s in zip(key, sizes):
        k = k * s + o
    return k


def arrived(topo, at, ref, send_sem, recv_sem):
    remote(ref, ref, send_sem, recv_sem, topo.device(at)).wait_recv()


class Gather:
    def __init__(self, topo, group, x, parts, beyond=None, need=None):
        self.topo, self.group, self.parts, self.beyond = topo, group, parts, beyond
        self.slots = "half" if beyond else group
        self.need = need or (lambda dims, key: 0)
        self.inputs = [x]
        rows, cols = x.shape
        n = topo.group_size(group)
        self.outputs = [jax.ShapeDtypeStruct((topo.group_size(self.slots), rows, cols), x.dtype)]
        self.in_specs = [pl.BlockSpec(memory_space=pl.ANY)]
        self.out_specs = [pl.BlockSpec(memory_space=pl.ANY)]
        self.scratch = [
            pltpu.SemaphoreType.DMA((len(parts), n)),
            pltpu.SemaphoreType.DMA((len(parts), n)),
            pltpu.SemaphoreType.DMA(()),
        ]

    def peers(self):
        return peers_of(self.topo, self.group)

    def keeps(self, order, key):
        return not self.beyond or key[order.index(self.beyond)] != 0

    def work(self):
        work = []
        for part, (row, rows, order) in enumerate(self.parts):
            for key in itertools.product(*[range(self.topo.size[dim]) for dim in order]):
                if not any(key) or self.keeps(order, key):
                    hops = sum(1 for o in key if o)
                    last = max([i for i, o in enumerate(key) if o], default=-1)
                    work.append((hops, self.need(order, key), last, part, key))
        work.sort()
        return [(w[3], w[4]) for w in work]

    def steps(self, at, ins, outs, scratch):
        topo = self.topo
        (x_ref,), (out_ref,) = ins, outs
        send_sem, recv_sem, own_sem = scratch
        size_of = lambda order: [topo.size[dim] for dim in order]

        def copy(part, key, stage, d):
            row, rows, order = self.parts[part]
            slot = topo.index(topo.moved(at, order, key, -1), self.slots)
            new_key = tuple(d if i == stage else o for i, o in enumerate(key))
            place = out_ref.at[slot, pl.ds(row, rows)]
            k = digits(new_key, size_of(order))
            target = topo.device(topo.moved(at, [order[stage]], [d]))
            source = place if any(key) else x_ref.at[pl.ds(row, rows)]
            return remote(source, place, send_sem.at[part, k], recv_sem.at[part, k], target)

        def own():
            return pltpu.make_async_copy(x_ref, out_ref.at[topo.index(at, self.slots)], own_sem)

        sent, steps = [], []
        for n, (part, key) in enumerate(self.work()):
            row, rows, order = self.parts[part]
            last = max([i for i, o in enumerate(key) if o], default=-1)
            sends = []
            for stage in range(last + 1, len(order)):
                for d in range(1, topo.size[order[stage]]):
                    new_key = tuple(d if i == stage else o for i, o in enumerate(key))
                    if self.keeps(order, new_key):
                        sends.append((self.need(order, new_key), stage, d))
            sends = [(part, key, stage, d) for _, stage, d in sorted(sends)]
            sent += sends

            def step(n=n, part=part, key=key, sends=sends):
                row, rows, order = self.parts[part]
                if n == 0 and not self.beyond:
                    own().start()
                if any(key):
                    slot = topo.index(topo.moved(at, order, key, -1), self.slots)
                    k = digits(key, size_of(order))
                    arrived(topo, at, out_ref.at[slot, pl.ds(row, rows)], send_sem.at[part, k], recv_sem.at[part, k])
                for send in sends:
                    copy(*send).start()

            steps.append(step)

        def end():
            for send in sent:
                copy(*send).wait_send()
            if not self.beyond:
                own().wait()

        return steps, [end]


TILE = 512


class Reduce:
    def __init__(self, topo, group, shape, dtype, parts):
        self.topo, self.group, self.parts, self.dtype = topo, group, parts, dtype
        n, rows, cols = shape
        assert n == topo.group_size(group), (n, group)
        self.tile = math.gcd(cols, TILE)

    def peers(self):
        return peers_of(self.topo, self.group)

    def stages(self, part):
        sizes = self.sizes(part)
        return [(max(s - 1, 1), math.prod(sizes[k + 1 :])) for k, s in enumerate(sizes)]

    def sizes(self, part):
        return [self.topo.size[dim] for dim in self.parts[part][2]]

    def jobs(self):
        jobs = []
        for part in range(len(self.parts)):
            sizes = self.sizes(part)
            keys = list(itertools.product(*[range(s) for s in sizes]))
            first = {k: min([i for i, o in enumerate(k) if o], default=len(sizes)) for k in keys}
            keys.sort(key=lambda k: (first[k], [0 if o else 1 for o in k]))
            jobs += [(first[key], rank, part, key) for rank, key in enumerate(keys)]
        jobs.sort()
        return [(first, part, key) for first, _, part, key in jobs]

    def block(self, at, part, key):
        return self.topo.index(self.topo.moved(at, self.parts[part][2], key), self.group)

    def target(self, at, part, key, stage):
        return self.topo.device(self.topo.moved(at, [self.parts[part][2][stage]], [key[stage]]))

    def place(self, part, key, stage):
        return key[stage] - 1, digits(key[stage + 1 :], self.sizes(part)[stage + 1 :])

    def terms(self, part, key, first):
        sizes = self.sizes(part)
        return [
            (stage, d - 1, digits(key[stage + 1 :], sizes[stage + 1 :]))
            for stage in range(first)
            for d in range(1, sizes[stage])
        ]


class VScatter(Reduce):
    def __init__(self, topo, group, shape, dtype, parts):
        super().__init__(topo, group, shape, dtype, parts)
        self.scratch = []
        for part, (row, nrows, order) in enumerate(parts):
            self.scratch.append(pltpu.VMEM((math.prod(self.sizes(part)[1:]), nrows, shape[2]), dtype))
            for m, rest in self.stages(part):
                self.scratch.append(pltpu.VMEM((m, rest, nrows, shape[2]), dtype))
                self.scratch.append(pltpu.SemaphoreType.DMA((m, rest)))
                self.scratch.append(pltpu.SemaphoreType.DMA((m, rest)))

    def steps(self, at, x_ref, out_ref, scratch):
        topo, tile = self.topo, self.tile
        scratch = list(scratch)
        bufs = []
        for part in range(len(self.parts)):
            acc = scratch.pop(0)
            bufs.append((acc, [tuple(scratch.pop(0) for _ in range(3)) for _ in self.sizes(part)]))
        jobs = self.jobs()

        def send(first, part, key):
            row, nrows, order = self.parts[part]
            acc, stages = bufs[part]
            buf, send_sem, recv_sem = stages[first]
            d, k = self.place(part, key, first)
            if first == 0:
                source = x_ref.at[self.block(at, part, key), pl.ds(row, nrows)]
            else:
                source = acc.at[digits(key[1:], self.sizes(part)[1:])]
            return remote(
                source, buf.at[d, k], send_sem.at[d, k], recv_sem.at[d, k], self.target(at, part, key, first)
            )

        def start():
            for job in jobs:
                if job[0] == 0:
                    send(*job).start()

        steps = [start]
        for job in jobs:
            if job[0] == 0:
                continue

            def step(job=job):
                first, part, key = job
                row, nrows, order = self.parts[part]
                acc, stages = bufs[part]
                terms = self.terms(part, key, first)
                for stage, d, k in terms:
                    buf, send_sem, recv_sem = stages[stage]
                    arrived(topo, at, buf.at[d, k], send_sem.at[d, k], recv_sem.at[d, k])
                block, kk = self.block(at, part, key), digits(key[1:], self.sizes(part)[1:])
                final = first == len(order)

                tiles = x_ref.shape[-1] // tile

                def add(n, _):
                    r0 = pl.multiple_of(lax.div(n, tiles) * 16, 16)
                    cols = pl.ds(pl.multiple_of(lax.rem(n, tiles) * tile, tile), tile)
                    r1 = pl.ds(pl.multiple_of(row + r0, 16), 16)
                    total = x_ref[block, r1, cols].astype(F32)
                    for stage, d, k in terms:
                        total = total + stages[stage][0][d, k, pl.ds(r0, 16), cols].astype(F32)
                    if final:
                        out_ref[r1, cols] = total.astype(out_ref.dtype)
                    else:
                        acc[kk, pl.ds(r0, 16), cols] = total.astype(acc.dtype)
                    return 0

                lax.fori_loop(0, nrows // 16 * tiles, add, 0)
                if not final:
                    send(*job).start()

            steps.append(step)

        def end():
            for job in jobs:
                if job[0] < len(self.parts[job[1]][2]):
                    send(*job).wait_send()

        return steps, [end]


class SlimScatter(Reduce):
    RING = 4

    def __init__(self, topo, group, shape, dtype, parts):
        super().__init__(topo, group, shape, dtype, parts)
        rows, cols = shape[1:]
        self.outputs = [jax.ShapeDtypeStruct((rows, cols), F32)]
        self.out_specs = [pl.BlockSpec(memory_space=pltpu.VMEM)]
        self.scratch = []
        self.most, self.cols = max(p[1] for p in parts), cols
        self.count = 1 + sum(topo.size[d] - 1 for d in GROUP_DIMS[group])
        for part, (row, nrows, order) in enumerate(parts):
            for m, rest in self.stages(part):
                self.outputs.append(jax.ShapeDtypeStruct((m, rest, nrows, cols), dtype))
                self.out_specs.append(pl.BlockSpec(memory_space=pl.ANY))
                self.scratch.append(pltpu.SemaphoreType.DMA((m, rest)))
                self.scratch.append(pltpu.SemaphoreType.DMA((m, rest)))

    def shared_scratch(self):
        return [
            pltpu.VMEM((2, self.count, self.most, self.cols), self.dtype),
            pltpu.SemaphoreType.DMA((2, self.count)),
            pltpu.VMEM((self.RING, self.most, self.cols), self.dtype),
        ]

    def steps(self, at, x_ref, outs, scratch, shared):
        topo, tile = self.topo, self.tile
        outs, scratch = list(outs), list(scratch)
        out_ref = outs.pop(0)
        stage_buf, stage_sem, ring = shared
        bufs = [
            [(outs.pop(0), scratch.pop(0), scratch.pop(0)) for _ in self.sizes(part)]
            for part in range(len(self.parts))
        ]
        jobs = self.jobs()
        later = [job for job in jobs if job[0] > 0]
        passed = [job for job in later if job[0] < len(self.parts[job[1]][2])]

        def own(part, key):
            row, nrows, order = self.parts[part]
            return x_ref.at[self.block(at, part, key), pl.ds(row, nrows)]

        def send(first, part, key, source=None):
            row, nrows, order = self.parts[part]
            buf, send_sem, recv_sem = bufs[part][first]
            d, k = self.place(part, key, first)
            if source is None:
                source = own(part, key) if first == 0 else ring.at[0, pl.ds(0, nrows)]
            return remote(
                source, buf.at[d, k], send_sem.at[d, k], recv_sem.at[d, k], self.target(at, part, key, first)
            )

        def loads(n):
            first, part, key = later[n]
            nrows = self.parts[part][1]
            sources = [own(part, key)] + [
                bufs[part][stage][0].at[d, k] for stage, d, k in self.terms(part, key, first)
            ]
            return [
                pltpu.make_async_copy(ref, stage_buf.at[n % 2, i, pl.ds(0, nrows)], stage_sem.at[n % 2, i])
                for i, ref in enumerate(sources)
            ]

        def fetch(n):
            first, part, key = later[n]
            for stage, d, k in self.terms(part, key, first):
                buf, send_sem, recv_sem = bufs[part][stage]
                arrived(topo, at, buf.at[d, k], send_sem.at[d, k], recv_sem.at[d, k])
            for cp in loads(n):
                cp.start()

        def start():
            for job in jobs:
                if job[0] == 0:
                    send(*job).start()

        steps = [start, lambda: fetch(0)]
        for n in range(len(later)):

            def step(n=n):
                first, part, key = later[n]
                row, nrows, order = self.parts[part]
                copies = loads(n)
                for cp in copies:
                    cp.wait()
                final = first == len(order)
                if not final:
                    sent = passed.index(later[n])
                    if sent >= self.RING:
                        send(*passed[sent - self.RING]).wait_send()

                tiles = self.cols // tile

                def add(n_tile, _):
                    r0 = pl.multiple_of(lax.div(n_tile, tiles) * 16, 16)
                    cols = pl.ds(pl.multiple_of(lax.rem(n_tile, tiles) * tile, tile), tile)
                    total = stage_buf[n % 2, 0, pl.ds(r0, 16), cols].astype(F32)
                    for i in range(1, len(copies)):
                        total = total + stage_buf[n % 2, i, pl.ds(r0, 16), cols].astype(F32)
                    if final:
                        out_ref[pl.ds(pl.multiple_of(row + r0, 16), 16), cols] = total
                    else:
                        ring[sent % self.RING, pl.ds(r0, 16), cols] = total.astype(ring.dtype)
                    return 0

                lax.fori_loop(0, nrows // 16 * tiles, add, 0)
                if not final:
                    send(first, part, key, ring.at[sent % self.RING, pl.ds(0, nrows)]).start()
                if n + 1 < len(later):
                    fetch(n + 1)

            steps.append(step)

        def end():
            for job in jobs:
                if job[0] == 0:
                    send(*job).wait_send()
            for job in passed[-self.RING :]:
                send(*job).wait_send()

        return steps, [end]


class Exchange:
    def __init__(self, topo, group, x):
        self.topo, self.group = topo, group
        self.inputs = [x]
        n = x.shape[0]
        assert n == topo.group_size(group)
        self.outputs = [jax.ShapeDtypeStruct(x.shape, x.dtype)]
        self.in_specs = [pl.BlockSpec(memory_space=pl.ANY)]
        self.out_specs = [pl.BlockSpec(memory_space=pl.ANY)]
        self.scratch = [
            pltpu.SemaphoreType.DMA((n,)),
            pltpu.SemaphoreType.DMA((n,)),
            pltpu.SemaphoreType.DMA(()),
        ]

    def offsets(self):
        dims = GROUP_DIMS[self.group]
        return dims, [
            o for o in itertools.product(*[range(self.topo.size[d]) for d in dims]) if any(o)
        ]

    def peers(self):
        dims, offsets = self.offsets()
        return {tuple((dim, o) for dim, o in zip(dims, off) if o) for off in offsets}

    def steps(self, at, ins, outs, scratch):
        topo = self.topo
        (x_ref,), (out_ref,) = ins, outs
        send_sem, recv_sem, own_sem = scratch
        dims, offsets = self.offsets()
        me = topo.index(at, self.group)

        def own():
            return pltpu.make_async_copy(x_ref.at[me], out_ref.at[me], own_sem)

        def send(i):
            there = topo.moved(at, dims, offsets[i])
            source = x_ref.at[topo.index(there, self.group)]
            return remote(source, out_ref.at[me], send_sem.at[i], recv_sem.at[i], topo.device(there))

        def start():
            own().start()
            for i in range(len(offsets)):
                send(i).start()

        def wait(i):
            ref = out_ref.at[topo.index(topo.moved(at, dims, offsets[i], -1), self.group)]
            arrived(topo, at, ref, send_sem.at[i], recv_sem.at[i])

        def end():
            for i in range(len(offsets)):
                send(i).wait_send()
            own().wait()

        return [start] + [lambda i=i: wait(i) for i in range(len(offsets))], [end]


class Finish:
    def __init__(self, topo, x, y):
        self.topo = topo
        self.inputs = [x, y]
        self.outputs = [
            jax.ShapeDtypeStruct(x.shape, x.dtype),
            jax.ShapeDtypeStruct(y.shape, y.dtype),
        ]
        self.in_specs = [pl.BlockSpec(memory_space=pl.ANY)] * 2
        self.out_specs = [pl.BlockSpec(memory_space=pl.ANY)] * 2
        self.inner = Exchange(topo, "seq", y)
        self.scratch = self.inner.scratch + [pltpu.SemaphoreType.DMA(())] * 3

    def peers(self):
        return self.inner.peers()

    def route(self):
        topo = self.topo
        dp, seq = lax.axis_index("dp"), lax.axis_index("seq")
        n = seq * topo.n_dp + dp
        target = (lax.div(n, topo.n_seq), lax.rem(n, topo.n_seq))
        m = dp * topo.n_seq + seq
        source = (lax.rem(m, topo.n_dp), lax.div(m, topo.n_dp))
        stays = (target[0] == dp) & (target[1] == seq)
        return target, source, stays

    def greet(self, barrier):
        target, source, stays = self.route()

        @pl.when(jnp.logical_not(stays))
        def _():
            pl.semaphore_signal(barrier, inc=1, device_id=source, device_id_type=MESH)

        return jnp.where(stays, 0, 1)

    def steps(self, at, ins, outs, scratch):
        (x_ref, y_ref), (x_out, y_out) = ins, outs
        send_sem, recv_sem, own_sem = scratch[3:]
        target, source, stays = self.route()
        cp = remote(x_ref, x_out, send_sem, recv_sem, target)
        own = pltpu.make_async_copy(x_ref, x_out, own_sem)
        inner, ends = self.inner.steps(at, [y_ref], [y_out], scratch[:3])

        def start():
            pl.when(stays)(own.start)
            pl.when(jnp.logical_not(stays))(cp.start)

        def end():
            pl.when(stays)(own.wait)
            pl.when(jnp.logical_not(stays))(cp.wait)

        return [start] + inner, ends + [end]


def greet(topo, ops):
    at = topo.here()
    peers = sorted(set().union(*[op.peers() for op in ops]))
    barrier = pltpu.get_barrier_semaphore()
    for peer in peers:
        there = topo.device(topo.moved(at, [p[0] for p in peer], [p[1] for p in peer]))
        pl.semaphore_signal(barrier, inc=1, device_id=there, device_id_type=MESH)
    count = len(peers)
    for op in ops:
        if hasattr(op, "greet"):
            count = count + op.greet(barrier)
    pl.semaphore_wait(barrier, count)
    return at


class Steps:
    def __init__(self, steps):
        self.todo = steps[0] + steps[1]

    def run(self, count=1):
        for _ in range(count):
            if self.todo:
                self.todo.pop(0)()

    def finish(self):
        self.run(len(self.todo))


def run_slot(t, slots):
    def tree(low, high):
        if not any(slots[low:high]):
            return
        if high - low == 1:
            for step in slots[low]:
                step()
            return
        middle = (low + high) // 2
        left, right = any(slots[low:middle]), any(slots[middle:high])
        if left and right:
            lax.cond(t < middle, lambda: tree(low, middle), lambda: tree(middle, high))
        elif left:
            pl.when(t < middle)(lambda: tree(low, middle))
        else:
            pl.when(t >= middle)(lambda: tree(middle, high))

    tree(0, len(slots))


def communicate(topo, name, collective_id, *ops):
    n_in = [len(op.inputs) for op in ops]
    n_out = [len(op.outputs) for op in ops]
    n_scratch = [len(op.scratch) for op in ops]

    def kernel(*refs):
        refs = list(refs)
        take = lambda counts: [[refs.pop(0) for _ in range(k)] for k in counts]
        ins, outs, scratch = take(n_in), take(n_out), take(n_scratch)
        at = greet(topo, ops)
        running = [Steps(op.steps(at, i, o, s)) for op, i, o, s in zip(ops, ins, outs, scratch)]
        while any(r.todo for r in running):
            for r in running:
                r.run()

    results = pl.pallas_call(
        kernel,
        name=name,
        out_shape=[s for op in ops for s in op.outputs],
        in_specs=[s for op in ops for s in op.in_specs],
        out_specs=[s for op in ops for s in op.out_specs],
        scratch_shapes=[s for op in ops for s in op.scratch],
        compiler_params=pltpu.CompilerParams(
            collective_id=collective_id, has_side_effects=True, vmem_limit_bytes=58 << 20
        ),
    )(*[x for op in ops for x in op.inputs])
    results = list(results)
    return [[results.pop(0) for _ in range(k)] for k in n_out]


class Scatter(VScatter):
    def __init__(self, topo, group, x, parts):
        super().__init__(topo, group, x.shape, x.dtype, parts)
        self.inputs = [x]
        self.outputs = [jax.ShapeDtypeStruct(x.shape[1:], F32)]
        self.in_specs = [pl.BlockSpec(memory_space=pltpu.VMEM)]
        self.out_specs = [pl.BlockSpec(memory_space=pltpu.VMEM)]

    def steps(self, at, ins, outs, scratch):
        return super().steps(at, ins[0], outs[0], scratch)


def row_parts(rows, orders, weights, step=16):
    parts, row, total = [], 0, sum(weights)
    for i, (order, weight) in enumerate(zip(orders, weights)):
        n = rows - row if i == len(orders) - 1 else min(rows - row, int(round(rows * weight / total / step)) * step)
        if n:
            parts.append((row, n, order))
            row += n
    return parts


def matmul(left, right):
    return jnp.dot(left, right, preferred_element_type=jnp.float32)


def contract(form, left, right):
    return jnp.einsum(form, left, right, preferred_element_type=jnp.float32)


def rotary(positions, size):
    half_size = size // 2
    frequency = ROTARY_BASE ** (-(jnp.arange(half_size, dtype=jnp.float32) * 2.0) / size)
    angles = positions.astype(jnp.float32)[:, None] * frequency[None, :]
    return (jnp.cos(angles), jnp.sin(angles))


def rotate(values, cosine_table, sine_table):
    half_size = values.shape[-1] // 2
    first_half = values[..., :half_size]
    second_half = values[..., half_size:]
    return jnp.concatenate(
        [
            first_half * cosine_table - second_half * sine_table,
            second_half * cosine_table + first_half * sine_table,
        ],
        axis=-1,
    )


def normalize(values, gain_vector):
    inverse_rms = lax.rsqrt(jnp.mean(values * values, axis=-1, keepdims=True) + EPSILON)
    unit_rows = values * inverse_rms
    return (unit_rows * gain_vector, unit_rows, inverse_rms)


def norm_backward(grad_normed, unit_rows, inverse_rms, gain_vector):
    gain_term = jnp.sum(grad_normed * unit_rows, axis=0)
    grad_unit = grad_normed * gain_vector
    inner = jnp.mean(grad_unit * unit_rows, axis=-1, keepdims=True)
    return (gain_term, inverse_rms * (grad_unit - unit_rows * inner))


def dot_t(left, right):
    return lax.dot_general(left, right, (((1,), (1,)), ((), ())), preferred_element_type=F32)


def t_dot(left, right):
    return lax.dot_general(left, right, (((0,), (0,)), ((), ())), preferred_element_type=F32)


GELU_C = math.sqrt(2.0 / math.pi)


def gelu_parts(v):
    square = v * v
    t = jnp.tanh(GELU_C * (v + 0.044715 * v * square))
    half_up = 0.5 * (1.0 + t)
    slope = half_up + 0.5 * v * (1.0 - t * t) * (GELU_C * (1.0 + 3.0 * 0.044715 * square))
    return v * half_up, slope


def feed_forward(
    topo, collective_id, normed, grads, grads_half,
    w_gate, w_up, w_down, gate_adapt, gate_expand, up_adapt, up_expand, down_adapt, down_expand,
):
    rows, width = normed.shape
    quad = topo.group_size("quad")
    half = topo.group_size("half")
    units = w_gate.shape[1] // quad
    rank = gate_adapt.shape[1]
    ranks = rank // 2
    half_width = width // 2
    d_rows, r_rows = half_width // quad, ranks // quad
    per_chunk = 512 // rows
    tile = 512
    block = 256

    dims = "hxclb"
    keys = list(itertools.product(*[range(topo.size[d]) for d in dims]))
    chunks = [keys[i : i + per_chunk] for i in range(0, len(keys), per_chunk)]
    own = len(chunks) // 2
    chunk_of = {key: i for i, keys_of in enumerate(chunks) for key in keys_of}

    def need(order, key):
        at_dim = dict(zip(order, key))
        return chunk_of[tuple(at_dim.get(d, 0) for d in dims)]

    near = row_parts(rows, ("xlbc", "lbxc", "bxlc"), (1, 1, 1))
    far = row_parts(rows, ("hxlbc", "hlbxc", "hbxlc"), (1, 1, 1))
    gather_n = Gather(topo, "half", normed, near, need=need)
    far_n = Gather(topo, "all", normed, far, beyond="h", need=need)
    far_g = Gather(topo, "all", grads, far, beyond="h", need=need)
    thirds = row_parts(rows, ("cxbl", "cblx", "clxb"), (1, 1, 1))
    sum_n = SlimScatter(topo, "half", (half, rows, width), BF16, thirds)
    sum_d = SlimScatter(topo, "half", (half, rows, width), BF16, thirds)
    comm = [gather_n, far_n, far_g, sum_n, sum_d]

    inputs = [
        normed, grads, grads_half, w_gate, w_up, w_down,
        gate_adapt, gate_expand, up_adapt, up_expand, down_adapt, down_expand,
    ]
    part = jax.ShapeDtypeStruct((half, rows, width), BF16)
    grad = jax.ShapeDtypeStruct((quad, d_rows + r_rows, units), BF16)
    any_spec = pl.BlockSpec(memory_space=pl.ANY)
    out_shape = [part, part, grad, grad, grad]
    out_specs = [any_spec] * 5
    scratch = [
        pltpu.VMEM((width, units), BF16), pltpu.VMEM((width, units), BF16), pltpu.VMEM((units, width), BF16),
        pltpu.VMEM((width, rank), BF16), pltpu.VMEM((rank, units), BF16),
        pltpu.VMEM((width, rank), BF16), pltpu.VMEM((rank, units), BF16),
        pltpu.VMEM((units, rank), BF16), pltpu.VMEM((rank, width), BF16),
        pltpu.VMEM((half_width + ranks, units), F32),
        pltpu.VMEM((half_width + ranks, units), F32),
        pltpu.VMEM((half_width + ranks, units), F32),
        pltpu.VMEM((3, tile, units), BF16),
        pltpu.VMEM((3, tile, ranks), BF16),
        pltpu.VMEM((2, tile, width), BF16), pltpu.VMEM((2, tile, width), BF16),
        pltpu.VMEM((tile, width), BF16), pltpu.VMEM((tile, width), BF16),
        pltpu.SemaphoreType.DMA((9,)),
        pltpu.SemaphoreType.DMA((2, 2, per_chunk)),
        pltpu.SemaphoreType.DMA((2, per_chunk)),
        pltpu.SemaphoreType.DMA((3,)),
    ]
    n_own = len(scratch)
    shared = sum_n.shared_scratch() + sum_d.shared_scratch()
    scratch = scratch + shared
    for op in comm:
        out_shape = out_shape + op.outputs
        out_specs = out_specs + op.out_specs
        scratch = scratch + op.scratch

    def kernel(*refs):
        refs = list(refs)
        (
            n_hbm, g_hbm, g_half, wg_hbm, wu_hbm, wd_hbm, ga_hbm, ge_hbm, ua_hbm, ue_hbm, da_hbm, de_hbm,
        ) = [refs.pop(0) for _ in inputs]
        down_part, gn_part, dg_out, du_out, dd_out = [refs.pop(0) for _ in range(5)]
        op_outs = [[refs.pop(0) for _ in op.outputs] for op in comm]
        (
            wg, wu, wd, ga, ge, ua, ue, da, de, acc_g, acc_u, acc_d, acts, low_s, n_buf, g_buf, down_st, gn_st,
            w_sem, load_sem, store_sem, grad_sem,
        ) = [refs.pop(0) for _ in range(n_own)]
        shared_refs = [refs.pop(0) for _ in shared]
        op_scratch = [[refs.pop(0) for _ in op.scratch] for op in comm]
        mix_s, gg_s, gu_s = acts.at[0], acts.at[1], acts.at[2]
        at = topo.here()
        high = at["h"]
        member = topo.index(at, "quad")
        unit_at = pl.multiple_of(member * units, units)

        w_copies = [
            pltpu.make_async_copy(src, dst, w_sem.at[i])
            for i, (src, dst) in enumerate(
                (
                    (de_hbm, de),
                    (da_hbm.at[pl.ds(unit_at, units), :], da),
                    (wd_hbm.at[pl.ds(unit_at, units), :], wd),
                    (ga_hbm, ga),
                    (ge_hbm.at[:, pl.ds(unit_at, units)], ge),
                    (wg_hbm.at[:, pl.ds(unit_at, units)], wg),
                    (ua_hbm, ua),
                    (ue_hbm.at[:, pl.ds(unit_at, units)], ue),
                    (wu_hbm.at[:, pl.ds(unit_at, units)], wu),
                )
            )
        ]
        for cp in w_copies:
            cp.start()

        greet(topo, comm)
        gathers = (gather_n, far_n, far_g)
        all_steps = [
            op.steps(at, [x], o, sc) for op, x, o, sc in zip(gathers, (n_hbm, n_hbm, g_hbm), op_outs, op_scratch)
        ]
        ranked = []
        for g, (op, (steps_g, _)) in enumerate(zip(gathers, all_steps)):
            for i, (f, (p, k)) in enumerate(zip(steps_g, op.work())):
                when = NEAR_US * i / len(steps_g) - 20.0 if g == 0 else FAR_AT + (g + 2 * i) * FAR_US
                ranked.append((when if any(k) or g else -1e3, g, i, f, need(op.parts[p][2], k)))
        ranked.sort(key=lambda w: w[:3])
        steps = [(f, chunk) for _, _, _, f, chunk in ranked]
        when_of = [w[0] for w in ranked]
        started = len(gather_n.parts)
        for f, _ in steps[:started]:
            f()

        def upto(chunk, done):
            last = [i for i, (_, c) in enumerate(steps) if c <= chunk and i >= started]
            return max([done] + [i + 1 for i in last])

        acc_g[...] = jnp.zeros_like(acc_g)
        acc_u[...] = jnp.zeros_like(acc_u)
        acc_d[...] = jnp.zeros_like(acc_d)

        def merge_rows(weight, adapt, expand, total):
            def one(i, _):
                r = pl.ds(pl.multiple_of(i * block, block), block)
                weight[r, :] = (weight[r, :].astype(F32) + matmul(adapt[r, :], expand[...])).astype(BF16)
                return 0

            lax.fori_loop(0, total // block, one, 0)

        for cp in w_copies[:3]:
            cp.wait()
        merge_rows(wd, da, de, units)
        for cp in w_copies[3:6]:
            cp.wait()
        merge_rows(wg, ga, ge, width)
        for cp in w_copies[6:]:
            cp.wait()
        merge_rows(wu, ua, ue, width)

        def key_of(c, i):
            k = c * per_chunk + i
            key = []
            for d in reversed(dims):
                key.append(lax.rem(k, topo.size[d]))
                k = lax.div(k, topo.size[d])
            return key[::-1]

        def chunk_copies(c, slot, other):
            copies = []
            for i in range(per_chunk):
                origin = topo.moved(at, dims, key_of(c, i), -1)
                r = pl.ds(i * rows, rows)
                in_half = topo.index(origin, "half")
                n_src, g_src = (op_outs[1][0], op_outs[2][0]) if other else (op_outs[0][0], g_half)
                copies.append(pltpu.make_async_copy(n_src.at[in_half], n_buf.at[slot, r], load_sem.at[slot, 0, i]))
                copies.append(pltpu.make_async_copy(g_src.at[in_half], g_buf.at[slot, r], load_sem.at[slot, 1, i]))
            return copies

        def first_copies():
            copies = chunk_copies(0, 0, False)
            r = pl.ds(0, rows)
            copies[0] = pltpu.make_async_copy(n_hbm, n_buf.at[0, r], load_sem.at[0, 0, 0])
            return copies

        def store_copies(c):
            copies = []
            for i in range(per_chunk):
                slot = topo.index(topo.moved(at, dims, key_of(c, i), -1), "half")
                r = pl.ds(i * rows, rows)
                copies.append(pltpu.make_async_copy(down_st.at[r], down_part.at[slot], store_sem.at[0, i]))
                copies.append(pltpu.make_async_copy(gn_st.at[r], gn_part.at[slot], store_sem.at[1, i]))
            return copies

        n_one, n_two, n_three = units // block, width // block, half_width // block
        scale = units / 1024
        kinds = {
            False: [("one", n_one, 1.9), ("two", n_two, 1.0 * scale), ("pre", 1, 2.0 * scale), ("three", n_three, 0.7 * scale)],
            True: [("one", n_one, 1.9), ("pre", 1, 2.0 * scale), ("three", n_three, 0.7 * scale)],
        }
        slots = {(other, kind): [[] for _ in range(own * n)] for other in (False, True) for kind, n, _ in kinds[other]}
        done = upto(0, started)
        for f, _ in steps[started:done]:
            f()
        clock = 0.0
        for c in range(len(chunks)):
            other = c >= own
            for kind, n, cost in kinds[other]:
                for i in range(n):
                    clock += cost
                    target = max(done, sum(1 for w in when_of if w <= clock))
                    if kind == "pre" and c + 1 < len(chunks):
                        target = upto(c + 1, target)
                    slots[other, kind][(c - own if other else c) * n + i] += [f for f, _ in steps[done:target]]
                    done = target
        sum_a = sum_n.steps(at, gn_part, op_outs[3], op_scratch[3], shared_refs[:3])
        sum_b = sum_d.steps(at, down_part, op_outs[4], op_scratch[4], shared_refs[3:])
        sums = [sum_a[0][0], sum_b[0][0]]
        for i in range(1, max(len(sum_a[0]), len(sum_b[0]))):
            sums += sum_a[0][i : i + 1] + sum_b[0][i : i + 1]
        clock, summed = 0.0, 0
        for c in range(own):
            for kind, n, cost in kinds[True]:
                for i in range(n):
                    clock += cost
                    target = min(len(sums), 2 + int(max(clock - 3.0, 0.0) / SUM_US))
                    if kind != "pre":
                        slots[True, kind][c * n + i] += sums[summed:target]
                        summed = target

        for cp in first_copies():
            cp.start()
        low_cols = pl.ds(pl.multiple_of(high * ranks, ranks), ranks)
        half_at = high * half_width

        def chunk_loop(other):
            first = own if other else 0

            def body(k, _):
                c = first + k
                slot = lax.rem(c, 2)
                nb, gb = n_buf.at[slot], g_buf.at[slot]
                for cp in chunk_copies(c, slot, other):
                    cp.wait()
                low_s[0] = matmul(nb[...], ga[:, low_cols]).astype(BF16)
                low_s[1] = matmul(nb[...], ua[:, low_cols]).astype(BF16)
                low_s[2] = dot_t(gb[...], de[low_cols, :]).astype(BF16)

                def one(i, _):
                    cols = pl.ds(pl.multiple_of(i * block, block), block)
                    gate = matmul(nb[...], wg[:, cols])
                    up = matmul(nb[...], wu[:, cols])
                    act, slope = gelu_parts(gate)
                    gm = dot_t(gb[...], wd[cols, :])
                    mix_s[:, cols] = (act * up).astype(BF16)
                    gg_s[:, cols] = (gm * up * slope).astype(BF16)
                    gu_s[:, cols] = (gm * act).astype(BF16)
                    run_slot(k * n_one + i, slots[other, "one"])
                    return 0

                lax.fori_loop(0, n_one, one, 0)
                if not other:

                    @pl.when(c > 0)
                    def _():
                        for cp in store_copies(c - 1):
                            cp.wait()

                    def two(i, _):
                        cols = pl.ds(pl.multiple_of(i * block, block), block)
                        down_st[:, cols] = matmul(mix_s[...], wd[:, cols]).astype(BF16)
                        gn_st[:, cols] = (dot_t(gg_s[...], wg[cols, :]) + dot_t(gu_s[...], wu[cols, :])).astype(BF16)
                        run_slot(k * n_two + i, slots[other, "two"])
                        return 0

                    lax.fori_loop(0, n_two, two, 0)
                    for cp in store_copies(c):
                        cp.start()
                for i, (acc, grads_s) in enumerate(((acc_g, gg_s), (acc_u, gu_s), (acc_d, mix_s))):
                    acc[half_width:, :] += t_dot(low_s[i], grads_s[...])
                run_slot(k, slots[other, "pre"])
                if other:

                    @pl.when(c + 1 < len(chunks))
                    def _():
                        for cp in chunk_copies(c + 1, 1 - slot, True):
                            cp.start()

                else:

                    @pl.when(c + 1 < own)
                    def _():
                        for cp in chunk_copies(c + 1, 1 - slot, False):
                            cp.start()

                    @pl.when(c + 1 == own)
                    def _():
                        for cp in chunk_copies(c + 1, 1 - slot, True):
                            cp.start()

                def three(i, _):
                    r = pl.ds(pl.multiple_of(i * block, block), block)
                    cols = pl.ds(pl.multiple_of(half_at + i * block, block), block)
                    acc_g[r, :] += t_dot(nb[:, cols], gg_s[...])
                    acc_u[r, :] += t_dot(nb[:, cols], gu_s[...])
                    acc_d[r, :] += t_dot(gb[:, cols], mix_s[...])
                    run_slot(k * n_three + i, slots[other, "three"])
                    return 0

                lax.fori_loop(0, n_three, three, 0)
                return 0

            lax.fori_loop(0, own, body, 0)

        chunk_loop(False)
        for cp in store_copies(own - 1):
            cp.wait()
        chunk_loop(True)

        pending = []
        for q in range(quad):
            for k, (acc, out) in enumerate(((acc_g, dg_out), (acc_u, du_out), (acc_d, dd_out))):
                if len(pending) >= 3:
                    pending.pop(0).wait()
                acts[k, :d_rows, :] = acc[q * d_rows : (q + 1) * d_rows, :].astype(BF16)
                acts[k, d_rows : d_rows + r_rows, :] = acc[
                    half_width + q * r_rows : half_width + (q + 1) * r_rows, :
                ].astype(BF16)
                cp = pltpu.make_async_copy(acts.at[k, pl.ds(0, d_rows + r_rows)], out.at[q], grad_sem.at[k])
                cp.start()
                pending.append(cp)
        for f in steps[done:]:
            f[0]()
        for f in sums[summed:]:
            f()
        for cp in pending:
            cp.wait()
        for f in [f for _, end in all_steps for f in end] + sum_a[1] + sum_b[1]:
            f()

    flops = 2 * rows * topo.n_dp * topo.n_seq * units * width * 9
    results = pl.pallas_call(
        kernel,
        name="feed_forward",
        out_shape=out_shape,
        in_specs=[any_spec] * len(inputs),
        out_specs=out_specs,
        scratch_shapes=scratch,
        compiler_params=pltpu.CompilerParams(
            collective_id=collective_id, has_side_effects=True, vmem_limit_bytes=60 << 20
        ),
        cost_estimate=pl.CostEstimate(flops=flops, bytes_accessed=1 << 27, transcendentals=0),
    )(*inputs)
    dg, du, dd = results[2:5]
    skip = 5 + sum(len(op.outputs) for op in (gather_n, far_n, far_g))
    return results[skip + len(sum_n.outputs)], results[skip], dg, du, dd


NEAR_US = 45.0
FAR_AT = 5.0
FAR_US = 0.55
SUM_US = 1.1


def attention_back(
    topo, collective_id, grad_branch, grad_middle, query_rot, heads_out, key_value, log_total, own_segs, key_segs,
    normed_all, unit_attn, rms_attn, gain_attn, gain_mlp_term, cosine, sine, wo, wq, wk, wv,
    query_adapt, out_expand, key_adapt, value_adapt, dg, du, dd,
):
    groups, rows, width = normed_all.shape
    n_seq = topo.n_seq
    length = rows * n_seq
    head_cols = heads_out.shape[1]
    heads = head_cols // HD
    tokens = groups * rows
    rank = query_adapt.shape[1]
    scale = HD ** (-0.5)
    d_rows, r_rows = width // n_seq, rank // n_seq
    share_d, share_r = width // groups, rank // groups
    kv_d, kv_r = d_rows // groups, r_rows // groups
    kv_pad = -(-kv_r // 16) * 16
    kv_rows = kv_d + kv_pad + 16

    gather_g = Gather(topo, "dp", grad_branch, [(0, rows, "xc")])
    gather_kv = Gather(topo, "dp", jax.ShapeDtypeStruct((rows, 2 * HD), BF16), [(0, rows, "xc")])
    swaps = [Exchange(topo, "quad", a) for a in (dg, du, dd)]
    seq_parts = lambda n: row_parts(n, ("blh", "lhb"), (9, 5))
    w_shape = (n_seq, d_rows + r_rows, head_cols)
    sum_o = VScatter(topo, "seq", w_shape, BF16, seq_parts(d_rows + r_rows))
    sum_q = VScatter(topo, "seq", w_shape, BF16, seq_parts(d_rows + r_rows))
    sum_k = VScatter(topo, "seq", (n_seq, kv_rows, 2 * HD), BF16, seq_parts(kv_rows))
    kv_shape = (groups * n_seq, rows, 2 * HD)
    sum_kv = VScatter(topo, "all", kv_shape, BF16, row_parts(rows, ("cxblh", "cblhx"), (1, 1)))
    sum_n = VScatter(topo, "dp", (groups, rows, width), BF16, [(0, rows, "cx")])

    inputs = [
        grad_branch, grad_middle, query_rot, heads_out, key_value, log_total, own_segs, key_segs,
        normed_all, unit_attn, rms_attn, gain_attn, gain_mlp_term, cosine, sine, wo, wq, wk, wv,
        query_adapt, out_expand, key_adapt, value_adapt, dg, du, dd,
    ]
    vmem, anywhere = pl.BlockSpec(memory_space=pltpu.VMEM), pl.BlockSpec(memory_space=pl.ANY)
    big = groups * n_seq > 32
    in_specs = [anywhere] + [vmem] * (len(inputs) - 4) + [anywhere] * 3
    if big:
        in_specs[4] = anywhere
    out_shape = [
        jax.ShapeDtypeStruct((rows, width), BF16),
        jax.ShapeDtypeStruct((d_rows + r_rows, head_cols), F32),
        jax.ShapeDtypeStruct((d_rows + r_rows, head_cols), F32),
        jax.ShapeDtypeStruct((kv_rows, 2 * HD), F32),
    ] + [op.outputs[0] for op in swaps]
    out_specs = [vmem] * 4 + [anywhere] * 3
    if big:
        sum_kv = SlimScatter(topo, "all", kv_shape, BF16, row_parts(rows, ("cxblh", "cblhx"), (1, 1)))
        out_shape = out_shape + [jax.ShapeDtypeStruct(kv_shape, BF16)] + sum_kv.outputs
        out_specs = out_specs + [anywhere] + sum_kv.out_specs
    scratch = [
        pltpu.VMEM((groups, rows, width), BF16),
        pltpu.VMEM((tokens, head_cols), BF16),
        pltpu.VMEM((tokens, head_cols), BF16),
        pltpu.VMEM(w_shape, BF16),
        pltpu.VMEM(w_shape, BF16),
        pltpu.VMEM((n_seq, kv_rows, 2 * HD), BF16),
        pltpu.VMEM((length, 2 * HD) if big else kv_shape, BF16),
        pltpu.VMEM((groups, rows, width), BF16),
        pltpu.VMEM((rows, 2 * HD), F32),
        pltpu.VMEM((rows, width), F32),
        pltpu.VMEM((rows, 2 * HD), BF16),
        pltpu.VMEM((groups, rows, 2 * HD), BF16),
        pltpu.SemaphoreType.DMA((n_seq,)),
    ]
    n_own = len(scratch)
    shared = sum_kv.shared_scratch() + [pltpu.VMEM((length, 2 * HD), BF16)] if big else []
    scratch = scratch + shared
    ops = [gather_g, gather_kv] + swaps + [sum_o, sum_q, sum_k, sum_kv, sum_n]
    for op in ops:
        scratch = scratch + op.scratch

    def kernel(*refs):
        refs = list(refs)
        (
            gb_hbm, gmid, qrot, hout, kv, lse, own_seg, key_seg, norm_all, unit, rms, gain, gain_term, cos, sin,
            wo_r, wq_r, wk_r, wv_r, qa, oe, ka, va, dg_r, du_r, dd_r,
        ) = [refs.pop(0) for _ in inputs]
        grad_rows, so_out, sq_out, sk_out, dg_o, du_o, dd_o = [refs.pop(0) for _ in range(7)]
        kv_outs = [refs.pop(0) for _ in out_shape[7:]]
        (
            ga, gh, gq, xo, xq, xk, xkv, xn, kv_sum, n_sum, gkv, gkv_all, load_sem,
        ) = [refs.pop(0) for _ in range(n_own)]
        shared_refs = [refs.pop(0) for _ in shared]
        op_scratch = [[refs.pop(0) for _ in op.scratch] for op in ops]
        dp = lax.axis_index("dp")
        at = greet(topo, ops)
        get_g = Steps(gather_g.steps(at, [gb_hbm], [ga], op_scratch[0]))
        get_g.run()
        moves = [
            Steps(op.steps(at, [r], [o], sc))
            for op, r, o, sc in zip(swaps, (dg_r, du_r, dd_r), (dg_o, du_o, dd_o), op_scratch[2:5])
        ]
        moves[0].run()
        get_g.finish()
        flat = lambda ref: ref[...].reshape(tokens, ref.shape[-1])
        moves[1].run()

        gh[...] = dot_t(flat(ga), wo_r[...]).astype(BF16)
        for j in range(n_seq):
            part = t_dot(ga[:, :, j * d_rows : (j + 1) * d_rows].reshape(tokens, d_rows), hout[...])
            xo[j, :d_rows, :] = part.astype(BF16)
        low = dot_t(flat(ga), oe[...]).astype(BF16)
        part = t_dot(low, hout[...]).astype(BF16)
        for j in range(n_seq):
            xo[j, d_rows:, :] = part[j * r_rows : (j + 1) * r_rows, :]
        get_o = Steps(sum_o.steps(at, xo, so_out, op_scratch[5]))
        get_o.run()

        seq = lax.axis_index("seq")
        key_at = lax.broadcasted_iota(jnp.int32, (heads * rows, length), 1)
        row_at = lax.broadcasted_iota(jnp.int32, (heads * rows, length), 0)
        causal = key_at <= seq * rows + lax.rem(row_at, rows)
        for s in range(groups):
            r = slice(s * rows, (s + 1) * rows)
            stack = lambda ref: jnp.concatenate([ref[r, h * HD : (h + 1) * HD] for h in range(heads)], axis=0)
            q, d_o = stack(qrot), stack(gh)
            if big:
                one = shared_refs[3]
                cp = pltpu.make_async_copy(kv.at[pl.ds(s * length, length)], one, load_sem.at[0])
                cp.start()
                cp.wait()
            else:
                one = kv.at[pl.ds(s * length, length)]
            keys, values = one[:, :HD], one[:, HD:]
            mine = jnp.concatenate([own_seg[:, s : s + 1]] * heads, axis=0)
            allowed = causal & (mine == key_seg[s : s + 1, :])
            scores = jnp.where(allowed, dot_t(q, keys) * scale, MASKED)
            probs = jnp.exp(scores - lse[s])
            grad_probs = dot_t(d_o, values)
            delta = jnp.sum(probs * grad_probs, axis=-1, keepdims=True)
            grad_scores = (probs * (grad_probs - delta)).astype(BF16)
            d_q = matmul(grad_scores, keys) * scale
            d_k = (t_dot(grad_scores, q) * scale).astype(BF16)
            d_v = t_dot(probs.astype(BF16), d_o).astype(BF16)
            both = jnp.concatenate([d_k, d_v], axis=1)
            if big:
                xkv[...] = both
                copies = [
                    pltpu.make_async_copy(
                        xkv.at[pl.ds(j * rows, rows)], kv_outs[0].at[s * n_seq + j], load_sem.at[j]
                    )
                    for j in range(n_seq)
                ]
                for cp in copies:
                    cp.start()
                for cp in copies:
                    cp.wait()
            else:
                xkv[s * n_seq : (s + 1) * n_seq] = both.reshape(n_seq, rows, 2 * HD)
            for h in range(heads):
                gq[r, h * HD : (h + 1) * HD] = rotate(
                    d_q[h * rows : (h + 1) * rows], cos[...], -sin[...]
                ).astype(BF16)
            get_o.run(3)
        if big:
            get_kv = Steps(sum_kv.steps(at, kv_outs[0], kv_outs[1:], op_scratch[8], shared_refs[:3]))
        else:
            get_kv = Steps(sum_kv.steps(at, xkv, kv_sum, op_scratch[8]))
        get_kv.run()
        for s in range(groups):
            xn[s] = dot_t(gq[s * rows : (s + 1) * rows, :], wq_r[...]).astype(BF16)
        get_n = Steps(sum_n.steps(at, xn, n_sum, op_scratch[9]))
        get_n.run()

        for j in range(n_seq):
            part = t_dot(norm_all[:, :, j * d_rows : (j + 1) * d_rows].reshape(tokens, d_rows), gq[...])
            xq[j, :d_rows, :] = part.astype(BF16)
            if j % 2:
                get_kv.run(2)
                get_n.run(1)
        low = matmul(flat(norm_all), qa[...]).astype(BF16)
        part = t_dot(low, gq[...]).astype(BF16)
        for j in range(n_seq):
            xq[j, d_rows:, :] = part[j * r_rows : (j + 1) * r_rows, :]
        get_kv.finish()
        get_q = Steps(sum_q.steps(at, xq, sq_out, op_scratch[6]))
        get_q.run()
        moves[2].run()
        get_n.finish()

        total_kv = kv_outs[1] if big else kv_sum
        gk = rotate(total_kv[:, :HD], cos[...], -sin[...]).astype(BF16)
        gv = total_kv[:, HD:].astype(BF16)
        gkv[:, :HD] = gk
        gkv[:, HD:] = gv
        get_kv2 = Steps(gather_kv.steps(at, [gkv], [gkv_all], op_scratch[1]))
        get_kv2.run()
        grad_normed = n_sum[...] + dot_t(gk, wk_r[...]) + dot_t(gv, wv_r[...])
        u_rows = unit[...]
        gain_attn_term = jnp.sum(grad_normed * u_rows, axis=0, keepdims=True)
        grad_unit = grad_normed * gain[...]
        inner = jnp.mean(grad_unit * u_rows, axis=-1, keepdims=True)
        grad_rows[...] = (gmid[...] + rms[...] * (grad_unit - u_rows * inner)).astype(BF16)
        get_kv2.finish()
        mine = pl.ds(pl.multiple_of(dp * share_d, share_d), share_d)
        part_rows = norm_all[:, :, mine].reshape(tokens, share_d)
        low_k = matmul(flat(norm_all), ka[...]).astype(BF16)
        low_v = matmul(flat(norm_all), va[...]).astype(BF16)
        g_rows = flat(gkv_all)
        part = t_dot(part_rows, g_rows).astype(BF16)
        low = jnp.concatenate(
            [t_dot(low_k, g_rows[:, :HD]), t_dot(low_v, g_rows[:, HD:])], axis=1
        )
        zero_r = jnp.zeros((kv_pad - kv_r, 2 * HD), F32)
        terms = jnp.concatenate([gain_attn_term, gain_term[...], jnp.zeros((14, width), F32)], axis=0)
        zero_c = jnp.zeros((16, 2 * HD - d_rows), F32)
        for j in range(n_seq):
            xk[j, :kv_d, :] = part[j * kv_d : (j + 1) * kv_d, :]
            xk[j, kv_d : kv_d + kv_pad, :] = jnp.concatenate(
                [low[j * kv_r : (j + 1) * kv_r, :], zero_r], axis=0
            ).astype(BF16)
            xk[j, kv_d + kv_pad :, :] = jnp.concatenate(
                [terms[:, j * d_rows : (j + 1) * d_rows], zero_c], axis=1
            ).astype(BF16)
        get_k = Steps(sum_k.steps(at, xk, sk_out, op_scratch[7]))
        get_k.run()
        get_o.finish()
        get_q.finish()
        get_k.finish()
        for move in moves:
            move.finish()

    results = pl.pallas_call(
        kernel,
        name="attention_back",
        out_shape=out_shape,
        in_specs=in_specs,
        out_specs=out_specs,
        scratch_shapes=scratch,
        compiler_params=pltpu.CompilerParams(
            collective_id=collective_id, has_side_effects=True, vmem_limit_bytes=60 << 20
        ),
    )(*inputs)
    return results[:7]


def unfold(d_rows, dg, du, dd, gate_expand, up_expand, down_adapt):
    quad, total, units = dg.shape
    rank = gate_expand.shape[0]
    r_rows = total - d_rows

    def kernel(dg_ref, du_ref, dd_ref, ge_ref, ue_ref, da_ref, wg, eg, wu, eu, wd, ad, ga, ua, de):
        first = pl.program_id(0) == 0
        for src, w, e in ((dg_ref, wg, eg), (du_ref, wu, eu)):
            w[...] = src[0, :d_rows, :].astype(F32)
            e[...] = src[0, d_rows:, :].astype(F32)
        both = dd_ref[0].astype(F32).T
        wd[...] = both[:, :d_rows]
        ad[...] = both[:, d_rows:]
        for out, term in (
            (ga, dot_t(dg_ref[0, :d_rows, :], ge_ref[...])),
            (ua, dot_t(du_ref[0, :d_rows, :], ue_ref[...])),
            (de, matmul(dd_ref[0, :d_rows, :], da_ref[...])),
        ):
            out[...] = jnp.where(first, term, term + out[...])

    cols = lambda n: pl.BlockSpec((n, units), lambda q: (0, q))
    side = lambda n: pl.BlockSpec((units, n), lambda q: (q, 0))
    block = pl.BlockSpec((1, total, units), lambda q: (q, 0, 0))
    kept = pl.BlockSpec((d_rows, rank), lambda q: (0, 0))
    shape = lambda *s: jax.ShapeDtypeStruct(s, F32)
    all_units = quad * units
    return pl.pallas_call(
        kernel,
        name="unfold",
        grid=(quad,),
        in_specs=[block, block, block, cols(rank), cols(rank), side(rank)],
        out_specs=[cols(d_rows), cols(r_rows), cols(d_rows), cols(r_rows), side(d_rows), side(r_rows)] + [kept] * 3,
        out_shape=[
            shape(d_rows, all_units), shape(r_rows, all_units), shape(d_rows, all_units), shape(r_rows, all_units),
            shape(all_units, d_rows), shape(all_units, r_rows),
        ] + [shape(d_rows, rank)] * 3,
        compiler_params=pltpu.CompilerParams(vmem_limit_bytes=48 << 20),
    )(dg, du, dd, gate_expand, up_expand, down_adapt)


def local(
    topo,
    tokens, segment_ids, out_grad, gain_attn, gain_mlp, w_query, w_key, w_value, w_out, w_gate, w_up, w_down,
    query_adapt, query_expand, key_adapt, key_expand, value_adapt, value_expand, out_adapt, out_expand,
    gate_adapt, gate_expand, up_adapt, up_expand, down_adapt, down_expand,
):
    rows, width = tokens.shape[2], tokens.shape[3]
    groups, n_seq = topo.n_dp, topo.n_seq
    length = rows * n_seq
    heads_dev = w_query.shape[1] // HD
    head_cols = heads_dev * HD
    rank = query_adapt.shape[1]
    scale_qk = HD ** (-0.5)
    quad = topo.group_size("quad")
    units = w_gate.shape[1] // quad
    seq = lax.axis_index("seq")
    dp = lax.axis_index("dp")

    def merged(weight, adapt, expand):
        return (weight.astype(F32) + matmul(adapt, expand)).astype(BF16)

    wq = merged(w_query, query_adapt, query_expand)
    wk = merged(w_key, key_adapt, key_expand)
    wv = merged(w_value, value_adapt, value_expand)
    wo = merged(w_out, out_adapt, out_expand)
    token_rows = tokens[0, 0].astype(F32)
    grad_rows_in = out_grad[0, 0]
    normed, unit_attn, rms_attn = normalize(token_rows, gain_attn)
    normed_attn = normed.astype(BF16)
    positions = seq * rows + jnp.arange(rows, dtype=jnp.int32)
    cosine_table, sine_table = rotary(positions, HD)
    cosine_heads, sine_heads = cosine_table[:, None, :], sine_table[:, None, :]
    key_rot = rotate(matmul(normed_attn, wk), cosine_table, sine_table).astype(BF16)
    value_rows = matmul(normed_attn, wv).astype(BF16)
    key_value = jnp.concatenate([key_rot, value_rows], axis=1)
    seg_rows = jnp.zeros((16, rows), F32).at[0].set(segment_ids[0, 0].astype(F32))

    zyx, xzy = "lhbxc", "xlhbc"
    (normed_all,), (kv_all,), (seg_all,), (grad_half,) = communicate(
        topo, "gather_attention", 0,
        Gather(topo, "dp", normed_attn, [(0, rows, "xc")]),
        Gather(topo, "all", key_value, row_parts(rows, (zyx, xzy), (7, 4))),
        Gather(topo, "all", seg_rows, [(0, 16, zyx)]),
        Gather(topo, "half", grad_rows_in, row_parts(rows, ("xlbc", "lbxc", "bxlc"), (1, 1, 1))),
    )
    kv_all = kv_all.reshape(groups, length, 2 * HD)
    keys_all, values_all = kv_all[..., :HD], kv_all[..., HD:]
    segments = seg_all[:, 0, :].reshape(groups, length)
    own_segments = lax.dynamic_slice_in_dim(segments, seq * rows, rows, 1)
    key_positions = jnp.arange(length, dtype=jnp.int32)
    causal = (key_positions[None, :] <= positions[:, None])[None, :, :]
    allowed = (causal & (own_segments[:, :, None] == segments[:, None, :]))[:, None, :, :]

    queries = matmul(normed_all.reshape(groups * rows, width), wq)
    query_rot = rotate(queries.reshape(groups, rows, heads_dev, HD), cosine_heads, sine_heads).astype(BF16)
    scores = jnp.where(allowed, contract("sthd,sjd->shtj", query_rot, keys_all) * scale_qk, MASKED)
    row_top = jnp.max(scores, axis=-1, keepdims=True)
    log_total = row_top + jnp.log(jnp.sum(jnp.exp(scores - row_top), axis=-1, keepdims=True))
    prob_low = jnp.exp(scores - log_total).astype(BF16)
    heads_out = (
        contract("shtj,sjd->sthd", prob_low, values_all).reshape(groups * rows, head_cols).astype(BF16)
    )
    out_part = matmul(heads_out, wo).astype(BF16).reshape(groups, rows, width)
    (out_sum,), = communicate(
        topo, "sum_attention", 1, Scatter(topo, "dp", out_part, [(0, rows, "cx")])
    )
    middle = token_rows + out_sum
    normed, unit_mlp, rms_mlp = normalize(middle, gain_mlp)
    normed_mlp = normed.astype(BF16)
    down_sum, gn_sum, dg, du, dd = feed_forward(
        topo, 2, normed_mlp, grad_rows_in, grad_half,
        w_gate, w_up, w_down, gate_adapt, gate_expand, up_adapt, up_expand, down_adapt, down_expand,
    )
    result_rows = (middle + down_sum).astype(BF16)
    gain_mlp_term, grad_from_mlp = norm_backward(gn_sum, unit_mlp, rms_mlp, gain_mlp)
    grad_middle = grad_rows_in.astype(F32) + grad_from_mlp
    grad_branch_attn = grad_middle.astype(BF16)
    my_kv_ranks = lambda a: lax.dynamic_slice_in_dim(a, dp * (rank // groups), rank // groups, 1)
    grad_rows, so, sq, sk, dg, du, dd = attention_back(
        topo, 4, grad_branch_attn, grad_middle,
        query_rot.reshape(groups * rows, head_cols), heads_out, kv_all.reshape(groups * length, 2 * HD),
        log_total.reshape(groups, heads_dev * rows, 1), own_segments.T, segments,
        normed_all, unit_attn, rms_attn, gain_attn[None], gain_mlp_term[None], cosine_table, sine_table,
        wo, wq, wk, wv, query_adapt, out_expand, my_kv_ranks(key_adapt), my_kv_ranks(value_adapt), dg, du, dd,
    )
    d_rows, r_rows = width // n_seq, rank // n_seq
    per_dev_d, per_dev_r = d_rows // groups, r_rows // groups
    kv_pad = -(-per_dev_r // 16) * 16
    grad_wg, grad_ge, grad_wu, grad_ue, grad_wd, grad_da, part_ga, part_ua, part_de = unfold(
        d_rows, dg, du, dd, gate_expand, up_expand, down_adapt
    )
    grad_wq, grad_qe = sq[:d_rows], sq[d_rows:]
    grad_wo, grad_oa = so[:d_rows].T, so[d_rows:].T
    grad_wkv, grad_kve = sk[:per_dev_d], sk[per_dev_d : per_dev_d + per_dev_r]
    gains = jnp.pad(sk[per_dev_d + kv_pad : per_dev_d + kv_pad + 2, :d_rows], ((0, 6), (0, 0)))

    adapt = jnp.stack(
        [
            part_ga,
            part_ua,
            dot_t(grad_wq.astype(BF16), query_expand),
        ]
    )
    expand = jnp.stack(
        [
            part_de.T,
            matmul(so[:d_rows].astype(BF16), out_adapt).T,
        ]
    )
    adapt = adapt.reshape(3, groups, per_dev_d, rank).transpose(1, 0, 2, 3).reshape(groups, -1, rank)
    expand = expand.reshape(2, groups, rank // groups, d_rows).transpose(1, 0, 2, 3).reshape(groups, -1, d_rows)
    expand = jnp.pad(expand, ((0, 0), (0, 0), (0, rank - d_rows)))
    small_gains = jnp.pad(
        gains[:, :d_rows].reshape(8, groups, per_dev_d).transpose(1, 0, 2), ((0, 0), (0, 8), (0, rank - per_dev_d))
    )
    small = jnp.concatenate([adapt, small_gains, expand], axis=1).astype(BF16)
    n_adapt = 3 * per_dev_d
    (small_sum,), = communicate(
        topo, "sum_small", 8, Scatter(topo, "dp", small, [(0, small.shape[1], "cx")])
    )
    per_seq = rank // groups // n_seq
    across = small_sum[n_adapt + 16 :, :d_rows].reshape(2, n_seq, per_seq, d_rows).transpose(1, 0, 2, 3)
    across = across.reshape(n_seq, 2 * per_seq, d_rows)
    (own_adapt, own_expand), = communicate(
        topo, "finish", 9, Finish(topo, small_sum[: n_adapt + 16], across)
    )
    grad_ga, grad_ua, grad_qa = own_adapt[:n_adapt].reshape(3, per_dev_d, rank)
    grad_gain_attn = own_adapt[n_adapt, :per_dev_d]
    grad_gain_mlp = own_adapt[n_adapt + 1, :per_dev_d]
    own_expand = own_expand.reshape(n_seq, 2, per_seq, d_rows).transpose(1, 2, 0, 3).reshape(2, per_seq, width)
    grad_de, grad_oe = own_expand[0], own_expand[1]
    grad_wk, grad_wv = grad_wkv[:, :HD], grad_wkv[:, HD:]
    grad_ka = dot_t(grad_wk.astype(BF16), key_expand)
    grad_va = dot_t(grad_wv.astype(BF16), value_expand)
    grad_ke, grad_ve = grad_kve[:, :HD], grad_kve[:, HD:]
    return (
        result_rows[None, None], grad_rows[None, None],
        grad_gain_attn, grad_gain_mlp,
        grad_wq, grad_wk, grad_wv, grad_wo, grad_wg, grad_wu, grad_wd,
        grad_qa, grad_qe, grad_ka, grad_ke, grad_va, grad_ve, grad_oa, grad_oe,
        grad_ga, grad_ge, grad_ua, grad_ue, grad_da, grad_de,
    )


def solution(mesh):
    topo = Topo(mesh.shape["dp"], mesh.shape["seq"])
    both = ("dp", "seq")
    in_specs = (
        P(None, "dp", "seq", None), P(None, "dp", "seq"), P(None, "dp", "seq", None),
        P(), P(), P(None, "dp"), P(), P(), P("dp", None), P(None, "dp"), P(None, "dp"), P("dp", None),
        P(), P(None, "dp"), P(), P(), P(), P(), P("dp", None), P(),
        P(), P(None, "dp"), P(), P(None, "dp"), P("dp", None), P(),
    )
    out_specs = (
        P(None, "dp", "seq", None), P(None, "dp", "seq", None), P(both), P(both),
        P("seq", "dp"), P(both, None), P(both, None), P("dp", "seq"), P("seq", "dp"), P("seq", "dp"), P("dp", "seq"),
        P(both, None), P("seq", "dp"), P(both, None), P(both, None), P(both, None), P(both, None),
        P("dp", "seq"), P(both, None), P(both, None), P("seq", "dp"), P(both, None), P("seq", "dp"),
        P("dp", "seq"), P(both, None),
    )
    return jax.shard_map(
        lambda *args: local(topo, *args), mesh=mesh, in_specs=in_specs, out_specs=out_specs, check_vma=False
    )
```

```python
import itertools
import math

import jax
import jax.numpy as jnp
from jax import lax
from jax.experimental import pallas as pl
from jax.experimental.pallas import tpu as pltpu
from jax.sharding import PartitionSpec as P

HD = 256
EPSILON = 1e-06
ROTARY_BASE = 10000.0
MASKED = -1e30

MESH = pl.DeviceIdType.MESH
BF16 = jnp.bfloat16
F32 = jnp.float32


class Topo:
    def __init__(self, n_dp, n_seq):
        self.n_dp, self.n_seq = n_dp, n_seq
        self.size = {"c": 2, "x": n_dp // 2, "b": n_seq // 4, "l": 2, "h": 2}

    def here(self):
        dp, seq = lax.axis_index("dp"), lax.axis_index("seq")
        nb = self.size["b"]
        outer = lax.div(seq, nb)
        return {
            "c": lax.rem(dp, 2),
            "x": lax.div(dp, 2),
            "b": lax.rem(seq, nb),
            "l": lax.rem(outer, 2),
            "h": lax.div(outer, 2),
        }

    def moved(self, at, dims, offsets, sign=1):
        new = dict(at)
        for dim, offset in zip(dims, offsets):
            n = self.size[dim]
            if not (isinstance(offset, int) and offset == 0):
                new[dim] = lax.rem(at[dim] + (offset if sign > 0 else n - offset), n)
        return new

    def seq_of(self, at):
        return (at["h"] * 2 + at["l"]) * self.size["b"] + at["b"]

    def device(self, at):
        return (at["x"] * 2 + at["c"], self.seq_of(at))

    def index(self, at, group):
        dp, seq = self.device(at)
        if group == "all":
            return dp * self.n_seq + seq
        if group == "half":
            nb = self.size["b"]
            return dp * (2 * nb) + at["l"] * nb + at["b"]
        if group == "dp":
            return dp
        if group == "seq":
            return seq
        if group == "quad":
            return at["l"] * self.size["b"] + at["b"]
        raise ValueError(group)

    def group_size(self, group):
        nb = self.size["b"]
        return {
            "all": self.n_dp * self.n_seq,
            "half": self.n_dp * 2 * nb,
            "dp": self.n_dp,
            "seq": self.n_seq,
            "quad": 2 * nb,
        }[group]


GROUP_DIMS = {"all": "cxblh", "half": "cxbl", "dp": "cx", "seq": "blh", "quad": "bl"}


def remote(src, dst, send_sem, recv_sem, device):
    return pltpu.make_async_remote_copy(
        src_ref=src,
        dst_ref=dst,
        send_sem=send_sem,
        recv_sem=recv_sem,
        device_id=device,
        device_id_type=MESH,
    )


def peers_of(topo, group):
    return {((dim, d),) for dim in GROUP_DIMS[group] for d in range(1, topo.size[dim])}


def digits(key, sizes):
    k = 0
    for o, s in zip(key, sizes):
        k = k * s + o
    return k


def arrived(topo, at, ref, send_sem, recv_sem):
    remote(ref, ref, send_sem, recv_sem, topo.device(at)).wait_recv()


class Gather:
    def __init__(self, topo, group, x, parts, beyond=None, need=None, keep=True):
        self.topo, self.group, self.parts, self.beyond = topo, group, parts, beyond
        self.keep = keep and not beyond
        self.slots = "half" if beyond else group
        self.need = need or (lambda dims, key: 0)
        self.inputs = [x]
        rows, cols = x.shape
        n = topo.group_size(group)
        self.outputs = [jax.ShapeDtypeStruct((topo.group_size(self.slots), rows, cols), x.dtype)]
        self.in_specs = [pl.BlockSpec(memory_space=pltpu.VMEM)]
        self.out_specs = [pl.BlockSpec(memory_space=pl.ANY)]
        self.scratch = [
            pltpu.SemaphoreType.DMA((len(parts), n)),
            pltpu.SemaphoreType.DMA((len(parts), n)),
            pltpu.SemaphoreType.DMA(()),
        ]

    def peers(self):
        return peers_of(self.topo, self.group)

    def keeps(self, order, key):
        return not self.beyond or key[order.index(self.beyond)] != 0

    def work(self):
        work = []
        for part, (row, rows, order) in enumerate(self.parts):
            for key in itertools.product(*[range(self.topo.size[dim]) for dim in order]):
                if not any(key) or self.keeps(order, key):
                    hops = sum(1 for o in key if o)
                    last = max([i for i, o in enumerate(key) if o], default=-1)
                    work.append((hops, self.need(order, key), last, part, key))
        work.sort()
        return [(w[3], w[4]) for w in work]

    def steps(self, at, ins, outs, scratch):
        topo = self.topo
        (x_ref,), (out_ref,) = ins, outs
        send_sem, recv_sem, own_sem = scratch
        size_of = lambda order: [topo.size[dim] for dim in order]

        def copy(part, key, stage, d):
            row, rows, order = self.parts[part]
            slot = topo.index(topo.moved(at, order, key, -1), self.slots)
            new_key = tuple(d if i == stage else o for i, o in enumerate(key))
            place = out_ref.at[slot, pl.ds(row, rows)]
            k = digits(new_key, size_of(order))
            target = topo.device(topo.moved(at, [order[stage]], [d]))
            source = place if any(key) else x_ref.at[pl.ds(row, rows)]
            return remote(source, place, send_sem.at[part, k], recv_sem.at[part, k], target)

        def own():
            return pltpu.make_async_copy(x_ref, out_ref.at[topo.index(at, self.slots)], own_sem)

        sent, steps = [], []
        for n, (part, key) in enumerate(self.work()):
            row, rows, order = self.parts[part]
            last = max([i for i, o in enumerate(key) if o], default=-1)
            sends = []
            for stage in range(last + 1, len(order)):
                for d in range(1, topo.size[order[stage]]):
                    new_key = tuple(d if i == stage else o for i, o in enumerate(key))
                    if self.keeps(order, new_key):
                        sends.append((self.need(order, new_key), stage, d))
            sends = [(part, key, stage, d) for _, stage, d in sorted(sends)]
            sent += sends

            def step(n=n, part=part, key=key, sends=sends):
                row, rows, order = self.parts[part]
                if n == 0 and self.keep:
                    own().start()
                if any(key):
                    slot = topo.index(topo.moved(at, order, key, -1), self.slots)
                    k = digits(key, size_of(order))
                    arrived(topo, at, out_ref.at[slot, pl.ds(row, rows)], send_sem.at[part, k], recv_sem.at[part, k])
                for send in sends:
                    copy(*send).start()

            steps.append(step)

        def end():
            for send in sent:
                copy(*send).wait_send()
            if self.keep:
                own().wait()

        return steps, [end]


TILE = 512


class Reduce:
    def __init__(self, topo, group, shape, dtype, parts):
        self.topo, self.group, self.parts, self.dtype = topo, group, parts, dtype
        n, rows, cols = shape
        assert n == topo.group_size(group), (n, group)
        self.tile = math.gcd(cols, TILE)

    def peers(self):
        return peers_of(self.topo, self.group)

    def stages(self, part):
        sizes = self.sizes(part)
        return [(max(s - 1, 1), math.prod(sizes[k + 1 :])) for k, s in enumerate(sizes)]

    def sizes(self, part):
        return [self.topo.size[dim] for dim in self.parts[part][2]]

    def jobs(self):
        jobs = []
        for part in range(len(self.parts)):
            sizes = self.sizes(part)
            keys = list(itertools.product(*[range(s) for s in sizes]))
            first = {k: min([i for i, o in enumerate(k) if o], default=len(sizes)) for k in keys}
            keys.sort(key=lambda k: (first[k], [0 if o else 1 for o in k]))
            jobs += [(first[key], rank, part, key) for rank, key in enumerate(keys)]
        jobs.sort()
        return [(first, part, key) for first, _, part, key in jobs]

    def block(self, at, part, key):
        return self.topo.index(self.topo.moved(at, self.parts[part][2], key), self.group)

    def target(self, at, part, key, stage):
        return self.topo.device(self.topo.moved(at, [self.parts[part][2][stage]], [key[stage]]))

    def place(self, part, key, stage):
        return key[stage] - 1, digits(key[stage + 1 :], self.sizes(part)[stage + 1 :])

    def terms(self, part, key, first):
        sizes = self.sizes(part)
        return [
            (stage, d - 1, digits(key[stage + 1 :], sizes[stage + 1 :]))
            for stage in range(first)
            for d in range(1, sizes[stage])
        ]


class VScatter(Reduce):
    def __init__(self, topo, group, shape, dtype, parts):
        super().__init__(topo, group, shape, dtype, parts)
        self.scratch = []
        for part, (row, nrows, order) in enumerate(parts):
            self.scratch.append(pltpu.VMEM((math.prod(self.sizes(part)[1:]), nrows, shape[2]), dtype))
            for m, rest in self.stages(part):
                self.scratch.append(pltpu.VMEM((m, rest, nrows, shape[2]), dtype))
                self.scratch.append(pltpu.SemaphoreType.DMA((m, rest)))
                self.scratch.append(pltpu.SemaphoreType.DMA((m, rest)))

    def steps(self, at, x_ref, out_ref, scratch):
        topo, tile = self.topo, self.tile
        scratch = list(scratch)
        bufs = []
        for part in range(len(self.parts)):
            acc = scratch.pop(0)
            bufs.append((acc, [tuple(scratch.pop(0) for _ in range(3)) for _ in self.sizes(part)]))
        jobs = self.jobs()

        def send(first, part, key):
            row, nrows, order = self.parts[part]
            acc, stages = bufs[part]
            buf, send_sem, recv_sem = stages[first]
            d, k = self.place(part, key, first)
            if first == 0:
                source = x_ref.at[self.block(at, part, key), pl.ds(row, nrows)]
            else:
                source = acc.at[digits(key[1:], self.sizes(part)[1:])]
            return remote(
                source, buf.at[d, k], send_sem.at[d, k], recv_sem.at[d, k], self.target(at, part, key, first)
            )

        def start():
            for job in jobs:
                if job[0] == 0:
                    send(*job).start()

        steps = [start]
        for job in jobs:
            if job[0] == 0:
                continue

            def step(job=job):
                first, part, key = job
                row, nrows, order = self.parts[part]
                acc, stages = bufs[part]
                terms = self.terms(part, key, first)
                for stage, d, k in terms:
                    buf, send_sem, recv_sem = stages[stage]
                    arrived(topo, at, buf.at[d, k], send_sem.at[d, k], recv_sem.at[d, k])
                block, kk = self.block(at, part, key), digits(key[1:], self.sizes(part)[1:])
                final = first == len(order)

                tiles = x_ref.shape[-1] // tile

                def add(n, _):
                    r0 = pl.multiple_of(lax.div(n, tiles) * 16, 16)
                    cols = pl.ds(pl.multiple_of(lax.rem(n, tiles) * tile, tile), tile)
                    r1 = pl.ds(pl.multiple_of(row + r0, 16), 16)
                    total = x_ref[block, r1, cols].astype(F32)
                    for stage, d, k in terms:
                        total = total + stages[stage][0][d, k, pl.ds(r0, 16), cols].astype(F32)
                    if final:
                        out_ref[r1, cols] = total.astype(out_ref.dtype)
                    else:
                        acc[kk, pl.ds(r0, 16), cols] = total.astype(acc.dtype)
                    return 0

                lax.fori_loop(0, nrows // 16 * tiles, add, 0)
                if not final:
                    send(*job).start()

            steps.append(step)

        def end():
            for job in jobs:
                if job[0] < len(self.parts[job[1]][2]):
                    send(*job).wait_send()

        return steps, [end]


class SlimScatter(Reduce):
    RING = 4

    def __init__(self, topo, group, shape, dtype, parts):
        super().__init__(topo, group, shape, dtype, parts)
        rows, cols = shape[1:]
        self.outputs = [jax.ShapeDtypeStruct((rows, cols), F32)]
        self.out_specs = [pl.BlockSpec(memory_space=pltpu.VMEM)]
        self.scratch = []
        self.most, self.cols = max(p[1] for p in parts), cols
        self.count = 1 + sum(topo.size[d] - 1 for d in GROUP_DIMS[group])
        for part, (row, nrows, order) in enumerate(parts):
            for m, rest in self.stages(part):
                self.outputs.append(jax.ShapeDtypeStruct((m, rest, nrows, cols), dtype))
                self.out_specs.append(pl.BlockSpec(memory_space=pl.ANY))
                self.scratch.append(pltpu.SemaphoreType.DMA((m, rest)))
                self.scratch.append(pltpu.SemaphoreType.DMA((m, rest)))

    def shared_scratch(self):
        return [
            pltpu.VMEM((2, self.count, self.most, self.cols), self.dtype),
            pltpu.SemaphoreType.DMA((2, self.count)),
            pltpu.VMEM((self.RING, self.most, self.cols), self.dtype),
        ]

    def steps(self, at, x_ref, outs, scratch, shared):
        topo, tile = self.topo, self.tile
        outs, scratch = list(outs), list(scratch)
        out_ref = outs.pop(0)
        stage_buf, stage_sem, ring = shared
        bufs = [
            [(outs.pop(0), scratch.pop(0), scratch.pop(0)) for _ in self.sizes(part)]
            for part in range(len(self.parts))
        ]
        jobs = self.jobs()
        later = [job for job in jobs if job[0] > 0]
        passed = [job for job in later if job[0] < len(self.parts[job[1]][2])]

        def own(part, key):
            row, nrows, order = self.parts[part]
            return x_ref.at[self.block(at, part, key), pl.ds(row, nrows)]

        def send(first, part, key, source=None):
            row, nrows, order = self.parts[part]
            buf, send_sem, recv_sem = bufs[part][first]
            d, k = self.place(part, key, first)
            if source is None:
                source = own(part, key) if first == 0 else ring.at[0, pl.ds(0, nrows)]
            return remote(
                source, buf.at[d, k], send_sem.at[d, k], recv_sem.at[d, k], self.target(at, part, key, first)
            )

        def loads(n):
            first, part, key = later[n]
            nrows = self.parts[part][1]
            sources = [own(part, key)] + [
                bufs[part][stage][0].at[d, k] for stage, d, k in self.terms(part, key, first)
            ]
            return [
                pltpu.make_async_copy(ref, stage_buf.at[n % 2, i, pl.ds(0, nrows)], stage_sem.at[n % 2, i])
                for i, ref in enumerate(sources)
            ]

        def fetch(n):
            first, part, key = later[n]
            for stage, d, k in self.terms(part, key, first):
                buf, send_sem, recv_sem = bufs[part][stage]
                arrived(topo, at, buf.at[d, k], send_sem.at[d, k], recv_sem.at[d, k])
            for cp in loads(n):
                cp.start()

        def start():
            for job in jobs:
                if job[0] == 0:
                    send(*job).start()

        steps = [start, lambda: fetch(0)]
        for n in range(len(later)):

            def step(n=n):
                first, part, key = later[n]
                row, nrows, order = self.parts[part]
                copies = loads(n)
                for cp in copies:
                    cp.wait()
                final = first == len(order)
                if not final:
                    sent = passed.index(later[n])
                    if sent >= self.RING:
                        send(*passed[sent - self.RING]).wait_send()

                tiles = self.cols // tile

                def add(n_tile, _):
                    r0 = pl.multiple_of(lax.div(n_tile, tiles) * 16, 16)
                    cols = pl.ds(pl.multiple_of(lax.rem(n_tile, tiles) * tile, tile), tile)
                    total = stage_buf[n % 2, 0, pl.ds(r0, 16), cols].astype(F32)
                    for i in range(1, len(copies)):
                        total = total + stage_buf[n % 2, i, pl.ds(r0, 16), cols].astype(F32)
                    if final:
                        out_ref[pl.ds(pl.multiple_of(row + r0, 16), 16), cols] = total
                    else:
                        ring[sent % self.RING, pl.ds(r0, 16), cols] = total.astype(ring.dtype)
                    return 0

                lax.fori_loop(0, nrows // 16 * tiles, add, 0)
                if not final:
                    send(first, part, key, ring.at[sent % self.RING, pl.ds(0, nrows)]).start()
                if n + 1 < len(later):
                    fetch(n + 1)

            steps.append(step)

        def end():
            for job in jobs:
                if job[0] == 0:
                    send(*job).wait_send()
            for job in passed[-self.RING :]:
                send(*job).wait_send()

        return steps, [end]


class Exchange:
    def __init__(self, topo, group, x, keep=True):
        self.topo, self.group, self.keep = topo, group, keep
        self.inputs = [x]
        n = x.shape[0]
        assert n == topo.group_size(group)
        self.outputs = [jax.ShapeDtypeStruct(x.shape, x.dtype)]
        self.in_specs = [pl.BlockSpec(memory_space=pl.ANY)]
        self.out_specs = [pl.BlockSpec(memory_space=pl.ANY)]
        self.scratch = [
            pltpu.SemaphoreType.DMA((n,)),
            pltpu.SemaphoreType.DMA((n,)),
            pltpu.SemaphoreType.DMA(()),
        ]

    def offsets(self):
        dims = GROUP_DIMS[self.group]
        return dims, [
            o for o in itertools.product(*[range(self.topo.size[d]) for d in dims]) if any(o)
        ]

    def peers(self):
        dims, offsets = self.offsets()
        return {tuple((dim, o) for dim, o in zip(dims, off) if o) for off in offsets}

    def steps(self, at, ins, outs, scratch):
        topo = self.topo
        (x_ref,), (out_ref,) = ins, outs
        send_sem, recv_sem, own_sem = scratch
        dims, offsets = self.offsets()
        me = topo.index(at, self.group)

        def own():
            return pltpu.make_async_copy(x_ref.at[me], out_ref.at[me], own_sem)

        def send(i):
            there = topo.moved(at, dims, offsets[i])
            source = x_ref.at[topo.index(there, self.group)]
            return remote(source, out_ref.at[me], send_sem.at[i], recv_sem.at[i], topo.device(there))

        def start():
            if self.keep:
                own().start()
            for i in range(len(offsets)):
                send(i).start()

        def wait(i):
            ref = out_ref.at[topo.index(topo.moved(at, dims, offsets[i], -1), self.group)]
            arrived(topo, at, ref, send_sem.at[i], recv_sem.at[i])

        def end():
            for i in range(len(offsets)):
                send(i).wait_send()
            if self.keep:
                own().wait()

        return [start] + [lambda i=i: wait(i) for i in range(len(offsets))], [end]


class Finish:
    def __init__(self, topo, x, y):
        self.topo = topo
        self.inputs = [x, y]
        self.outputs = [
            jax.ShapeDtypeStruct(x.shape, x.dtype),
            jax.ShapeDtypeStruct(y.shape, y.dtype),
        ]
        self.in_specs = [pl.BlockSpec(memory_space=pl.ANY)] * 2
        self.out_specs = [pl.BlockSpec(memory_space=pl.ANY)] * 2
        self.inner = Exchange(topo, "seq", y)
        self.scratch = self.inner.scratch + [pltpu.SemaphoreType.DMA(())] * 3

    def peers(self):
        return self.inner.peers()

    def route(self):
        topo = self.topo
        dp, seq = lax.axis_index("dp"), lax.axis_index("seq")
        n = seq * topo.n_dp + dp
        target = (lax.div(n, topo.n_seq), lax.rem(n, topo.n_seq))
        m = dp * topo.n_seq + seq
        source = (lax.rem(m, topo.n_dp), lax.div(m, topo.n_dp))
        stays = (target[0] == dp) & (target[1] == seq)
        return target, source, stays

    def greet(self, barrier):
        target, source, stays = self.route()

        @pl.when(jnp.logical_not(stays))
        def _():
            pl.semaphore_signal(barrier, inc=1, device_id=source, device_id_type=MESH)

        return jnp.where(stays, 0, 1)

    def steps(self, at, ins, outs, scratch):
        (x_ref, y_ref), (x_out, y_out) = ins, outs
        send_sem, recv_sem, own_sem = scratch[3:]
        target, source, stays = self.route()
        cp = remote(x_ref, x_out, send_sem, recv_sem, target)
        own = pltpu.make_async_copy(x_ref, x_out, own_sem)
        inner, ends = self.inner.steps(at, [y_ref], [y_out], scratch[:3])

        def start():
            pl.when(stays)(own.start)
            pl.when(jnp.logical_not(stays))(cp.start)

        def end():
            pl.when(stays)(own.wait)
            pl.when(jnp.logical_not(stays))(cp.wait)

        return [start] + inner, ends + [end]


def greet(topo, ops):
    at = topo.here()
    peers = sorted(set().union(*[op.peers() for op in ops]))
    barrier = pltpu.get_barrier_semaphore()
    for peer in peers:
        there = topo.device(topo.moved(at, [p[0] for p in peer], [p[1] for p in peer]))
        pl.semaphore_signal(barrier, inc=1, device_id=there, device_id_type=MESH)
    count = len(peers)
    for op in ops:
        if hasattr(op, "greet"):
            count = count + op.greet(barrier)
    pl.semaphore_wait(barrier, count)
    return at


class Steps:
    def __init__(self, steps):
        self.todo = steps[0] + steps[1]

    def run(self, count=1):
        for _ in range(count):
            if self.todo:
                self.todo.pop(0)()

    def finish(self):
        self.run(len(self.todo))


def run_slot(t, slots):
    def tree(low, high):
        if not any(slots[low:high]):
            return
        if high - low == 1:
            for step in slots[low]:
                step()
            return
        middle = (low + high) // 2
        left, right = any(slots[low:middle]), any(slots[middle:high])
        if left and right:
            lax.cond(t < middle, lambda: tree(low, middle), lambda: tree(middle, high))
        elif left:
            pl.when(t < middle)(lambda: tree(low, middle))
        else:
            pl.when(t >= middle)(lambda: tree(middle, high))

    tree(0, len(slots))


def communicate(topo, name, collective_id, *ops):
    n_in = [len(op.inputs) for op in ops]
    n_out = [len(op.outputs) for op in ops]
    n_scratch = [len(op.scratch) for op in ops]

    def kernel(*refs):
        refs = list(refs)
        take = lambda counts: [[refs.pop(0) for _ in range(k)] for k in counts]
        ins, outs, scratch = take(n_in), take(n_out), take(n_scratch)
        at = greet(topo, ops)
        running = [Steps(op.steps(at, i, o, s)) for op, i, o, s in zip(ops, ins, outs, scratch)]
        while any(r.todo for r in running):
            for r in running:
                r.run()

    results = pl.pallas_call(
        kernel,
        name=name,
        out_shape=[s for op in ops for s in op.outputs],
        in_specs=[s for op in ops for s in op.in_specs],
        out_specs=[s for op in ops for s in op.out_specs],
        scratch_shapes=[s for op in ops for s in op.scratch],
        compiler_params=pltpu.CompilerParams(
            collective_id=collective_id, has_side_effects=True, vmem_limit_bytes=58 << 20
        ),
    )(*[x for op in ops for x in op.inputs])
    results = list(results)
    return [[results.pop(0) for _ in range(k)] for k in n_out]


class Scatter(VScatter):
    def __init__(self, topo, group, x, parts):
        super().__init__(topo, group, x.shape, x.dtype, parts)
        self.inputs = [x]
        self.outputs = [jax.ShapeDtypeStruct(x.shape[1:], F32)]
        self.in_specs = [pl.BlockSpec(memory_space=pltpu.VMEM)]
        self.out_specs = [pl.BlockSpec(memory_space=pltpu.VMEM)]

    def steps(self, at, ins, outs, scratch):
        return super().steps(at, ins[0], outs[0], scratch)


def row_parts(rows, orders, weights, step=16):
    parts, row, total = [], 0, sum(weights)
    for i, (order, weight) in enumerate(zip(orders, weights)):
        n = rows - row if i == len(orders) - 1 else min(rows - row, int(round(rows * weight / total / step)) * step)
        if n:
            parts.append((row, n, order))
            row += n
    return parts


def matmul(left, right):
    return jnp.dot(left, right, preferred_element_type=jnp.float32)


def contract(form, left, right):
    return jnp.einsum(form, left, right, preferred_element_type=jnp.float32)


def rotary(positions, size):
    half_size = size // 2
    frequency = ROTARY_BASE ** (-(jnp.arange(half_size, dtype=jnp.float32) * 2.0) / size)
    angles = positions.astype(jnp.float32)[:, None] * frequency[None, :]
    return (jnp.cos(angles), jnp.sin(angles))


def rotate(values, cosine_table, sine_table):
    half_size = values.shape[-1] // 2
    first_half = values[..., :half_size]
    second_half = values[..., half_size:]
    return jnp.concatenate(
        [
            first_half * cosine_table - second_half * sine_table,
            second_half * cosine_table + first_half * sine_table,
        ],
        axis=-1,
    )


def normalize(values, gain_vector):
    inverse_rms = lax.rsqrt(jnp.mean(values * values, axis=-1, keepdims=True) + EPSILON)
    unit_rows = values * inverse_rms
    return (unit_rows * gain_vector, unit_rows, inverse_rms)


def norm_backward(grad_normed, unit_rows, inverse_rms, gain_vector):
    gain_term = jnp.sum(grad_normed * unit_rows, axis=0)
    grad_unit = grad_normed * gain_vector
    inner = jnp.mean(grad_unit * unit_rows, axis=-1, keepdims=True)
    return (gain_term, inverse_rms * (grad_unit - unit_rows * inner))


def dot_t(left, right):
    return lax.dot_general(left, right, (((1,), (1,)), ((), ())), preferred_element_type=F32)


def t_dot(left, right):
    return lax.dot_general(left, right, (((0,), (0,)), ((), ())), preferred_element_type=F32)


GELU_C = math.sqrt(2.0 / math.pi)


def gelu_parts(v):
    square = v * v
    t = jnp.tanh(GELU_C * (v + 0.044715 * v * square))
    half_up = 0.5 * (1.0 + t)
    slope = half_up + 0.5 * v * (1.0 - t * t) * (GELU_C * (1.0 + 3.0 * 0.044715 * square))
    return v * half_up, slope


def feed_forward(
    topo, collective_id, normed, grads, grads_half,
    w_gate, w_up, w_down, gate_adapt, gate_expand, up_adapt, up_expand, down_adapt, down_expand,
):
    rows, width = normed.shape
    quad = topo.group_size("quad")
    half = topo.group_size("half")
    units = w_gate.shape[1] // quad
    rank = gate_adapt.shape[1]
    ranks = rank // 2
    half_width = width // 2
    d_rows, r_rows = half_width // quad, ranks // quad
    per_chunk = 512 // rows
    tile = 512
    block = 256

    dims = "hxclb"
    keys = list(itertools.product(*[range(topo.size[d]) for d in dims]))
    chunks = [keys[i : i + per_chunk] for i in range(0, len(keys), per_chunk)]
    own = len(chunks) // 2
    chunk_of = {key: i for i, keys_of in enumerate(chunks) for key in keys_of}

    def need(order, key):
        at_dim = dict(zip(order, key))
        return chunk_of[tuple(at_dim.get(d, 0) for d in dims)]

    near = row_parts(rows, ("xlbc", "lbxc", "bxlc"), (1, 1, 1))
    both = jnp.concatenate([normed, grads], axis=0)
    far = row_parts(2 * rows, ("hxlbc", "hlbxc", "hbxlc"), (1, 1, 1))
    gather_n = Gather(topo, "half", normed, near, need=need, keep=False)
    gather_far = Gather(topo, "all", both, far, beyond="h", need=need)
    thirds = row_parts(2 * rows, ("cxlb", "cbxl", "clbx"), (1, 1, 1))
    sum_both = SlimScatter(topo, "half", (half, 2 * rows, width), BF16, thirds)
    comm = [gather_n, gather_far, sum_both]

    inputs = [
        normed, both, grads_half, w_gate, w_up, w_down,
        gate_adapt, gate_expand, up_adapt, up_expand, down_adapt, down_expand,
    ]
    part = jax.ShapeDtypeStruct((half, 2 * rows, width), BF16)
    grad = jax.ShapeDtypeStruct((quad, d_rows + r_rows, units), BF16)
    any_spec = pl.BlockSpec(memory_space=pl.ANY)
    out_shape = [part, grad, grad, grad]
    out_specs = [any_spec] * 4
    scratch = [
        pltpu.VMEM((width, units), BF16), pltpu.VMEM((width, units), BF16), pltpu.VMEM((units, width), BF16),
        pltpu.VMEM((width, rank), BF16), pltpu.VMEM((rank, units), BF16),
        pltpu.VMEM((width, rank), BF16), pltpu.VMEM((rank, units), BF16),
        pltpu.VMEM((units, rank), BF16), pltpu.VMEM((rank, width), BF16),
        pltpu.VMEM((half_width + ranks, units), F32),
        pltpu.VMEM((half_width + ranks, units), F32),
        pltpu.VMEM((half_width + ranks, units), F32),
        pltpu.VMEM((3, tile, units), BF16),
        pltpu.VMEM((3, tile, ranks), BF16),
        pltpu.VMEM((2, tile, width), BF16), pltpu.VMEM((2, tile, width), BF16),
        pltpu.VMEM((tile, width), BF16), pltpu.VMEM((tile, width), BF16),
        pltpu.SemaphoreType.DMA((9,)),
        pltpu.SemaphoreType.DMA((2, 2, per_chunk)),
        pltpu.SemaphoreType.DMA((2, per_chunk)),
        pltpu.SemaphoreType.DMA((3,)),
    ]
    n_own = len(scratch)
    shared = sum_both.shared_scratch()
    scratch = scratch + shared
    for op in comm:
        out_shape = out_shape + op.outputs
        out_specs = out_specs + op.out_specs
        scratch = scratch + op.scratch

    def kernel(*refs):
        refs = list(refs)
        (
            n_hbm, both_hbm, g_half, wg_hbm, wu_hbm, wd_hbm, ga_hbm, ge_hbm, ua_hbm, ue_hbm, da_hbm, de_hbm,
        ) = [refs.pop(0) for _ in inputs]
        part_hbm, dg_out, du_out, dd_out = [refs.pop(0) for _ in range(4)]
        op_outs = [[refs.pop(0) for _ in op.outputs] for op in comm]
        (
            wg, wu, wd, ga, ge, ua, ue, da, de, acc_g, acc_u, acc_d, acts, low_s, n_buf, g_buf, down_st, gn_st,
            w_sem, load_sem, store_sem, grad_sem,
        ) = [refs.pop(0) for _ in range(n_own)]
        shared_refs = [refs.pop(0) for _ in shared]
        op_scratch = [[refs.pop(0) for _ in op.scratch] for op in comm]
        mix_s, gg_s, gu_s = acts.at[0], acts.at[1], acts.at[2]
        at = topo.here()
        high = at["h"]
        member = topo.index(at, "quad")
        unit_at = pl.multiple_of(member * units, units)

        w_copies = [
            pltpu.make_async_copy(src, dst, w_sem.at[i])
            for i, (src, dst) in enumerate(
                (
                    (de_hbm, de),
                    (da_hbm.at[pl.ds(unit_at, units), :], da),
                    (wd_hbm.at[pl.ds(unit_at, units), :], wd),
                    (ga_hbm, ga),
                    (ge_hbm.at[:, pl.ds(unit_at, units)], ge),
                    (wg_hbm.at[:, pl.ds(unit_at, units)], wg),
                    (ua_hbm, ua),
                    (ue_hbm.at[:, pl.ds(unit_at, units)], ue),
                    (wu_hbm.at[:, pl.ds(unit_at, units)], wu),
                )
            )
        ]
        for cp in w_copies:
            cp.start()

        greet(topo, comm)
        gathers = (gather_n, gather_far)
        all_steps = [op.steps(at, [x], o, sc) for op, x, o, sc in zip(gathers, (n_hbm, both_hbm), op_outs, op_scratch)]
        ranked = []
        for g, (op, (steps_g, _)) in enumerate(zip(gathers, all_steps)):
            for i, (f, (p, k)) in enumerate(zip(steps_g, op.work())):
                when = NEAR_US * i / len(steps_g) - 20.0 if g == 0 else FAR_AT + i * FAR_US
                ranked.append((when if any(k) or g else -1e3, g, i, f, need(op.parts[p][2], k)))
        ranked.sort(key=lambda w: w[:3])
        steps = [(f, chunk) for _, _, _, f, chunk in ranked]
        when_of = [w[0] for w in ranked]
        started = len(gather_n.parts)
        for f, _ in steps[:started]:
            f()

        def upto(chunk, done):
            last = [i for i, (_, c) in enumerate(steps) if c <= chunk and i >= started]
            return max([done] + [i + 1 for i in last])

        acc_g[...] = jnp.zeros_like(acc_g)
        acc_u[...] = jnp.zeros_like(acc_u)
        acc_d[...] = jnp.zeros_like(acc_d)

        def merge_rows(weight, adapt, expand, total):
            def one(i, _):
                r = pl.ds(pl.multiple_of(i * block, block), block)
                weight[r, :] = (weight[r, :].astype(F32) + matmul(adapt[r, :], expand[...])).astype(BF16)
                return 0

            lax.fori_loop(0, total // block, one, 0)

        for cp in w_copies[:3]:
            cp.wait()
        merge_rows(wd, da, de, units)
        for cp in w_copies[3:6]:
            cp.wait()
        merge_rows(wg, ga, ge, width)
        for cp in w_copies[6:]:
            cp.wait()
        merge_rows(wu, ua, ue, width)

        def key_of(c, i):
            k = c * per_chunk + i
            key = []
            for d in reversed(dims):
                key.append(lax.rem(k, topo.size[d]))
                k = lax.div(k, topo.size[d])
            return key[::-1]

        def chunk_copies(c, slot, other):
            copies = []
            for i in range(per_chunk):
                origin = topo.moved(at, dims, key_of(c, i), -1)
                r = pl.ds(i * rows, rows)
                in_half = topo.index(origin, "half")
                if other:
                    n_src = op_outs[1][0].at[in_half, pl.ds(0, rows)]
                    g_src = op_outs[1][0].at[in_half, pl.ds(rows, rows)]
                else:
                    n_src, g_src = op_outs[0][0].at[in_half], g_half.at[in_half]
                copies.append(pltpu.make_async_copy(n_src, n_buf.at[slot, r], load_sem.at[slot, 0, i]))
                copies.append(pltpu.make_async_copy(g_src, g_buf.at[slot, r], load_sem.at[slot, 1, i]))
            return copies

        def first_copies():
            copies = chunk_copies(0, 0, False)
            r = pl.ds(0, rows)
            copies[0] = pltpu.make_async_copy(n_hbm, n_buf.at[0, r], load_sem.at[0, 0, 0])
            return copies

        def store_copies(c):
            copies = []
            for i in range(per_chunk):
                slot = topo.index(topo.moved(at, dims, key_of(c, i), -1), "half")
                r = pl.ds(i * rows, rows)
                for k, source in enumerate((gn_st, down_st)):
                    place = part_hbm.at[slot, pl.ds(k * rows, rows)]
                    copies.append(pltpu.make_async_copy(source.at[r], place, store_sem.at[k, i]))
            return copies

        n_one, n_two, n_three = units // block, width // block, half_width // block
        scale = units / 1024
        kinds = {
            False: [("one", n_one, 1.9), ("two", n_two, 1.0 * scale), ("pre", 1, 2.0 * scale), ("three", n_three, 0.7 * scale)],
            True: [("one", n_one, 1.9), ("pre", 1, 2.0 * scale), ("three", n_three, 0.7 * scale)],
        }
        slots = {(other, kind): [[] for _ in range(own * n)] for other in (False, True) for kind, n, _ in kinds[other]}
        done = upto(0, started)
        for f, _ in steps[started:done]:
            f()
        clock = 0.0
        for c in range(len(chunks)):
            other = c >= own
            for kind, n, cost in kinds[other]:
                for i in range(n):
                    clock += cost
                    target = max(done, sum(1 for w in when_of if w <= clock))
                    if kind == "pre" and c + 1 < len(chunks):
                        target = upto(c + 1, target)
                    slots[other, kind][(c - own if other else c) * n + i] += [f for f, _ in steps[done:target]]
                    done = target
        sums, sums_end = sum_both.steps(at, part_hbm, op_outs[2], op_scratch[2], shared_refs)
        clock, summed = 0.0, 0
        for c in range(own):
            for kind, n, cost in kinds[True]:
                for i in range(n):
                    clock += cost
                    target = min(len(sums), 1 + int(max(clock - 3.0, 0.0) / SUM_US))
                    if kind != "pre":
                        slots[True, kind][c * n + i] += sums[summed:target]
                        summed = target

        for cp in first_copies():
            cp.start()
        low_cols = pl.ds(pl.multiple_of(high * ranks, ranks), ranks)
        half_at = high * half_width

        def chunk_loop(other):
            first = own if other else 0

            def body(k, _):
                c = first + k
                slot = lax.rem(c, 2)
                nb, gb = n_buf.at[slot], g_buf.at[slot]
                for cp in chunk_copies(c, slot, other):
                    cp.wait()
                low_s[0] = matmul(nb[...], ga[:, low_cols]).astype(BF16)
                low_s[1] = matmul(nb[...], ua[:, low_cols]).astype(BF16)
                low_s[2] = dot_t(gb[...], de[low_cols, :]).astype(BF16)

                def one(i, _):
                    cols = pl.ds(pl.multiple_of(i * block, block), block)
                    gate = matmul(nb[...], wg[:, cols])
                    up = matmul(nb[...], wu[:, cols])
                    act, slope = gelu_parts(gate)
                    gm = dot_t(gb[...], wd[cols, :])
                    mix_s[:, cols] = (act * up).astype(BF16)
                    gg_s[:, cols] = (gm * up * slope).astype(BF16)
                    gu_s[:, cols] = (gm * act).astype(BF16)
                    run_slot(k * n_one + i, slots[other, "one"])
                    return 0

                lax.fori_loop(0, n_one, one, 0)
                if not other:

                    @pl.when(c > 0)
                    def _():
                        for cp in store_copies(c - 1):
                            cp.wait()

                    def two(i, _):
                        cols = pl.ds(pl.multiple_of(i * block, block), block)
                        down_st[:, cols] = matmul(mix_s[...], wd[:, cols]).astype(BF16)
                        gn_st[:, cols] = (dot_t(gg_s[...], wg[cols, :]) + dot_t(gu_s[...], wu[cols, :])).astype(BF16)
                        run_slot(k * n_two + i, slots[other, "two"])
                        return 0

                    lax.fori_loop(0, n_two, two, 0)
                    for cp in store_copies(c):
                        cp.start()
                for i, (acc, grads_s) in enumerate(((acc_g, gg_s), (acc_u, gu_s), (acc_d, mix_s))):
                    acc[half_width:, :] += t_dot(low_s[i], grads_s[...])
                run_slot(k, slots[other, "pre"])
                if other:

                    @pl.when(c + 1 < len(chunks))
                    def _():
                        for cp in chunk_copies(c + 1, 1 - slot, True):
                            cp.start()

                else:

                    @pl.when(c + 1 < own)
                    def _():
                        for cp in chunk_copies(c + 1, 1 - slot, False):
                            cp.start()

                    @pl.when(c + 1 == own)
                    def _():
                        for cp in chunk_copies(c + 1, 1 - slot, True):
                            cp.start()

                def three(i, _):
                    r = pl.ds(pl.multiple_of(i * block, block), block)
                    cols = pl.ds(pl.multiple_of(half_at + i * block, block), block)
                    acc_g[r, :] += t_dot(nb[:, cols], gg_s[...])
                    acc_u[r, :] += t_dot(nb[:, cols], gu_s[...])
                    acc_d[r, :] += t_dot(gb[:, cols], mix_s[...])
                    run_slot(k * n_three + i, slots[other, "three"])
                    return 0

                lax.fori_loop(0, n_three, three, 0)
                return 0

            lax.fori_loop(0, own, body, 0)

        chunk_loop(False)
        for cp in store_copies(own - 1):
            cp.wait()
        chunk_loop(True)

        pending = []
        for q in range(quad):
            for k, (acc, out) in enumerate(((acc_g, dg_out), (acc_u, du_out), (acc_d, dd_out))):
                if len(pending) >= 3:
                    pending.pop(0).wait()
                acts[k, :d_rows, :] = acc[q * d_rows : (q + 1) * d_rows, :].astype(BF16)
                acts[k, d_rows : d_rows + r_rows, :] = acc[
                    half_width + q * r_rows : half_width + (q + 1) * r_rows, :
                ].astype(BF16)
                cp = pltpu.make_async_copy(acts.at[k, pl.ds(0, d_rows + r_rows)], out.at[q], grad_sem.at[k])
                cp.start()
                pending.append(cp)
        for f in steps[done:]:
            f[0]()
        for f in sums[summed:]:
            f()
        for cp in pending:
            cp.wait()
        for f in [f for _, end in all_steps for f in end] + sums_end:
            f()

    flops = 2 * rows * topo.n_dp * topo.n_seq * units * width * 9
    results = pl.pallas_call(
        kernel,
        name="feed_forward",
        out_shape=out_shape,
        in_specs=[any_spec] * len(inputs),
        out_specs=out_specs,
        scratch_shapes=scratch,
        compiler_params=pltpu.CompilerParams(
            collective_id=collective_id, has_side_effects=True, vmem_limit_bytes=60 << 20
        ),
        cost_estimate=pl.CostEstimate(flops=flops, bytes_accessed=1 << 27, transcendentals=0),
    )(*inputs)
    dg, du, dd = results[1:4]
    total = results[4 + len(gather_n.outputs) + len(gather_far.outputs)]
    return total[rows:], total[:rows], dg, du, dd


KV_STEPS = 3
NEAR_US = 45.0
FAR_AT = 5.0
FAR_US = 1.4
SUM_US = 2.4


def attention_back(
    topo, collective_id, grad_branch, grad_middle, query_rot, heads_out, key_value, log_total, own_segs, key_segs,
    normed_all, unit_attn, rms_attn, gain_attn, gain_mlp_term, cosine, sine, wo, wq, wk, wv,
    query_adapt, out_expand, key_adapt, value_adapt, dg, du, dd,
):
    groups, rows, width = normed_all.shape
    n_seq = topo.n_seq
    length = rows * n_seq
    head_cols = heads_out.shape[1]
    heads = head_cols // HD
    tokens = groups * rows
    rank = query_adapt.shape[1]
    scale = HD ** (-0.5)
    d_rows, r_rows = width // n_seq, rank // n_seq
    share_d, share_r = width // groups, rank // groups
    kv_d, kv_r = d_rows // groups, r_rows // groups
    kv_pad = -(-kv_r // 16) * 16
    kv_rows = kv_d + kv_pad + 16

    gather_g = Gather(topo, "dp", grad_branch, [(0, rows, "xc")])
    gather_kv = Gather(topo, "dp", jax.ShapeDtypeStruct((rows, 2 * HD), BF16), [(0, rows, "xc")])
    swaps = [Exchange(topo, "quad", a, keep=False) for a in (dg, du, dd)]
    seq_parts = lambda n: row_parts(n, ("blh", "lbh"), (2, 1))
    w_shape = (n_seq, d_rows + r_rows, head_cols)
    sum_o = VScatter(topo, "seq", w_shape, BF16, seq_parts(d_rows + r_rows))
    sum_q = VScatter(topo, "seq", w_shape, BF16, seq_parts(d_rows + r_rows))
    sum_k = VScatter(topo, "seq", (n_seq, kv_rows, 2 * HD), BF16, seq_parts(kv_rows))
    kv_shape = (groups * n_seq, rows, 2 * HD)
    sum_kv = VScatter(topo, "all", kv_shape, BF16, row_parts(rows, ("cxblh", "cblxh"), (1, 1)))
    sum_n = VScatter(topo, "dp", (groups, rows, width), BF16, [(0, rows, "cx")])

    inputs = [
        grad_branch, grad_middle, query_rot, heads_out, key_value, log_total, own_segs, key_segs,
        normed_all, unit_attn, rms_attn, gain_attn, gain_mlp_term, cosine, sine, wo, wq, wk, wv,
        query_adapt, out_expand, key_adapt, value_adapt, dg, du, dd,
    ]
    vmem, anywhere = pl.BlockSpec(memory_space=pltpu.VMEM), pl.BlockSpec(memory_space=pl.ANY)
    big = groups * n_seq > 32
    in_specs = [anywhere] + [vmem] * (len(inputs) - 4) + [anywhere] * 3
    if big:
        in_specs[4] = anywhere
    out_shape = [
        jax.ShapeDtypeStruct((rows, width), BF16),
        jax.ShapeDtypeStruct((d_rows + r_rows, head_cols), F32),
        jax.ShapeDtypeStruct((d_rows + r_rows, head_cols), F32),
        jax.ShapeDtypeStruct((kv_rows, 2 * HD), F32),
    ] + [op.outputs[0] for op in swaps]
    out_specs = [vmem] * 4 + [anywhere] * 3
    if big:
        sum_kv = SlimScatter(topo, "all", kv_shape, BF16, row_parts(rows, ("cxblh", "cblxh"), (1, 1)))
        out_shape = out_shape + [jax.ShapeDtypeStruct(kv_shape, BF16)] + sum_kv.outputs
        out_specs = out_specs + [anywhere] + sum_kv.out_specs
    scratch = [
        pltpu.VMEM((groups, rows, width), BF16),
        pltpu.VMEM((tokens, head_cols), BF16),
        pltpu.VMEM((tokens, head_cols), BF16),
        pltpu.VMEM(w_shape, BF16),
        pltpu.VMEM(w_shape, BF16),
        pltpu.VMEM((n_seq, kv_rows, 2 * HD), BF16),
        pltpu.VMEM((length, 2 * HD) if big else kv_shape, BF16),
        pltpu.VMEM((groups, rows, width), BF16),
        pltpu.VMEM((rows, 2 * HD), F32),
        pltpu.VMEM((rows, width), F32),
        pltpu.VMEM((rows, 2 * HD), BF16),
        pltpu.VMEM((groups, rows, 2 * HD), BF16),
        pltpu.SemaphoreType.DMA((n_seq,)),
    ]
    n_own = len(scratch)
    shared = sum_kv.shared_scratch() + [pltpu.VMEM((length, 2 * HD), BF16)] if big else []
    scratch = scratch + shared
    ops = [gather_g, gather_kv] + swaps + [sum_o, sum_q, sum_k, sum_kv, sum_n]
    for op in ops:
        scratch = scratch + op.scratch

    def kernel(*refs):
        refs = list(refs)
        (
            gb_hbm, gmid, qrot, hout, kv, lse, own_seg, key_seg, norm_all, unit, rms, gain, gain_term, cos, sin,
            wo_r, wq_r, wk_r, wv_r, qa, oe, ka, va, dg_r, du_r, dd_r,
        ) = [refs.pop(0) for _ in inputs]
        grad_rows, so_out, sq_out, sk_out, dg_o, du_o, dd_o = [refs.pop(0) for _ in range(7)]
        kv_outs = [refs.pop(0) for _ in out_shape[7:]]
        (
            ga, gh, gq, xo, xq, xk, xkv, xn, kv_sum, n_sum, gkv, gkv_all, load_sem,
        ) = [refs.pop(0) for _ in range(n_own)]
        shared_refs = [refs.pop(0) for _ in shared]
        op_scratch = [[refs.pop(0) for _ in op.scratch] for op in ops]
        dp = lax.axis_index("dp")
        at = greet(topo, ops)
        get_g = Steps(gather_g.steps(at, [gb_hbm], [ga], op_scratch[0]))
        get_g.run()
        moves = [
            Steps(op.steps(at, [r], [o], sc))
            for op, r, o, sc in zip(swaps, (dg_r, du_r, dd_r), (dg_o, du_o, dd_o), op_scratch[2:5])
        ]
        moves[0].run()
        get_g.finish()
        flat = lambda ref: ref[...].reshape(tokens, ref.shape[-1])

        gh[...] = dot_t(flat(ga), wo_r[...]).astype(BF16)

        for j in range(n_seq):
            part = t_dot(ga[:, :, j * d_rows : (j + 1) * d_rows].reshape(tokens, d_rows), hout[...])
            xo[j, :d_rows, :] = part.astype(BF16)
        low = dot_t(flat(ga), oe[...]).astype(BF16)
        part = t_dot(low, hout[...]).astype(BF16)
        for j in range(n_seq):
            xo[j, d_rows:, :] = part[j * r_rows : (j + 1) * r_rows, :]
        get_o = Steps(sum_o.steps(at, xo, so_out, op_scratch[5]))
        get_o.run()

        seq = lax.axis_index("seq")
        key_at = lax.broadcasted_iota(jnp.int32, (heads * rows, length), 1)
        row_at = lax.broadcasted_iota(jnp.int32, (heads * rows, length), 0)
        causal = key_at <= seq * rows + lax.rem(row_at, rows)
        for s in range(groups):
            r = slice(s * rows, (s + 1) * rows)
            stack = lambda ref: jnp.concatenate([ref[r, h * HD : (h + 1) * HD] for h in range(heads)], axis=0)
            q, d_o = stack(qrot), stack(gh)
            if big:
                one = shared_refs[3]
                cp = pltpu.make_async_copy(kv.at[pl.ds(s * length, length)], one, load_sem.at[0])
                cp.start()
                cp.wait()
            else:
                one = kv.at[pl.ds(s * length, length)]
            keys, values = one[:, :HD], one[:, HD:]
            mine = jnp.concatenate([own_seg[:, s : s + 1]] * heads, axis=0)
            allowed = causal & (mine == key_seg[s : s + 1, :])
            scores = jnp.where(allowed, dot_t(q, keys) * scale, MASKED)
            probs = jnp.exp(scores - lse[s])
            grad_probs = dot_t(d_o, values)
            delta = jnp.sum(probs * grad_probs, axis=-1, keepdims=True)
            grad_scores = (probs * (grad_probs - delta)).astype(BF16)
            d_q = matmul(grad_scores, keys) * scale
            d_k = (t_dot(grad_scores, q) * scale).astype(BF16)
            d_v = t_dot(probs.astype(BF16), d_o).astype(BF16)
            both = jnp.concatenate([d_k, d_v], axis=1)
            if big:
                xkv[...] = both
                copies = [
                    pltpu.make_async_copy(
                        xkv.at[pl.ds(j * rows, rows)], kv_outs[0].at[s * n_seq + j], load_sem.at[j]
                    )
                    for j in range(n_seq)
                ]
                for cp in copies:
                    cp.start()
                for cp in copies:
                    cp.wait()
            else:
                xkv[s * n_seq : (s + 1) * n_seq] = both.reshape(n_seq, rows, 2 * HD)
            for h in range(heads):
                gq[r, h * HD : (h + 1) * HD] = rotate(
                    d_q[h * rows : (h + 1) * rows], cos[...], -sin[...]
                ).astype(BF16)
            if s + 2 >= groups:
                get_o.run(4 if s + 2 == groups else 2)
        if big:
            get_kv = Steps(sum_kv.steps(at, kv_outs[0], kv_outs[1:], op_scratch[8], shared_refs[:3]))
        else:
            get_kv = Steps(sum_kv.steps(at, xkv, kv_sum, op_scratch[8]))
        get_kv.run()
        moves[1].run()
        for s in range(groups):
            xn[s] = dot_t(gq[s * rows : (s + 1) * rows, :], wq_r[...]).astype(BF16)
        get_n = Steps(sum_n.steps(at, xn, n_sum, op_scratch[9]))
        get_n.run()

        def poll():
            get_kv.run(1)

        for j in range(n_seq):
            part = t_dot(norm_all[:, :, j * d_rows : (j + 1) * d_rows].reshape(tokens, d_rows), gq[...])
            xq[j, :d_rows, :] = part.astype(BF16)
            poll()
        low = matmul(flat(norm_all), qa[...]).astype(BF16)
        part = t_dot(low, gq[...]).astype(BF16)
        for j in range(n_seq):
            xq[j, d_rows:, :] = part[j * r_rows : (j + 1) * r_rows, :]
        get_q = Steps(sum_q.steps(at, xq, sq_out, op_scratch[6]))
        get_q.run()
        get_n.run(2)
        while get_kv.todo:
            get_kv.run(KV_STEPS)
            get_o.run()
        get_n.finish()
        moves[2].run()

        total_kv = kv_outs[1] if big else kv_sum
        gk = rotate(total_kv[:, :HD], cos[...], -sin[...]).astype(BF16)
        gv = total_kv[:, HD:].astype(BF16)
        gkv[:, :HD] = gk
        gkv[:, HD:] = gv
        get_kv2 = Steps(gather_kv.steps(at, [gkv], [gkv_all], op_scratch[1]))
        get_kv2.run()
        grad_normed = n_sum[...] + dot_t(gk, wk_r[...]) + dot_t(gv, wv_r[...])
        u_rows = unit[...]
        gain_attn_term = jnp.sum(grad_normed * u_rows, axis=0, keepdims=True)
        grad_unit = grad_normed * gain[...]
        inner = jnp.mean(grad_unit * u_rows, axis=-1, keepdims=True)
        get_o.run(2)
        get_q.run(2)
        grad_rows[...] = (gmid[...] + rms[...] * (grad_unit - u_rows * inner)).astype(BF16)
        get_kv2.finish()
        get_q.run(2)
        mine = pl.ds(pl.multiple_of(dp * share_d, share_d), share_d)
        part_rows = norm_all[:, :, mine].reshape(tokens, share_d)
        low_k = matmul(flat(norm_all), ka[...]).astype(BF16)
        low_v = matmul(flat(norm_all), va[...]).astype(BF16)
        g_rows = flat(gkv_all)
        part = t_dot(part_rows, g_rows).astype(BF16)
        low = jnp.concatenate(
            [t_dot(low_k, g_rows[:, :HD]), t_dot(low_v, g_rows[:, HD:])], axis=1
        )
        zero_r = jnp.zeros((kv_pad - kv_r, 2 * HD), F32)
        terms = jnp.concatenate([gain_attn_term, gain_term[...], jnp.zeros((14, width), F32)], axis=0)
        zero_c = jnp.zeros((16, 2 * HD - d_rows), F32)
        for j in range(n_seq):
            xk[j, :kv_d, :] = part[j * kv_d : (j + 1) * kv_d, :]
            xk[j, kv_d : kv_d + kv_pad, :] = jnp.concatenate(
                [low[j * kv_r : (j + 1) * kv_r, :], zero_r], axis=0
            ).astype(BF16)
            xk[j, kv_d + kv_pad :, :] = jnp.concatenate(
                [terms[:, j * d_rows : (j + 1) * d_rows], zero_c], axis=1
            ).astype(BF16)
        get_k = Steps(sum_k.steps(at, xk, sk_out, op_scratch[7]))
        get_k.run()
        left = [get_o, get_q, get_k]
        while any(g.todo for g in left):
            for g in left:
                g.run()
        for move in moves:
            move.finish()

    results = pl.pallas_call(
        kernel,
        name="attention_back",
        out_shape=out_shape,
        in_specs=in_specs,
        out_specs=out_specs,
        scratch_shapes=scratch,
        compiler_params=pltpu.CompilerParams(
            collective_id=collective_id, has_side_effects=True, vmem_limit_bytes=60 << 20
        ),
    )(*inputs)
    return results[:7]


def unfold(d_rows, member, owns, dg, du, dd, gate_expand, up_expand, down_adapt):
    quad, total, units = dg.shape
    rank = gate_expand.shape[0]
    r_rows = total - d_rows

    def kernel(
        me, dg_own, du_own, dd_own, dg_ref, du_ref, dd_ref, ge_ref, ue_ref, da_ref,
        wg, eg, wu, eu, wd, ad, ga, ua, de, term_g, term_u, term_d,
    ):
        first = pl.program_id(0) == 0
        mine = pl.program_id(0) == me[0]
        for own, got, term in ((dg_own, dg_ref, term_g), (du_own, du_ref, term_u), (dd_own, dd_ref, term_d)):
            term[...] = jnp.where(mine, own[0], got[0])
        for src, w, e in ((term_g, wg, eg), (term_u, wu, eu)):
            w[...] = src[:d_rows, :].astype(F32)
            e[...] = src[d_rows:, :].astype(F32)
        both = term_d[...].astype(F32).T
        wd[...] = both[:, :d_rows]
        ad[...] = both[:, d_rows:]
        for out, term in (
            (ga, dot_t(term_g[:d_rows, :], ge_ref[...])),
            (ua, dot_t(term_u[:d_rows, :], ue_ref[...])),
            (de, matmul(term_d[:d_rows, :], da_ref[...])),
        ):
            out[...] = jnp.where(first, term, term + out[...])

    cols = lambda n: pl.BlockSpec((n, units), lambda q, me: (0, q))
    side = lambda n: pl.BlockSpec((units, n), lambda q, me: (q, 0))
    block = pl.BlockSpec((1, total, units), lambda q, me: (q, 0, 0))
    own = pl.BlockSpec((1, total, units), lambda q, me: (me[0], 0, 0))
    kept = pl.BlockSpec((d_rows, rank), lambda q, me: (0, 0))
    shape = lambda *s: jax.ShapeDtypeStruct(s, F32)
    all_units = quad * units
    return pl.pallas_call(
        kernel,
        name="unfold",
        grid_spec=pltpu.PrefetchScalarGridSpec(
            num_scalar_prefetch=1,
            grid=(quad,),
            in_specs=[own] * 3 + [block] * 3 + [cols(rank), cols(rank), side(rank)],
            out_specs=[cols(d_rows), cols(r_rows), cols(d_rows), cols(r_rows), side(d_rows), side(r_rows)] + [kept] * 3,
            scratch_shapes=[pltpu.VMEM((total, units), BF16)] * 3,
        ),
        out_shape=[
            shape(d_rows, all_units), shape(r_rows, all_units), shape(d_rows, all_units), shape(r_rows, all_units),
            shape(all_units, d_rows), shape(all_units, r_rows),
        ] + [shape(d_rows, rank)] * 3,
        compiler_params=pltpu.CompilerParams(vmem_limit_bytes=56 << 20),
    )(member, *owns, dg, du, dd, gate_expand, up_expand, down_adapt)


def local(
    topo,
    tokens, segment_ids, out_grad, gain_attn, gain_mlp, w_query, w_key, w_value, w_out, w_gate, w_up, w_down,
    query_adapt, query_expand, key_adapt, key_expand, value_adapt, value_expand, out_adapt, out_expand,
    gate_adapt, gate_expand, up_adapt, up_expand, down_adapt, down_expand,
):
    rows, width = tokens.shape[2], tokens.shape[3]
    groups, n_seq = topo.n_dp, topo.n_seq
    length = rows * n_seq
    heads_dev = w_query.shape[1] // HD
    head_cols = heads_dev * HD
    rank = query_adapt.shape[1]
    scale_qk = HD ** (-0.5)
    quad = topo.group_size("quad")
    units = w_gate.shape[1] // quad
    seq = lax.axis_index("seq")
    dp = lax.axis_index("dp")

    def merged(weight, adapt, expand):
        return (weight.astype(F32) + matmul(adapt, expand)).astype(BF16)

    wq = merged(w_query, query_adapt, query_expand)
    wk = merged(w_key, key_adapt, key_expand)
    wv = merged(w_value, value_adapt, value_expand)
    wo = merged(w_out, out_adapt, out_expand)
    token_rows = tokens[0, 0].astype(F32)
    grad_rows_in = out_grad[0, 0]
    normed, unit_attn, rms_attn = normalize(token_rows, gain_attn)
    normed_attn = normed.astype(BF16)
    positions = seq * rows + jnp.arange(rows, dtype=jnp.int32)
    cosine_table, sine_table = rotary(positions, HD)
    cosine_heads, sine_heads = cosine_table[:, None, :], sine_table[:, None, :]
    key_rot = rotate(matmul(normed_attn, wk), cosine_table, sine_table).astype(BF16)
    value_rows = matmul(normed_attn, wv).astype(BF16)
    key_value = jnp.concatenate([key_rot, value_rows], axis=1)
    seg_rows = jnp.zeros((16, rows), F32).at[0].set(segment_ids[0, 0].astype(F32))

    zyx, xzy = "lhbxc", "xlhbc"
    (normed_all,), (kv_all,), (seg_all,), (grad_half,) = communicate(
        topo, "gather_attention", 0,
        Gather(topo, "dp", normed_attn, [(0, rows, "xc")]),
        Gather(topo, "all", key_value, row_parts(rows, (zyx, xzy), (7, 4))),
        Gather(topo, "all", seg_rows, [(0, 16, zyx)]),
        Gather(topo, "half", grad_rows_in, row_parts(rows, ("xlbc", "lbxc", "bxlc"), (1, 1, 1))),
    )
    kv_all = kv_all.reshape(groups, length, 2 * HD)
    keys_all, values_all = kv_all[..., :HD], kv_all[..., HD:]
    segments = seg_all[:, 0, :].reshape(groups, length)
    own_segments = lax.dynamic_slice_in_dim(segments, seq * rows, rows, 1)
    key_positions = jnp.arange(length, dtype=jnp.int32)
    causal = (key_positions[None, :] <= positions[:, None])[None, :, :]
    allowed = (causal & (own_segments[:, :, None] == segments[:, None, :]))[:, None, :, :]

    queries = matmul(normed_all.reshape(groups * rows, width), wq)
    query_rot = rotate(queries.reshape(groups, rows, heads_dev, HD), cosine_heads, sine_heads).astype(BF16)
    scores = jnp.where(allowed, contract("sthd,sjd->shtj", query_rot, keys_all) * scale_qk, MASKED)
    row_top = jnp.max(scores, axis=-1, keepdims=True)
    log_total = row_top + jnp.log(jnp.sum(jnp.exp(scores - row_top), axis=-1, keepdims=True))
    prob_low = jnp.exp(scores - log_total).astype(BF16)
    heads_out = (
        contract("shtj,sjd->sthd", prob_low, values_all).reshape(groups * rows, head_cols).astype(BF16)
    )
    out_part = matmul(heads_out, wo).astype(BF16).reshape(groups, rows, width)
    (out_sum,), = communicate(
        topo, "sum_attention", 1, Scatter(topo, "dp", out_part, [(0, rows, "cx")])
    )
    middle = token_rows + out_sum
    normed, unit_mlp, rms_mlp = normalize(middle, gain_mlp)
    normed_mlp = normed.astype(BF16)
    down_sum, gn_sum, dg, du, dd = feed_forward(
        topo, 2, normed_mlp, grad_rows_in, grad_half,
        w_gate, w_up, w_down, gate_adapt, gate_expand, up_adapt, up_expand, down_adapt, down_expand,
    )
    result_rows = (middle + down_sum).astype(BF16)
    gain_mlp_term, grad_from_mlp = norm_backward(gn_sum, unit_mlp, rms_mlp, gain_mlp)
    grad_middle = grad_rows_in.astype(F32) + grad_from_mlp
    grad_branch_attn = grad_middle.astype(BF16)
    my_kv_ranks = lambda a: lax.dynamic_slice_in_dim(a, dp * (rank // groups), rank // groups, 1)
    owns = (dg, du, dd)
    grad_rows, so, sq, sk, dg, du, dd = attention_back(
        topo, 4, grad_branch_attn, grad_middle,
        query_rot.reshape(groups * rows, head_cols), heads_out, kv_all.reshape(groups * length, 2 * HD),
        log_total.reshape(groups, heads_dev * rows, 1), own_segments.T, segments,
        normed_all, unit_attn, rms_attn, gain_attn[None], gain_mlp_term[None], cosine_table, sine_table,
        wo, wq, wk, wv, query_adapt, out_expand, my_kv_ranks(key_adapt), my_kv_ranks(value_adapt), dg, du, dd,
    )
    d_rows, r_rows = width // n_seq, rank // n_seq
    per_dev_d, per_dev_r = d_rows // groups, r_rows // groups
    kv_pad = -(-per_dev_r // 16) * 16
    grad_wg, grad_ge, grad_wu, grad_ue, grad_wd, grad_da, part_ga, part_ua, part_de = unfold(
        d_rows, lax.rem(seq, topo.group_size("quad")).reshape(1), owns, dg, du, dd, gate_expand, up_expand, down_adapt
    )
    grad_wq, grad_qe = sq[:d_rows], sq[d_rows:]
    grad_wo, grad_oa = so[:d_rows].T, so[d_rows:].T
    grad_wkv, grad_kve = sk[:per_dev_d], sk[per_dev_d : per_dev_d + per_dev_r]
    gains = jnp.pad(sk[per_dev_d + kv_pad : per_dev_d + kv_pad + 2, :d_rows], ((0, 6), (0, 0)))

    adapt = jnp.stack(
        [
            part_ga,
            part_ua,
            dot_t(grad_wq.astype(BF16), query_expand),
        ]
    )
    expand = jnp.stack(
        [
            part_de.T,
            matmul(so[:d_rows].astype(BF16), out_adapt).T,
        ]
    )
    adapt = adapt.reshape(3, groups, per_dev_d, rank).transpose(1, 0, 2, 3).reshape(groups, -1, rank)
    expand = expand.reshape(2, groups, rank // groups, d_rows).transpose(1, 0, 2, 3).reshape(groups, -1, d_rows)
    expand = jnp.pad(expand, ((0, 0), (0, 0), (0, rank - d_rows)))
    small_gains = jnp.pad(
        gains[:, :d_rows].reshape(8, groups, per_dev_d).transpose(1, 0, 2), ((0, 0), (0, 8), (0, rank - per_dev_d))
    )
    small = jnp.concatenate([adapt, small_gains, expand], axis=1).astype(BF16)
    n_adapt = 3 * per_dev_d
    (small_sum,), = communicate(
        topo, "sum_small", 8, Scatter(topo, "dp", small, [(0, small.shape[1], "cx")])
    )
    per_seq = rank // groups // n_seq
    across = small_sum[n_adapt + 16 :, :d_rows].reshape(2, n_seq, per_seq, d_rows).transpose(1, 0, 2, 3)
    across = across.reshape(n_seq, 2 * per_seq, d_rows)
    (own_adapt, own_expand), = communicate(
        topo, "finish", 9, Finish(topo, small_sum[: n_adapt + 16], across)
    )
    grad_ga, grad_ua, grad_qa = own_adapt[:n_adapt].reshape(3, per_dev_d, rank)
    grad_gain_attn = own_adapt[n_adapt, :per_dev_d]
    grad_gain_mlp = own_adapt[n_adapt + 1, :per_dev_d]
    own_expand = own_expand.reshape(n_seq, 2, per_seq, d_rows).transpose(1, 2, 0, 3).reshape(2, per_seq, width)
    grad_de, grad_oe = own_expand[0], own_expand[1]
    grad_wk, grad_wv = grad_wkv[:, :HD], grad_wkv[:, HD:]
    grad_ka = dot_t(grad_wk.astype(BF16), key_expand)
    grad_va = dot_t(grad_wv.astype(BF16), value_expand)
    grad_ke, grad_ve = grad_kve[:, :HD], grad_kve[:, HD:]
    return (
        result_rows[None, None], grad_rows[None, None],
        grad_gain_attn, grad_gain_mlp,
        grad_wq, grad_wk, grad_wv, grad_wo, grad_wg, grad_wu, grad_wd,
        grad_qa, grad_qe, grad_ka, grad_ke, grad_va, grad_ve, grad_oa, grad_oe,
        grad_ga, grad_ge, grad_ua, grad_ue, grad_da, grad_de,
    )


def solution(mesh):
    topo = Topo(mesh.shape["dp"], mesh.shape["seq"])
    both = ("dp", "seq")
    in_specs = (
        P(None, "dp", "seq", None), P(None, "dp", "seq"), P(None, "dp", "seq", None),
        P(), P(), P(None, "dp"), P(), P(), P("dp", None), P(None, "dp"), P(None, "dp"), P("dp", None),
        P(), P(None, "dp"), P(), P(), P(), P(), P("dp", None), P(),
        P(), P(None, "dp"), P(), P(None, "dp"), P("dp", None), P(),
    )
    out_specs = (
        P(None, "dp", "seq", None), P(None, "dp", "seq", None), P(both), P(both),
        P("seq", "dp"), P(both, None), P(both, None), P("dp", "seq"), P("seq", "dp"), P("seq", "dp"), P("dp", "seq"),
        P(both, None), P("seq", "dp"), P(both, None), P(both, None), P(both, None), P(both, None),
        P("dp", "seq"), P(both, None), P(both, None), P("seq", "dp"), P(both, None), P("seq", "dp"),
        P("dp", "seq"), P(both, None),
    )
    return jax.shard_map(
        lambda *args: local(topo, *args), mesh=mesh, in_specs=in_specs, out_specs=out_specs, check_vma=False
    )
```

```python
import itertools
import math

import jax
import jax.numpy as jnp
from jax import lax
from jax.experimental import pallas as pl
from jax.experimental.pallas import tpu as pltpu
from jax.sharding import PartitionSpec as P

HD = 256
EPSILON = 1e-06
ROTARY_BASE = 10000.0
MASKED = -1e30

MESH = pl.DeviceIdType.MESH
BF16 = jnp.bfloat16
F32 = jnp.float32


class Topo:
    def __init__(self, n_dp, n_seq):
        self.n_dp, self.n_seq = n_dp, n_seq
        self.size = {"c": 2, "x": n_dp // 2, "b": n_seq // 4, "l": 2, "h": 2}

    def here(self):
        dp, seq = lax.axis_index("dp"), lax.axis_index("seq")
        nb = self.size["b"]
        outer = lax.div(seq, nb)
        return {
            "c": lax.rem(dp, 2),
            "x": lax.div(dp, 2),
            "b": lax.rem(seq, nb),
            "l": lax.rem(outer, 2),
            "h": lax.div(outer, 2),
        }

    def moved(self, at, dims, offsets, sign=1):
        new = dict(at)
        for dim, offset in zip(dims, offsets):
            n = self.size[dim]
            if not (isinstance(offset, int) and offset == 0):
                new[dim] = lax.rem(at[dim] + (offset if sign > 0 else n - offset), n)
        return new

    def seq_of(self, at):
        return (at["h"] * 2 + at["l"]) * self.size["b"] + at["b"]

    def device(self, at):
        return (at["x"] * 2 + at["c"], self.seq_of(at))

    def index(self, at, group):
        dp, seq = self.device(at)
        if group == "all":
            return dp * self.n_seq + seq
        if group == "half":
            nb = self.size["b"]
            return dp * (2 * nb) + at["l"] * nb + at["b"]
        if group == "dp":
            return dp
        if group == "seq":
            return seq
        if group == "quad":
            return at["l"] * self.size["b"] + at["b"]
        raise ValueError(group)

    def group_size(self, group):
        nb = self.size["b"]
        return {
            "all": self.n_dp * self.n_seq,
            "half": self.n_dp * 2 * nb,
            "dp": self.n_dp,
            "seq": self.n_seq,
            "quad": 2 * nb,
        }[group]


GROUP_DIMS = {"all": "cxblh", "half": "cxbl", "dp": "cx", "seq": "blh", "quad": "bl"}


def remote(src, dst, send_sem, recv_sem, device):
    return pltpu.make_async_remote_copy(
        src_ref=src,
        dst_ref=dst,
        send_sem=send_sem,
        recv_sem=recv_sem,
        device_id=device,
        device_id_type=MESH,
    )


def peers_of(topo, group):
    return {((dim, d),) for dim in GROUP_DIMS[group] for d in range(1, topo.size[dim])}


def digits(key, sizes):
    k = 0
    for o, s in zip(key, sizes):
        k = k * s + o
    return k


def arrived(topo, at, ref, send_sem, recv_sem):
    remote(ref, ref, send_sem, recv_sem, topo.device(at)).wait_recv()


class Gather:
    def __init__(self, topo, group, x, parts, beyond=None, need=None, keep=True):
        self.topo, self.group, self.parts, self.beyond = topo, group, parts, beyond
        self.keep = keep and not beyond
        self.slots = "half" if beyond else group
        self.need = need or (lambda dims, key: 0)
        self.inputs = [x]
        rows, cols = x.shape
        n = topo.group_size(group)
        self.outputs = [jax.ShapeDtypeStruct((topo.group_size(self.slots), rows, cols), x.dtype)]
        self.in_specs = [pl.BlockSpec(memory_space=pltpu.VMEM)]
        self.out_specs = [pl.BlockSpec(memory_space=pl.ANY)]
        self.scratch = [
            pltpu.SemaphoreType.DMA((len(parts), n)),
            pltpu.SemaphoreType.DMA((len(parts), n)),
            pltpu.SemaphoreType.DMA(()),
        ]

    def peers(self):
        return peers_of(self.topo, self.group)

    def keeps(self, order, key):
        return not self.beyond or key[order.index(self.beyond)] != 0

    def work(self):
        work = []
        for part, (row, rows, order) in enumerate(self.parts):
            for key in itertools.product(*[range(self.topo.size[dim]) for dim in order]):
                if not any(key) or self.keeps(order, key):
                    hops = sum(1 for o in key if o)
                    last = max([i for i, o in enumerate(key) if o], default=-1)
                    work.append((hops, self.need(order, key), last, part, key))
        work.sort()
        return [(w[3], w[4]) for w in work]

    def steps(self, at, ins, outs, scratch):
        topo = self.topo
        (x_ref,), (out_ref,) = ins, outs
        send_sem, recv_sem, own_sem = scratch
        size_of = lambda order: [topo.size[dim] for dim in order]

        def copy(part, key, stage, d):
            row, rows, order = self.parts[part]
            slot = topo.index(topo.moved(at, order, key, -1), self.slots)
            new_key = tuple(d if i == stage else o for i, o in enumerate(key))
            place = out_ref.at[slot, pl.ds(row, rows)]
            k = digits(new_key, size_of(order))
            target = topo.device(topo.moved(at, [order[stage]], [d]))
            source = place if any(key) else x_ref.at[pl.ds(row, rows)]
            return remote(source, place, send_sem.at[part, k], recv_sem.at[part, k], target)

        def own():
            return pltpu.make_async_copy(x_ref, out_ref.at[topo.index(at, self.slots)], own_sem)

        sent, steps = [], []
        for n, (part, key) in enumerate(self.work()):
            row, rows, order = self.parts[part]
            last = max([i for i, o in enumerate(key) if o], default=-1)
            sends = []
            for stage in range(last + 1, len(order)):
                for d in range(1, topo.size[order[stage]]):
                    new_key = tuple(d if i == stage else o for i, o in enumerate(key))
                    if self.keeps(order, new_key):
                        sends.append((self.need(order, new_key), stage, d))
            sends = [(part, key, stage, d) for _, stage, d in sorted(sends)]
            sent += sends

            def step(n=n, part=part, key=key, sends=sends):
                row, rows, order = self.parts[part]
                if n == 0 and self.keep:
                    own().start()
                if any(key):
                    slot = topo.index(topo.moved(at, order, key, -1), self.slots)
                    k = digits(key, size_of(order))
                    arrived(topo, at, out_ref.at[slot, pl.ds(row, rows)], send_sem.at[part, k], recv_sem.at[part, k])
                for send in sends:
                    copy(*send).start()

            steps.append(step)

        def end():
            for send in sent:
                copy(*send).wait_send()
            if self.keep:
                own().wait()

        return steps, [end]


TILE = 512


class Reduce:
    def __init__(self, topo, group, shape, dtype, parts):
        self.topo, self.group, self.parts, self.dtype = topo, group, parts, dtype
        n, rows, cols = shape
        assert n == topo.group_size(group), (n, group)
        self.tile = math.gcd(cols, TILE)

    def peers(self):
        return peers_of(self.topo, self.group)

    def stages(self, part):
        sizes = self.sizes(part)
        return [(max(s - 1, 1), math.prod(sizes[k + 1 :])) for k, s in enumerate(sizes)]

    def sizes(self, part):
        return [self.topo.size[dim] for dim in self.parts[part][2]]

    def jobs(self):
        jobs = []
        for part in range(len(self.parts)):
            sizes = self.sizes(part)
            keys = list(itertools.product(*[range(s) for s in sizes]))
            first = {k: min([i for i, o in enumerate(k) if o], default=len(sizes)) for k in keys}
            keys.sort(key=lambda k: (first[k], [0 if o else 1 for o in k]))
            jobs += [(first[key], rank, part, key) for rank, key in enumerate(keys)]
        jobs.sort()
        return [(first, part, key) for first, _, part, key in jobs]

    def block(self, at, part, key):
        return self.topo.index(self.topo.moved(at, self.parts[part][2], key), self.group)

    def target(self, at, part, key, stage):
        return self.topo.device(self.topo.moved(at, [self.parts[part][2][stage]], [key[stage]]))

    def place(self, part, key, stage):
        return key[stage] - 1, digits(key[stage + 1 :], self.sizes(part)[stage + 1 :])

    def terms(self, part, key, first):
        sizes = self.sizes(part)
        return [
            (stage, d - 1, digits(key[stage + 1 :], sizes[stage + 1 :]))
            for stage in range(first)
            for d in range(1, sizes[stage])
        ]


class VScatter(Reduce):
    def __init__(self, topo, group, shape, dtype, parts):
        super().__init__(topo, group, shape, dtype, parts)
        self.scratch = []
        for part, (row, nrows, order) in enumerate(parts):
            self.scratch.append(pltpu.VMEM((math.prod(self.sizes(part)[1:]), nrows, shape[2]), dtype))
            for m, rest in self.stages(part):
                self.scratch.append(pltpu.VMEM((m, rest, nrows, shape[2]), dtype))
                self.scratch.append(pltpu.SemaphoreType.DMA((m, rest)))
                self.scratch.append(pltpu.SemaphoreType.DMA((m, rest)))

    def steps(self, at, x_ref, out_ref, scratch):
        topo, tile = self.topo, self.tile
        scratch = list(scratch)
        bufs = []
        for part in range(len(self.parts)):
            acc = scratch.pop(0)
            bufs.append((acc, [tuple(scratch.pop(0) for _ in range(3)) for _ in self.sizes(part)]))
        jobs = self.jobs()

        def send(first, part, key):
            row, nrows, order = self.parts[part]
            acc, stages = bufs[part]
            buf, send_sem, recv_sem = stages[first]
            d, k = self.place(part, key, first)
            if first == 0:
                source = x_ref.at[self.block(at, part, key), pl.ds(row, nrows)]
            else:
                source = acc.at[digits(key[1:], self.sizes(part)[1:])]
            return remote(
                source, buf.at[d, k], send_sem.at[d, k], recv_sem.at[d, k], self.target(at, part, key, first)
            )

        def start():
            for job in jobs:
                if job[0] == 0:
                    send(*job).start()

        steps = [start]
        for job in jobs:
            if job[0] == 0:
                continue

            def step(job=job):
                first, part, key = job
                row, nrows, order = self.parts[part]
                acc, stages = bufs[part]
                terms = self.terms(part, key, first)
                for stage, d, k in terms:
                    buf, send_sem, recv_sem = stages[stage]
                    arrived(topo, at, buf.at[d, k], send_sem.at[d, k], recv_sem.at[d, k])
                block, kk = self.block(at, part, key), digits(key[1:], self.sizes(part)[1:])
                final = first == len(order)

                tiles = x_ref.shape[-1] // tile

                def add(n, _):
                    r0 = pl.multiple_of(lax.div(n, tiles) * 16, 16)
                    cols = pl.ds(pl.multiple_of(lax.rem(n, tiles) * tile, tile), tile)
                    r1 = pl.ds(pl.multiple_of(row + r0, 16), 16)
                    total = x_ref[block, r1, cols].astype(F32)
                    for stage, d, k in terms:
                        total = total + stages[stage][0][d, k, pl.ds(r0, 16), cols].astype(F32)
                    if final:
                        out_ref[r1, cols] = total.astype(out_ref.dtype)
                    else:
                        acc[kk, pl.ds(r0, 16), cols] = total.astype(acc.dtype)
                    return 0

                lax.fori_loop(0, nrows // 16 * tiles, add, 0)
                if not final:
                    send(*job).start()

            steps.append(step)

        def end():
            for job in jobs:
                if job[0] < len(self.parts[job[1]][2]):
                    send(*job).wait_send()

        return steps, [end]


class SlimScatter(Reduce):
    RING = 4

    def __init__(self, topo, group, shape, dtype, parts):
        super().__init__(topo, group, shape, dtype, parts)
        rows, cols = shape[1:]
        self.outputs = [jax.ShapeDtypeStruct((rows, cols), F32)]
        self.out_specs = [pl.BlockSpec(memory_space=pltpu.VMEM)]
        self.scratch = []
        self.most, self.cols = max(p[1] for p in parts), cols
        self.count = 1 + sum(topo.size[d] - 1 for d in GROUP_DIMS[group])
        for part, (row, nrows, order) in enumerate(parts):
            for m, rest in self.stages(part):
                self.outputs.append(jax.ShapeDtypeStruct((m, rest, nrows, cols), dtype))
                self.out_specs.append(pl.BlockSpec(memory_space=pl.ANY))
                self.scratch.append(pltpu.SemaphoreType.DMA((m, rest)))
                self.scratch.append(pltpu.SemaphoreType.DMA((m, rest)))

    def shared_scratch(self):
        return [
            pltpu.VMEM((2, self.count, self.most, self.cols), self.dtype),
            pltpu.SemaphoreType.DMA((2, self.count)),
            pltpu.VMEM((self.RING, self.most, self.cols), self.dtype),
        ]

    def steps(self, at, x_ref, outs, scratch, shared):
        topo, tile = self.topo, self.tile
        outs, scratch = list(outs), list(scratch)
        out_ref = outs.pop(0)
        stage_buf, stage_sem, ring = shared
        bufs = [
            [(outs.pop(0), scratch.pop(0), scratch.pop(0)) for _ in self.sizes(part)]
            for part in range(len(self.parts))
        ]
        jobs = self.jobs()
        later = [job for job in jobs if job[0] > 0]
        passed = [job for job in later if job[0] < len(self.parts[job[1]][2])]

        def own(part, key):
            row, nrows, order = self.parts[part]
            return x_ref.at[self.block(at, part, key), pl.ds(row, nrows)]

        def send(first, part, key, source=None):
            row, nrows, order = self.parts[part]
            buf, send_sem, recv_sem = bufs[part][first]
            d, k = self.place(part, key, first)
            if source is None:
                source = own(part, key) if first == 0 else ring.at[0, pl.ds(0, nrows)]
            return remote(
                source, buf.at[d, k], send_sem.at[d, k], recv_sem.at[d, k], self.target(at, part, key, first)
            )

        def loads(n):
            first, part, key = later[n]
            nrows = self.parts[part][1]
            sources = [own(part, key)] + [
                bufs[part][stage][0].at[d, k] for stage, d, k in self.terms(part, key, first)
            ]
            return [
                pltpu.make_async_copy(ref, stage_buf.at[n % 2, i, pl.ds(0, nrows)], stage_sem.at[n % 2, i])
                for i, ref in enumerate(sources)
            ]

        def fetch(n):
            first, part, key = later[n]
            for stage, d, k in self.terms(part, key, first):
                buf, send_sem, recv_sem = bufs[part][stage]
                arrived(topo, at, buf.at[d, k], send_sem.at[d, k], recv_sem.at[d, k])
            for cp in loads(n):
                cp.start()

        def start():
            for job in jobs:
                if job[0] == 0:
                    send(*job).start()

        steps = [start, lambda: fetch(0)]
        for n in range(len(later)):

            def step(n=n):
                first, part, key = later[n]
                row, nrows, order = self.parts[part]
                copies = loads(n)
                for cp in copies:
                    cp.wait()
                final = first == len(order)
                if not final:
                    sent = passed.index(later[n])
                    if sent >= self.RING:
                        send(*passed[sent - self.RING]).wait_send()

                tiles = self.cols // tile

                def add(n_tile, _):
                    r0 = pl.multiple_of(lax.div(n_tile, tiles) * 16, 16)
                    cols = pl.ds(pl.multiple_of(lax.rem(n_tile, tiles) * tile, tile), tile)
                    total = stage_buf[n % 2, 0, pl.ds(r0, 16), cols].astype(F32)
                    for i in range(1, len(copies)):
                        total = total + stage_buf[n % 2, i, pl.ds(r0, 16), cols].astype(F32)
                    if final:
                        out_ref[pl.ds(pl.multiple_of(row + r0, 16), 16), cols] = total
                    else:
                        ring[sent % self.RING, pl.ds(r0, 16), cols] = total.astype(ring.dtype)
                    return 0

                lax.fori_loop(0, nrows // 16 * tiles, add, 0)
                if not final:
                    send(first, part, key, ring.at[sent % self.RING, pl.ds(0, nrows)]).start()
                if n + 1 < len(later):
                    fetch(n + 1)

            steps.append(step)

        def end():
            for job in jobs:
                if job[0] == 0:
                    send(*job).wait_send()
            for job in passed[-self.RING :]:
                send(*job).wait_send()

        return steps, [end]


class Exchange:
    def __init__(self, topo, group, x, keep=True):
        self.topo, self.group, self.keep = topo, group, keep
        self.inputs = [x]
        n = x.shape[0]
        assert n == topo.group_size(group)
        self.outputs = [jax.ShapeDtypeStruct(x.shape, x.dtype)]
        self.in_specs = [pl.BlockSpec(memory_space=pl.ANY)]
        self.out_specs = [pl.BlockSpec(memory_space=pl.ANY)]
        self.scratch = [
            pltpu.SemaphoreType.DMA((n,)),
            pltpu.SemaphoreType.DMA((n,)),
            pltpu.SemaphoreType.DMA(()),
        ]

    def offsets(self):
        dims = GROUP_DIMS[self.group]
        return dims, [
            o for o in itertools.product(*[range(self.topo.size[d]) for d in dims]) if any(o)
        ]

    def peers(self):
        dims, offsets = self.offsets()
        return {tuple((dim, o) for dim, o in zip(dims, off) if o) for off in offsets}

    def steps(self, at, ins, outs, scratch):
        topo = self.topo
        (x_ref,), (out_ref,) = ins, outs
        send_sem, recv_sem, own_sem = scratch
        dims, offsets = self.offsets()
        me = topo.index(at, self.group)

        def own():
            return pltpu.make_async_copy(x_ref.at[me], out_ref.at[me], own_sem)

        def send(i):
            there = topo.moved(at, dims, offsets[i])
            source = x_ref.at[topo.index(there, self.group)]
            return remote(source, out_ref.at[me], send_sem.at[i], recv_sem.at[i], topo.device(there))

        def start():
            if self.keep:
                own().start()
            for i in range(len(offsets)):
                send(i).start()

        def wait(i):
            ref = out_ref.at[topo.index(topo.moved(at, dims, offsets[i], -1), self.group)]
            arrived(topo, at, ref, send_sem.at[i], recv_sem.at[i])

        def end():
            for i in range(len(offsets)):
                send(i).wait_send()
            if self.keep:
                own().wait()

        return [start] + [lambda i=i: wait(i) for i in range(len(offsets))], [end]


class Finish:
    def __init__(self, topo, x, y):
        self.topo = topo
        self.inputs = [x, y]
        self.outputs = [
            jax.ShapeDtypeStruct(x.shape, x.dtype),
            jax.ShapeDtypeStruct(y.shape, y.dtype),
        ]
        self.in_specs = [pl.BlockSpec(memory_space=pl.ANY)] * 2
        self.out_specs = [pl.BlockSpec(memory_space=pl.ANY)] * 2
        self.inner = Exchange(topo, "seq", y)
        self.scratch = self.inner.scratch + [pltpu.SemaphoreType.DMA(())] * 3

    def peers(self):
        return self.inner.peers()

    def route(self):
        topo = self.topo
        dp, seq = lax.axis_index("dp"), lax.axis_index("seq")
        n = seq * topo.n_dp + dp
        target = (lax.div(n, topo.n_seq), lax.rem(n, topo.n_seq))
        m = dp * topo.n_seq + seq
        source = (lax.rem(m, topo.n_dp), lax.div(m, topo.n_dp))
        stays = (target[0] == dp) & (target[1] == seq)
        return target, source, stays

    def greet(self, barrier):
        target, source, stays = self.route()

        @pl.when(jnp.logical_not(stays))
        def _():
            pl.semaphore_signal(barrier, inc=1, device_id=source, device_id_type=MESH)

        return jnp.where(stays, 0, 1)

    def steps(self, at, ins, outs, scratch):
        (x_ref, y_ref), (x_out, y_out) = ins, outs
        send_sem, recv_sem, own_sem = scratch[3:]
        target, source, stays = self.route()
        cp = remote(x_ref, x_out, send_sem, recv_sem, target)
        own = pltpu.make_async_copy(x_ref, x_out, own_sem)
        inner, ends = self.inner.steps(at, [y_ref], [y_out], scratch[:3])

        def start():
            pl.when(stays)(own.start)
            pl.when(jnp.logical_not(stays))(cp.start)

        def end():
            pl.when(stays)(own.wait)
            pl.when(jnp.logical_not(stays))(cp.wait)

        return [start] + inner, ends + [end]


def greet(topo, ops):
    at = topo.here()
    peers = sorted(set().union(*[op.peers() for op in ops]))
    barrier = pltpu.get_barrier_semaphore()
    for peer in peers:
        there = topo.device(topo.moved(at, [p[0] for p in peer], [p[1] for p in peer]))
        pl.semaphore_signal(barrier, inc=1, device_id=there, device_id_type=MESH)
    count = len(peers)
    for op in ops:
        if hasattr(op, "greet"):
            count = count + op.greet(barrier)
    pl.semaphore_wait(barrier, count)
    return at


class Steps:
    def __init__(self, steps):
        self.todo = steps[0] + steps[1]

    def run(self, count=1):
        for _ in range(count):
            if self.todo:
                self.todo.pop(0)()

    def finish(self):
        self.run(len(self.todo))


def run_slot(t, slots):
    def tree(low, high):
        if not any(slots[low:high]):
            return
        if high - low == 1:
            for step in slots[low]:
                step()
            return
        middle = (low + high) // 2
        left, right = any(slots[low:middle]), any(slots[middle:high])
        if left and right:
            lax.cond(t < middle, lambda: tree(low, middle), lambda: tree(middle, high))
        elif left:
            pl.when(t < middle)(lambda: tree(low, middle))
        else:
            pl.when(t >= middle)(lambda: tree(middle, high))

    tree(0, len(slots))


def communicate(topo, name, collective_id, *ops):
    n_in = [len(op.inputs) for op in ops]
    n_out = [len(op.outputs) for op in ops]
    n_scratch = [len(op.scratch) for op in ops]

    def kernel(*refs):
        refs = list(refs)
        take = lambda counts: [[refs.pop(0) for _ in range(k)] for k in counts]
        ins, outs, scratch = take(n_in), take(n_out), take(n_scratch)
        at = greet(topo, ops)
        running = [Steps(op.steps(at, i, o, s)) for op, i, o, s in zip(ops, ins, outs, scratch)]
        while any(r.todo for r in running):
            for r in running:
                r.run()

    results = pl.pallas_call(
        kernel,
        name=name,
        out_shape=[s for op in ops for s in op.outputs],
        in_specs=[s for op in ops for s in op.in_specs],
        out_specs=[s for op in ops for s in op.out_specs],
        scratch_shapes=[s for op in ops for s in op.scratch],
        compiler_params=pltpu.CompilerParams(
            collective_id=collective_id, has_side_effects=True, vmem_limit_bytes=58 << 20
        ),
    )(*[x for op in ops for x in op.inputs])
    results = list(results)
    return [[results.pop(0) for _ in range(k)] for k in n_out]


class Scatter(VScatter):
    def __init__(self, topo, group, x, parts):
        super().__init__(topo, group, x.shape, x.dtype, parts)
        self.inputs = [x]
        self.outputs = [jax.ShapeDtypeStruct(x.shape[1:], F32)]
        self.in_specs = [pl.BlockSpec(memory_space=pltpu.VMEM)]
        self.out_specs = [pl.BlockSpec(memory_space=pltpu.VMEM)]

    def steps(self, at, ins, outs, scratch):
        return super().steps(at, ins[0], outs[0], scratch)


def row_parts(rows, orders, weights, step=16):
    parts, row, total = [], 0, sum(weights)
    for i, (order, weight) in enumerate(zip(orders, weights)):
        n = rows - row if i == len(orders) - 1 else min(rows - row, int(round(rows * weight / total / step)) * step)
        if n:
            parts.append((row, n, order))
            row += n
    return parts


def matmul(left, right):
    return jnp.dot(left, right, preferred_element_type=jnp.float32)


def contract(form, left, right):
    return jnp.einsum(form, left, right, preferred_element_type=jnp.float32)


def rotary(positions, size):
    half_size = size // 2
    frequency = ROTARY_BASE ** (-(jnp.arange(half_size, dtype=jnp.float32) * 2.0) / size)
    angles = positions.astype(jnp.float32)[:, None] * frequency[None, :]
    return (jnp.cos(angles), jnp.sin(angles))


def rotate(values, cosine_table, sine_table):
    half_size = values.shape[-1] // 2
    first_half = values[..., :half_size]
    second_half = values[..., half_size:]
    return jnp.concatenate(
        [
            first_half * cosine_table - second_half * sine_table,
            second_half * cosine_table + first_half * sine_table,
        ],
        axis=-1,
    )


def normalize(values, gain_vector):
    inverse_rms = lax.rsqrt(jnp.mean(values * values, axis=-1, keepdims=True) + EPSILON)
    unit_rows = values * inverse_rms
    return (unit_rows * gain_vector, unit_rows, inverse_rms)


def norm_backward(grad_normed, unit_rows, inverse_rms, gain_vector):
    gain_term = jnp.sum(grad_normed * unit_rows, axis=0)
    grad_unit = grad_normed * gain_vector
    inner = jnp.mean(grad_unit * unit_rows, axis=-1, keepdims=True)
    return (gain_term, inverse_rms * (grad_unit - unit_rows * inner))


def dot_t(left, right):
    return lax.dot_general(left, right, (((1,), (1,)), ((), ())), preferred_element_type=F32)


def t_dot(left, right):
    return lax.dot_general(left, right, (((0,), (0,)), ((), ())), preferred_element_type=F32)


GELU_C = math.sqrt(2.0 / math.pi)


def gelu_parts(v):
    square = v * v
    t = jnp.tanh(GELU_C * (v + 0.044715 * v * square))
    half_up = 0.5 * (1.0 + t)
    slope = half_up + 0.5 * v * (1.0 - t * t) * (GELU_C * (1.0 + 3.0 * 0.044715 * square))
    return v * half_up, slope


def feed_forward(
    topo, collective_id, normed, grads, grads_half,
    w_gate, w_up, w_down, gate_adapt, gate_expand, up_adapt, up_expand, down_adapt, down_expand,
):
    rows, width = normed.shape
    quad = topo.group_size("quad")
    half = topo.group_size("half")
    units = w_gate.shape[1] // quad
    rank = gate_adapt.shape[1]
    ranks = rank // 2
    half_width = width // 2
    d_rows, r_rows = half_width // quad, ranks // quad
    per_chunk = 512 // rows
    tile = 512
    block = 256

    dims = "hxclb"
    keys = list(itertools.product(*[range(topo.size[d]) for d in dims]))
    chunks = [keys[i : i + per_chunk] for i in range(0, len(keys), per_chunk)]
    own = len(chunks) // 2
    chunk_of = {key: i for i, keys_of in enumerate(chunks) for key in keys_of}

    def need(order, key):
        at_dim = dict(zip(order, key))
        return chunk_of[tuple(at_dim.get(d, 0) for d in dims)]

    near = row_parts(rows, ("xlbc", "lbxc", "bxlc"), (1, 1, 1))
    both = jnp.concatenate([normed, grads], axis=0)
    far = row_parts(2 * rows, ("hxlbc", "hlbxc", "hbxlc"), (1, 1, 1))
    gather_n = Gather(topo, "half", normed, near, need=need, keep=False)
    gather_far = Gather(topo, "all", both, far, beyond="h", need=need)
    thirds = row_parts(2 * rows, ("cxlb", "cbxl", "clbx"), (1, 1, 1))
    sum_both = SlimScatter(topo, "half", (half, 2 * rows, width), BF16, thirds)
    comm = [gather_n, gather_far, sum_both]

    inputs = [
        normed, both, grads_half, w_gate, w_up, w_down,
        gate_adapt, gate_expand, up_adapt, up_expand, down_adapt, down_expand,
    ]
    part = jax.ShapeDtypeStruct((half, 2 * rows, width), BF16)
    grad = jax.ShapeDtypeStruct((quad, d_rows + r_rows, units), BF16)
    any_spec = pl.BlockSpec(memory_space=pl.ANY)
    out_shape = [part, grad, grad, grad]
    out_specs = [any_spec] * 4
    scratch = [
        pltpu.VMEM((width, units), BF16), pltpu.VMEM((width, units), BF16), pltpu.VMEM((units, width), BF16),
        pltpu.VMEM((width, rank), BF16), pltpu.VMEM((rank, units), BF16),
        pltpu.VMEM((width, rank), BF16), pltpu.VMEM((rank, units), BF16),
        pltpu.VMEM((units, rank), BF16), pltpu.VMEM((rank, width), BF16),
        pltpu.VMEM((half_width + ranks, units), F32),
        pltpu.VMEM((half_width + ranks, units), F32),
        pltpu.VMEM((half_width + ranks, units), F32),
        pltpu.VMEM((3, tile, units), BF16),
        pltpu.VMEM((3, tile, ranks), BF16),
        pltpu.VMEM((2, tile, width), BF16), pltpu.VMEM((2, tile, width), BF16),
        pltpu.VMEM((tile, width), BF16), pltpu.VMEM((tile, width), BF16),
        pltpu.SemaphoreType.DMA((9,)),
        pltpu.SemaphoreType.DMA((2, 2, per_chunk)),
        pltpu.SemaphoreType.DMA((2, per_chunk)),
        pltpu.SemaphoreType.DMA((3,)),
    ]
    n_own = len(scratch)
    shared = sum_both.shared_scratch()
    scratch = scratch + shared
    for op in comm:
        out_shape = out_shape + op.outputs
        out_specs = out_specs + op.out_specs
        scratch = scratch + op.scratch

    def kernel(*refs):
        refs = list(refs)
        (
            n_hbm, both_hbm, g_half, wg_hbm, wu_hbm, wd_hbm, ga_hbm, ge_hbm, ua_hbm, ue_hbm, da_hbm, de_hbm,
        ) = [refs.pop(0) for _ in inputs]
        part_hbm, dg_out, du_out, dd_out = [refs.pop(0) for _ in range(4)]
        op_outs = [[refs.pop(0) for _ in op.outputs] for op in comm]
        (
            wg, wu, wd, ga, ge, ua, ue, da, de, acc_g, acc_u, acc_d, acts, low_s, n_buf, g_buf, down_st, gn_st,
            w_sem, load_sem, store_sem, grad_sem,
        ) = [refs.pop(0) for _ in range(n_own)]
        shared_refs = [refs.pop(0) for _ in shared]
        op_scratch = [[refs.pop(0) for _ in op.scratch] for op in comm]
        mix_s, gg_s, gu_s = acts.at[0], acts.at[1], acts.at[2]
        at = topo.here()
        high = at["h"]
        member = topo.index(at, "quad")
        unit_at = pl.multiple_of(member * units, units)

        w_copies = [
            pltpu.make_async_copy(src, dst, w_sem.at[i])
            for i, (src, dst) in enumerate(
                (
                    (de_hbm, de),
                    (da_hbm.at[pl.ds(unit_at, units), :], da),
                    (wd_hbm.at[pl.ds(unit_at, units), :], wd),
                    (ga_hbm, ga),
                    (ge_hbm.at[:, pl.ds(unit_at, units)], ge),
                    (wg_hbm.at[:, pl.ds(unit_at, units)], wg),
                    (ua_hbm, ua),
                    (ue_hbm.at[:, pl.ds(unit_at, units)], ue),
                    (wu_hbm.at[:, pl.ds(unit_at, units)], wu),
                )
            )
        ]
        for cp in w_copies:
            cp.start()

        greet(topo, comm)
        gathers = (gather_n, gather_far)
        all_steps = [op.steps(at, [x], o, sc) for op, x, o, sc in zip(gathers, (n_hbm, both_hbm), op_outs, op_scratch)]
        ranked = []
        for g, (op, (steps_g, _)) in enumerate(zip(gathers, all_steps)):
            for i, (f, (p, k)) in enumerate(zip(steps_g, op.work())):
                when = NEAR_US * i / len(steps_g) - 20.0 if g == 0 else FAR_AT + i * FAR_US
                ranked.append((when if any(k) or g else -1e3, g, i, f, need(op.parts[p][2], k)))
        ranked.sort(key=lambda w: w[:3])
        steps = [(f, chunk) for _, _, _, f, chunk in ranked]
        when_of = [w[0] for w in ranked]
        started = len(gather_n.parts)
        for f, _ in steps[:started]:
            f()

        def upto(chunk, done):
            last = [i for i, (_, c) in enumerate(steps) if c <= chunk and i >= started]
            return max([done] + [i + 1 for i in last])

        acc_g[...] = jnp.zeros_like(acc_g)
        acc_u[...] = jnp.zeros_like(acc_u)
        acc_d[...] = jnp.zeros_like(acc_d)

        def merge_rows(weight, adapt, expand, total):
            def one(i, _):
                r = pl.ds(pl.multiple_of(i * block, block), block)
                weight[r, :] = (weight[r, :].astype(F32) + matmul(adapt[r, :], expand[...])).astype(BF16)
                return 0

            lax.fori_loop(0, total // block, one, 0)

        first_chunk = upto(0, started)
        ready = [started]

        def early(count):
            last = min(ready[0] + count, first_chunk)
            for f, _ in steps[ready[0] : last]:
                f()
            ready[0] = last

        for cp in w_copies[:3]:
            cp.wait()
        merge_rows(wd, da, de, units)
        early(int(EARLY))
        for cp in w_copies[3:6]:
            cp.wait()
        merge_rows(wg, ga, ge, width)
        early(int(EARLY))
        for cp in w_copies[6:]:
            cp.wait()
        merge_rows(wu, ua, ue, width)

        def key_of(c, i):
            k = c * per_chunk + i
            key = []
            for d in reversed(dims):
                key.append(lax.rem(k, topo.size[d]))
                k = lax.div(k, topo.size[d])
            return key[::-1]

        def chunk_copies(c, slot, other):
            copies = []
            for i in range(per_chunk):
                origin = topo.moved(at, dims, key_of(c, i), -1)
                r = pl.ds(i * rows, rows)
                in_half = topo.index(origin, "half")
                if other:
                    n_src = op_outs[1][0].at[in_half, pl.ds(0, rows)]
                    g_src = op_outs[1][0].at[in_half, pl.ds(rows, rows)]
                else:
                    n_src, g_src = op_outs[0][0].at[in_half], g_half.at[in_half]
                copies.append(pltpu.make_async_copy(n_src, n_buf.at[slot, r], load_sem.at[slot, 0, i]))
                copies.append(pltpu.make_async_copy(g_src, g_buf.at[slot, r], load_sem.at[slot, 1, i]))
            return copies

        def first_copies():
            copies = chunk_copies(0, 0, False)
            r = pl.ds(0, rows)
            copies[0] = pltpu.make_async_copy(n_hbm, n_buf.at[0, r], load_sem.at[0, 0, 0])
            return copies

        def store_copies(c):
            copies = []
            for i in range(per_chunk):
                slot = topo.index(topo.moved(at, dims, key_of(c, i), -1), "half")
                r = pl.ds(i * rows, rows)
                for k, source in enumerate((gn_st, down_st)):
                    place = part_hbm.at[slot, pl.ds(k * rows, rows)]
                    copies.append(pltpu.make_async_copy(source.at[r], place, store_sem.at[k, i]))
            return copies

        n_one, n_two, n_three = units // block, width // block, half_width // block
        scale = units / 1024
        kinds = {
            False: [("one", n_one, 1.9), ("two", n_two, 1.0 * scale), ("pre", 1, 2.0 * scale), ("three", n_three, 0.7 * scale)],
            True: [("one", n_one, 1.9), ("pre", 1, 2.0 * scale), ("three", n_three, 0.7 * scale)],
        }
        slots = {(other, kind): [[] for _ in range(own * n)] for other in (False, True) for kind, n, _ in kinds[other]}
        done = first_chunk
        for f, _ in steps[ready[0] : done]:
            f()
        clock = 0.0
        for c in range(len(chunks)):
            other = c >= own
            for kind, n, cost in kinds[other]:
                for i in range(n):
                    clock += cost
                    target = max(done, sum(1 for w in when_of if w <= clock))
                    if kind == "pre" and c + 1 < len(chunks):
                        target = upto(c + 1, target)
                    slots[other, kind][(c - own if other else c) * n + i] += [f for f, _ in steps[done:target]]
                    done = target
        sums, sums_end = sum_both.steps(at, part_hbm, op_outs[2], op_scratch[2], shared_refs)
        clock, summed = 0.0, 0
        for c in range(own):
            for kind, n, cost in kinds[True]:
                for i in range(n):
                    clock += cost
                    target = min(len(sums), 1 + int(max(clock - 3.0, 0.0) / SUM_US))
                    if kind != "pre":
                        slots[True, kind][c * n + i] += sums[summed:target]
                        summed = target

        for cp in first_copies():
            cp.start()
        low_cols = pl.ds(pl.multiple_of(high * ranks, ranks), ranks)
        half_at = high * half_width

        def chunk_loop(other):
            first = own if other else 0

            def body(k, _):
                c = first + k
                slot = lax.rem(c, 2)
                nb, gb = n_buf.at[slot], g_buf.at[slot]
                for cp in chunk_copies(c, slot, other):
                    cp.wait()
                low_s[0] = matmul(nb[...], ga[:, low_cols]).astype(BF16)
                low_s[1] = matmul(nb[...], ua[:, low_cols]).astype(BF16)
                low_s[2] = dot_t(gb[...], de[low_cols, :]).astype(BF16)

                def one(i, _):
                    cols = pl.ds(pl.multiple_of(i * block, block), block)
                    gate = matmul(nb[...], wg[:, cols])
                    up = matmul(nb[...], wu[:, cols])
                    act, slope = gelu_parts(gate)
                    gm = dot_t(gb[...], wd[cols, :])
                    mix_s[:, cols] = (act * up).astype(BF16)
                    gg_s[:, cols] = (gm * up * slope).astype(BF16)
                    gu_s[:, cols] = (gm * act).astype(BF16)
                    run_slot(k * n_one + i, slots[other, "one"])
                    return 0

                lax.fori_loop(0, n_one, one, 0)
                if not other:

                    @pl.when(c > 0)
                    def _():
                        for cp in store_copies(c - 1):
                            cp.wait()

                    def two(i, _):
                        cols = pl.ds(pl.multiple_of(i * block, block), block)
                        down_st[:, cols] = matmul(mix_s[...], wd[:, cols]).astype(BF16)
                        gn_st[:, cols] = (dot_t(gg_s[...], wg[cols, :]) + dot_t(gu_s[...], wu[cols, :])).astype(BF16)
                        run_slot(k * n_two + i, slots[other, "two"])
                        return 0

                    lax.fori_loop(0, n_two, two, 0)
                    for cp in store_copies(c):
                        cp.start()
                for i, (acc, grads_s) in enumerate(((acc_g, gg_s), (acc_u, gu_s), (acc_d, mix_s))):
                    acc[half_width:, :] += t_dot(low_s[i], grads_s[...])
                run_slot(k, slots[other, "pre"])
                if other:

                    @pl.when(c + 1 < len(chunks))
                    def _():
                        for cp in chunk_copies(c + 1, 1 - slot, True):
                            cp.start()

                else:

                    @pl.when(c + 1 < own)
                    def _():
                        for cp in chunk_copies(c + 1, 1 - slot, False):
                            cp.start()

                    @pl.when(c + 1 == own)
                    def _():
                        for cp in chunk_copies(c + 1, 1 - slot, True):
                            cp.start()

                def three(i, _):
                    r = pl.ds(pl.multiple_of(i * block, block), block)
                    cols = pl.ds(pl.multiple_of(half_at + i * block, block), block)
                    acc_g[r, :] += t_dot(nb[:, cols], gg_s[...])
                    acc_u[r, :] += t_dot(nb[:, cols], gu_s[...])
                    acc_d[r, :] += t_dot(gb[:, cols], mix_s[...])
                    run_slot(k * n_three + i, slots[other, "three"])
                    return 0

                lax.fori_loop(0, n_three, three, 0)
                return 0

            lax.fori_loop(0, own, body, 0)

        chunk_loop(False)
        for cp in store_copies(own - 1):
            cp.wait()
        chunk_loop(True)

        pending = []
        for q in range(quad):
            for k, (acc, out) in enumerate(((acc_g, dg_out), (acc_u, du_out), (acc_d, dd_out))):
                if len(pending) >= 3:
                    pending.pop(0).wait()
                acts[k, :d_rows, :] = acc[q * d_rows : (q + 1) * d_rows, :].astype(BF16)
                acts[k, d_rows : d_rows + r_rows, :] = acc[
                    half_width + q * r_rows : half_width + (q + 1) * r_rows, :
                ].astype(BF16)
                cp = pltpu.make_async_copy(acts.at[k, pl.ds(0, d_rows + r_rows)], out.at[q], grad_sem.at[k])
                cp.start()
                pending.append(cp)
        for f in steps[done:]:
            f[0]()
        for f in sums[summed:]:
            f()
        for cp in pending:
            cp.wait()
        for f in [f for _, end in all_steps for f in end] + sums_end:
            f()

    flops = 2 * rows * topo.n_dp * topo.n_seq * units * width * 9
    results = pl.pallas_call(
        kernel,
        name="feed_forward",
        out_shape=out_shape,
        in_specs=[any_spec] * len(inputs),
        out_specs=out_specs,
        scratch_shapes=scratch,
        compiler_params=pltpu.CompilerParams(
            collective_id=collective_id, has_side_effects=True, vmem_limit_bytes=60 << 20
        ),
        cost_estimate=pl.CostEstimate(flops=flops, bytes_accessed=1 << 27, transcendentals=0),
    )(*inputs)
    dg, du, dd = results[1:4]
    total = results[4 + len(gather_n.outputs) + len(gather_far.outputs)]
    return total[rows:], total[:rows], dg, du, dd


KV_STEPS = 3
EARLY = 8
NEAR_US = 45.0
FAR_AT = 5.0
FAR_US = 1.4
SUM_US = 2.4


def attention_back(
    topo, collective_id, grad_branch, grad_middle, query_rot, heads_out, key_value, log_total, own_segs, key_segs,
    normed_all, unit_attn, rms_attn, gain_attn, gain_mlp_term, cosine, sine, wo, wq, wk, wv,
    query_adapt, out_expand, key_adapt, value_adapt, dg, du, dd,
):
    groups, rows, width = normed_all.shape
    n_seq = topo.n_seq
    length = rows * n_seq
    head_cols = heads_out.shape[1]
    heads = head_cols // HD
    tokens = groups * rows
    rank = query_adapt.shape[1]
    scale = HD ** (-0.5)
    d_rows, r_rows = width // n_seq, rank // n_seq
    share_d, share_r = width // groups, rank // groups
    kv_d, kv_r = d_rows // groups, r_rows // groups
    kv_pad = -(-kv_r // 16) * 16
    kv_rows = kv_d + kv_pad + 16

    gather_g = Gather(topo, "dp", grad_branch, row_parts(rows, ("xc", "xc"), (1, 1)))
    gather_kv = Gather(topo, "dp", jax.ShapeDtypeStruct((rows, 2 * HD), BF16), [(0, rows, "xc")])
    swaps = [Exchange(topo, "quad", a, keep=False) for a in (dg, du, dd)]
    seq_parts = lambda n: row_parts(n, ("blh", "lbh"), (2, 1))
    w_shape = (n_seq, d_rows + r_rows, head_cols)
    sum_o = VScatter(topo, "seq", w_shape, BF16, seq_parts(d_rows + r_rows))
    sum_q = VScatter(topo, "seq", w_shape, BF16, seq_parts(d_rows + r_rows))
    sum_k = VScatter(topo, "seq", (n_seq, kv_rows, 2 * HD), BF16, seq_parts(kv_rows))
    kv_shape = (groups * n_seq, rows, 2 * HD)
    sum_kv = VScatter(topo, "all", kv_shape, BF16, row_parts(rows, ("cxblh", "cblxh"), (1, 1)))
    sum_n = VScatter(topo, "dp", (groups, rows, width), BF16, row_parts(rows, ("cx", "cx"), (1, 1)))

    inputs = [
        grad_branch, grad_middle, query_rot, heads_out, key_value, log_total, own_segs, key_segs,
        normed_all, unit_attn, rms_attn, gain_attn, gain_mlp_term, cosine, sine, wo, wq, wk, wv,
        query_adapt, out_expand, key_adapt, value_adapt, dg, du, dd,
    ]
    vmem, anywhere = pl.BlockSpec(memory_space=pltpu.VMEM), pl.BlockSpec(memory_space=pl.ANY)
    big = groups * n_seq > 32
    in_specs = [anywhere] + [vmem] * (len(inputs) - 4) + [anywhere] * 3
    if big:
        in_specs[4] = anywhere
    out_shape = [
        jax.ShapeDtypeStruct((rows, width), BF16),
        jax.ShapeDtypeStruct((d_rows + r_rows, head_cols), F32),
        jax.ShapeDtypeStruct((d_rows + r_rows, head_cols), F32),
        jax.ShapeDtypeStruct((kv_rows, 2 * HD), F32),
    ] + [op.outputs[0] for op in swaps]
    out_specs = [vmem] * 4 + [anywhere] * 3
    if big:
        sum_kv = SlimScatter(topo, "all", kv_shape, BF16, row_parts(rows, ("cxblh", "cblxh"), (1, 1)))
        out_shape = out_shape + [jax.ShapeDtypeStruct(kv_shape, BF16)] + sum_kv.outputs
        out_specs = out_specs + [anywhere] + sum_kv.out_specs
    scratch = [
        pltpu.VMEM((groups, rows, width), BF16),
        pltpu.VMEM((tokens, head_cols), BF16),
        pltpu.VMEM((tokens, head_cols), BF16),
        pltpu.VMEM(w_shape, BF16),
        pltpu.VMEM(w_shape, BF16),
        pltpu.VMEM((n_seq, kv_rows, 2 * HD), BF16),
        pltpu.VMEM((length, 2 * HD) if big else kv_shape, BF16),
        pltpu.VMEM((groups, rows, width), BF16),
        pltpu.VMEM((rows, 2 * HD), F32),
        pltpu.VMEM((rows, width), F32),
        pltpu.VMEM((rows, 2 * HD), BF16),
        pltpu.VMEM((groups, rows, 2 * HD), BF16),
        pltpu.SemaphoreType.DMA((n_seq,)),
    ]
    n_own = len(scratch)
    shared = sum_kv.shared_scratch() + [pltpu.VMEM((length, 2 * HD), BF16)] if big else []
    scratch = scratch + shared
    ops = [gather_g, gather_kv] + swaps + [sum_o, sum_q, sum_k, sum_kv, sum_n]
    for op in ops:
        scratch = scratch + op.scratch

    def kernel(*refs):
        refs = list(refs)
        (
            gb_hbm, gmid, qrot, hout, kv, lse, own_seg, key_seg, norm_all, unit, rms, gain, gain_term, cos, sin,
            wo_r, wq_r, wk_r, wv_r, qa, oe, ka, va, dg_r, du_r, dd_r,
        ) = [refs.pop(0) for _ in inputs]
        grad_rows, so_out, sq_out, sk_out, dg_o, du_o, dd_o = [refs.pop(0) for _ in range(7)]
        kv_outs = [refs.pop(0) for _ in out_shape[7:]]
        (
            ga, gh, gq, xo, xq, xk, xkv, xn, kv_sum, n_sum, gkv, gkv_all, load_sem,
        ) = [refs.pop(0) for _ in range(n_own)]
        shared_refs = [refs.pop(0) for _ in shared]
        op_scratch = [[refs.pop(0) for _ in op.scratch] for op in ops]
        dp = lax.axis_index("dp")
        at = greet(topo, ops)
        get_g = Steps(gather_g.steps(at, [gb_hbm], [ga], op_scratch[0]))
        get_g.run()
        moves = [
            Steps(op.steps(at, [r], [o], sc))
            for op, r, o, sc in zip(swaps, (dg_r, du_r, dd_r), (dg_o, du_o, dd_o), op_scratch[2:5])
        ]
        moves[0].run()
        get_g.finish()
        flat = lambda ref: ref[...].reshape(tokens, ref.shape[-1])

        gh[...] = dot_t(flat(ga), wo_r[...]).astype(BF16)

        for j in range(n_seq):
            part = t_dot(ga[:, :, j * d_rows : (j + 1) * d_rows].reshape(tokens, d_rows), hout[...])
            xo[j, :d_rows, :] = part.astype(BF16)
        low = dot_t(flat(ga), oe[...]).astype(BF16)
        part = t_dot(low, hout[...]).astype(BF16)
        for j in range(n_seq):
            xo[j, d_rows:, :] = part[j * r_rows : (j + 1) * r_rows, :]
        get_o = Steps(sum_o.steps(at, xo, so_out, op_scratch[5]))
        get_o.run()

        seq = lax.axis_index("seq")
        key_at = lax.broadcasted_iota(jnp.int32, (heads * rows, length), 1)
        row_at = lax.broadcasted_iota(jnp.int32, (heads * rows, length), 0)
        causal = key_at <= seq * rows + lax.rem(row_at, rows)
        for s in range(groups):
            r = slice(s * rows, (s + 1) * rows)
            stack = lambda ref: jnp.concatenate([ref[r, h * HD : (h + 1) * HD] for h in range(heads)], axis=0)
            q, d_o = stack(qrot), stack(gh)
            if big:
                one = shared_refs[3]
                cp = pltpu.make_async_copy(kv.at[pl.ds(s * length, length)], one, load_sem.at[0])
                cp.start()
                cp.wait()
            else:
                one = kv.at[pl.ds(s * length, length)]
            keys, values = one[:, :HD], one[:, HD:]
            mine = jnp.concatenate([own_seg[:, s : s + 1]] * heads, axis=0)
            allowed = causal & (mine == key_seg[s : s + 1, :])
            scores = jnp.where(allowed, dot_t(q, keys) * scale, MASKED)
            probs = jnp.exp(scores - lse[s])
            grad_probs = dot_t(d_o, values)
            delta = jnp.sum(probs * grad_probs, axis=-1, keepdims=True)
            grad_scores = (probs * (grad_probs - delta)).astype(BF16)
            d_q = matmul(grad_scores, keys) * scale
            d_k = (t_dot(grad_scores, q) * scale).astype(BF16)
            d_v = t_dot(probs.astype(BF16), d_o).astype(BF16)
            both = jnp.concatenate([d_k, d_v], axis=1)
            if big:
                xkv[...] = both
                copies = [
                    pltpu.make_async_copy(
                        xkv.at[pl.ds(j * rows, rows)], kv_outs[0].at[s * n_seq + j], load_sem.at[j]
                    )
                    for j in range(n_seq)
                ]
                for cp in copies:
                    cp.start()
                for cp in copies:
                    cp.wait()
            else:
                xkv[s * n_seq : (s + 1) * n_seq] = both.reshape(n_seq, rows, 2 * HD)
            for h in range(heads):
                gq[r, h * HD : (h + 1) * HD] = rotate(
                    d_q[h * rows : (h + 1) * rows], cos[...], -sin[...]
                ).astype(BF16)
            if s + 2 >= groups:
                get_o.run(4 if s + 2 == groups else 2)
        if big:
            get_kv = Steps(sum_kv.steps(at, kv_outs[0], kv_outs[1:], op_scratch[8], shared_refs[:3]))
        else:
            get_kv = Steps(sum_kv.steps(at, xkv, kv_sum, op_scratch[8]))
        get_kv.run()
        moves[1].run()
        for s in range(groups):
            xn[s] = dot_t(gq[s * rows : (s + 1) * rows, :], wq_r[...]).astype(BF16)
        get_n = Steps(sum_n.steps(at, xn, n_sum, op_scratch[9]))
        get_n.run()

        def poll():
            get_kv.run(1)

        for j in range(n_seq):
            part = t_dot(norm_all[:, :, j * d_rows : (j + 1) * d_rows].reshape(tokens, d_rows), gq[...])
            xq[j, :d_rows, :] = part.astype(BF16)
            poll()
        low = matmul(flat(norm_all), qa[...]).astype(BF16)
        part = t_dot(low, gq[...]).astype(BF16)
        for j in range(n_seq):
            xq[j, d_rows:, :] = part[j * r_rows : (j + 1) * r_rows, :]
        get_q = Steps(sum_q.steps(at, xq, sq_out, op_scratch[6]))
        get_q.run()
        get_n.run(2)
        while get_kv.todo:
            get_kv.run(KV_STEPS)
            get_o.run()
        get_n.finish()
        moves[2].run()

        total_kv = kv_outs[1] if big else kv_sum
        gk = rotate(total_kv[:, :HD], cos[...], -sin[...]).astype(BF16)
        gv = total_kv[:, HD:].astype(BF16)
        gkv[:, :HD] = gk
        gkv[:, HD:] = gv
        get_kv2 = Steps(gather_kv.steps(at, [gkv], [gkv_all], op_scratch[1]))
        get_kv2.run()
        grad_normed = n_sum[...] + dot_t(gk, wk_r[...]) + dot_t(gv, wv_r[...])
        u_rows = unit[...]
        gain_attn_term = jnp.sum(grad_normed * u_rows, axis=0, keepdims=True)
        grad_unit = grad_normed * gain[...]
        inner = jnp.mean(grad_unit * u_rows, axis=-1, keepdims=True)
        get_o.run(2)
        get_q.run(2)
        grad_rows[...] = (gmid[...] + rms[...] * (grad_unit - u_rows * inner)).astype(BF16)
        get_kv2.finish()
        get_q.run(2)
        mine = pl.ds(pl.multiple_of(dp * share_d, share_d), share_d)
        part_rows = norm_all[:, :, mine].reshape(tokens, share_d)
        low_k = matmul(flat(norm_all), ka[...]).astype(BF16)
        low_v = matmul(flat(norm_all), va[...]).astype(BF16)
        g_rows = flat(gkv_all)
        part = t_dot(part_rows, g_rows).astype(BF16)
        low = jnp.concatenate(
            [t_dot(low_k, g_rows[:, :HD]), t_dot(low_v, g_rows[:, HD:])], axis=1
        )
        zero_r = jnp.zeros((kv_pad - kv_r, 2 * HD), F32)
        terms = jnp.concatenate([gain_attn_term, gain_term[...], jnp.zeros((14, width), F32)], axis=0)
        zero_c = jnp.zeros((16, 2 * HD - d_rows), F32)
        for j in range(n_seq):
            xk[j, :kv_d, :] = part[j * kv_d : (j + 1) * kv_d, :]
            xk[j, kv_d : kv_d + kv_pad, :] = jnp.concatenate(
                [low[j * kv_r : (j + 1) * kv_r, :], zero_r], axis=0
            ).astype(BF16)
            xk[j, kv_d + kv_pad :, :] = jnp.concatenate(
                [terms[:, j * d_rows : (j + 1) * d_rows], zero_c], axis=1
            ).astype(BF16)
        get_k = Steps(sum_k.steps(at, xk, sk_out, op_scratch[7]))
        get_k.run()
        left = [get_o, get_q, get_k]
        while any(g.todo for g in left):
            for g in left:
                g.run()
        for move in moves:
            move.finish()

    results = pl.pallas_call(
        kernel,
        name="attention_back",
        out_shape=out_shape,
        in_specs=in_specs,
        out_specs=out_specs,
        scratch_shapes=scratch,
        compiler_params=pltpu.CompilerParams(
            collective_id=collective_id, has_side_effects=True, vmem_limit_bytes=60 << 20
        ),
    )(*inputs)
    return results[:7]


def unfold(d_rows, member, owns, dg, du, dd, gate_expand, up_expand, down_adapt):
    quad, total, units = dg.shape
    rank = gate_expand.shape[0]
    r_rows = total - d_rows

    def kernel(
        me, dg_own, du_own, dd_own, dg_ref, du_ref, dd_ref, ge_ref, ue_ref, da_ref,
        wg, eg, wu, eu, wd, ad, ga, ua, de, term_g, term_u, term_d,
    ):
        first = pl.program_id(0) == 0
        mine = pl.program_id(0) == me[0]
        for own, got, term in ((dg_own, dg_ref, term_g), (du_own, du_ref, term_u), (dd_own, dd_ref, term_d)):
            term[...] = jnp.where(mine, own[0], got[0])
        for src, w, e in ((term_g, wg, eg), (term_u, wu, eu)):
            w[...] = src[:d_rows, :].astype(F32)
            e[...] = src[d_rows:, :].astype(F32)
        both = term_d[...].astype(F32).T
        wd[...] = both[:, :d_rows]
        ad[...] = both[:, d_rows:]
        for out, term in (
            (ga, dot_t(term_g[:d_rows, :], ge_ref[...])),
            (ua, dot_t(term_u[:d_rows, :], ue_ref[...])),
            (de, matmul(term_d[:d_rows, :], da_ref[...])),
        ):
            out[...] = jnp.where(first, term, term + out[...])

    cols = lambda n: pl.BlockSpec((n, units), lambda q, me: (0, q))
    side = lambda n: pl.BlockSpec((units, n), lambda q, me: (q, 0))
    block = pl.BlockSpec((1, total, units), lambda q, me: (q, 0, 0))
    own = pl.BlockSpec((1, total, units), lambda q, me: (me[0], 0, 0))
    kept = pl.BlockSpec((d_rows, rank), lambda q, me: (0, 0))
    shape = lambda *s: jax.ShapeDtypeStruct(s, F32)
    all_units = quad * units
    return pl.pallas_call(
        kernel,
        name="unfold",
        grid_spec=pltpu.PrefetchScalarGridSpec(
            num_scalar_prefetch=1,
            grid=(quad,),
            in_specs=[own] * 3 + [block] * 3 + [cols(rank), cols(rank), side(rank)],
            out_specs=[cols(d_rows), cols(r_rows), cols(d_rows), cols(r_rows), side(d_rows), side(r_rows)] + [kept] * 3,
            scratch_shapes=[pltpu.VMEM((total, units), BF16)] * 3,
        ),
        out_shape=[
            shape(d_rows, all_units), shape(r_rows, all_units), shape(d_rows, all_units), shape(r_rows, all_units),
            shape(all_units, d_rows), shape(all_units, r_rows),
        ] + [shape(d_rows, rank)] * 3,
        compiler_params=pltpu.CompilerParams(vmem_limit_bytes=56 << 20),
    )(member, *owns, dg, du, dd, gate_expand, up_expand, down_adapt)


def finish_small(topo, collective_id, small, n_moved, per_seq):
    rows, rank = small.shape[1:]
    n_seq = topo.n_seq
    sums = VScatter(topo, "dp", small.shape, small.dtype, [(0, rows, "cx")])
    moved = jax.ShapeDtypeStruct((n_moved, rank), F32)
    spread = jax.ShapeDtypeStruct((n_seq, 2 * per_seq, rank), F32)
    last = Finish(topo, moved, spread)
    scratch = [pltpu.VMEM((rows, rank), F32), pltpu.VMEM(moved.shape, F32), pltpu.VMEM(spread.shape, F32)]

    def kernel(x_ref, moved_out, spread_out, total, moved_in, spread_in, *refs):
        at = greet(topo, [sums, last])
        Steps(sums.steps(at, x_ref, total, refs[: len(sums.scratch)])).finish()
        moved_in[...] = total[:n_moved, :]
        for j in range(n_seq):
            for k in range(2):
                first = n_moved + (k * n_seq + j) * per_seq
                spread_in[j, k * per_seq : (k + 1) * per_seq, :] = total[first : first + per_seq, :]
        refs = refs[len(sums.scratch) :]
        Steps(last.steps(at, [moved_in, spread_in], [moved_out, spread_out], refs)).finish()

    return pl.pallas_call(
        kernel,
        name="finish_small",
        out_shape=[moved, spread],
        in_specs=[pl.BlockSpec(memory_space=pltpu.VMEM)],
        out_specs=[pl.BlockSpec(memory_space=pl.ANY)] * 2,
        scratch_shapes=scratch + sums.scratch + last.scratch,
        compiler_params=pltpu.CompilerParams(
            collective_id=collective_id, has_side_effects=True, vmem_limit_bytes=32 << 20
        ),
    )(small)


def local(
    topo,
    tokens, segment_ids, out_grad, gain_attn, gain_mlp, w_query, w_key, w_value, w_out, w_gate, w_up, w_down,
    query_adapt, query_expand, key_adapt, key_expand, value_adapt, value_expand, out_adapt, out_expand,
    gate_adapt, gate_expand, up_adapt, up_expand, down_adapt, down_expand,
):
    rows, width = tokens.shape[2], tokens.shape[3]
    groups, n_seq = topo.n_dp, topo.n_seq
    length = rows * n_seq
    heads_dev = w_query.shape[1] // HD
    head_cols = heads_dev * HD
    rank = query_adapt.shape[1]
    scale_qk = HD ** (-0.5)
    quad = topo.group_size("quad")
    units = w_gate.shape[1] // quad
    seq = lax.axis_index("seq")
    dp = lax.axis_index("dp")

    def merged(weight, adapt, expand):
        return (weight.astype(F32) + matmul(adapt, expand)).astype(BF16)

    wq = merged(w_query, query_adapt, query_expand)
    wk = merged(w_key, key_adapt, key_expand)
    wv = merged(w_value, value_adapt, value_expand)
    wo = merged(w_out, out_adapt, out_expand)
    token_rows = tokens[0, 0].astype(F32)
    grad_rows_in = out_grad[0, 0]
    normed, unit_attn, rms_attn = normalize(token_rows, gain_attn)
    normed_attn = normed.astype(BF16)
    positions = seq * rows + jnp.arange(rows, dtype=jnp.int32)
    cosine_table, sine_table = rotary(positions, HD)
    cosine_heads, sine_heads = cosine_table[:, None, :], sine_table[:, None, :]
    key_rot = rotate(matmul(normed_attn, wk), cosine_table, sine_table).astype(BF16)
    value_rows = matmul(normed_attn, wv).astype(BF16)
    key_value = jnp.concatenate([key_rot, value_rows], axis=1)
    seg_rows = jnp.zeros((16, rows), F32).at[0].set(segment_ids[0, 0].astype(F32))

    zyx, xzy = "lhbxc", "xlhbc"
    (normed_all,), (kv_all,), (seg_all,) = communicate(
        topo, "gather_attention", 0,
        Gather(topo, "dp", normed_attn, row_parts(rows, ("xc", "xc"), (1, 1))),
        Gather(topo, "all", key_value, row_parts(rows, (zyx, xzy), (7, 4))),
        Gather(topo, "all", seg_rows, [(0, 16, zyx)]),
    )
    kv_all = kv_all.reshape(groups, length, 2 * HD)
    keys_all, values_all = kv_all[..., :HD], kv_all[..., HD:]
    segments = seg_all[:, 0, :].reshape(groups, length)
    own_segments = lax.dynamic_slice_in_dim(segments, seq * rows, rows, 1)
    key_positions = jnp.arange(length, dtype=jnp.int32)
    causal = (key_positions[None, :] <= positions[:, None])[None, :, :]
    allowed = (causal & (own_segments[:, :, None] == segments[:, None, :]))[:, None, :, :]

    queries = matmul(normed_all.reshape(groups * rows, width), wq)
    query_rot = rotate(queries.reshape(groups, rows, heads_dev, HD), cosine_heads, sine_heads).astype(BF16)
    scores = jnp.where(allowed, contract("sthd,sjd->shtj", query_rot, keys_all) * scale_qk, MASKED)
    row_top = jnp.max(scores, axis=-1, keepdims=True)
    log_total = row_top + jnp.log(jnp.sum(jnp.exp(scores - row_top), axis=-1, keepdims=True))
    prob_low = jnp.exp(scores - log_total).astype(BF16)
    heads_out = (
        contract("shtj,sjd->sthd", prob_low, values_all).reshape(groups * rows, head_cols).astype(BF16)
    )
    out_part = matmul(heads_out, wo).astype(BF16).reshape(groups, rows, width)
    (out_sum,), (grad_half,) = communicate(
        topo, "sum_attention", 1,
        Scatter(topo, "dp", out_part, row_parts(rows, ("cx", "cx"), (1, 1))),
        Gather(topo, "half", grad_rows_in, row_parts(rows, ("xlbc", "lbxc", "bxlc"), (1, 1, 1))),
    )
    middle = token_rows + out_sum
    normed, unit_mlp, rms_mlp = normalize(middle, gain_mlp)
    normed_mlp = normed.astype(BF16)
    down_sum, gn_sum, dg, du, dd = feed_forward(
        topo, 2, normed_mlp, grad_rows_in, grad_half,
        w_gate, w_up, w_down, gate_adapt, gate_expand, up_adapt, up_expand, down_adapt, down_expand,
    )
    result_rows = (middle + down_sum).astype(BF16)
    gain_mlp_term, grad_from_mlp = norm_backward(gn_sum, unit_mlp, rms_mlp, gain_mlp)
    grad_middle = grad_rows_in.astype(F32) + grad_from_mlp
    grad_branch_attn = grad_middle.astype(BF16)
    my_kv_ranks = lambda a: lax.dynamic_slice_in_dim(a, dp * (rank // groups), rank // groups, 1)
    owns = (dg, du, dd)
    grad_rows, so, sq, sk, dg, du, dd = attention_back(
        topo, 4, grad_branch_attn, grad_middle,
        query_rot.reshape(groups * rows, head_cols), heads_out, kv_all.reshape(groups * length, 2 * HD),
        log_total.reshape(groups, heads_dev * rows, 1), own_segments.T, segments,
        normed_all, unit_attn, rms_attn, gain_attn[None], gain_mlp_term[None], cosine_table, sine_table,
        wo, wq, wk, wv, query_adapt, out_expand, my_kv_ranks(key_adapt), my_kv_ranks(value_adapt), dg, du, dd,
    )
    d_rows, r_rows = width // n_seq, rank // n_seq
    per_dev_d, per_dev_r = d_rows // groups, r_rows // groups
    kv_pad = -(-per_dev_r // 16) * 16
    grad_wg, grad_ge, grad_wu, grad_ue, grad_wd, grad_da, part_ga, part_ua, part_de = unfold(
        d_rows, lax.rem(seq, topo.group_size("quad")).reshape(1), owns, dg, du, dd, gate_expand, up_expand, down_adapt
    )
    grad_wq, grad_qe = sq[:d_rows], sq[d_rows:]
    grad_wo, grad_oa = so[:d_rows].T, so[d_rows:].T
    grad_wkv, grad_kve = sk[:per_dev_d], sk[per_dev_d : per_dev_d + per_dev_r]
    gains = jnp.pad(sk[per_dev_d + kv_pad : per_dev_d + kv_pad + 2, :d_rows], ((0, 6), (0, 0)))

    adapt = jnp.stack(
        [
            part_ga,
            part_ua,
            dot_t(grad_wq.astype(BF16), query_expand),
        ]
    )
    expand = jnp.stack(
        [
            part_de.T,
            matmul(so[:d_rows].astype(BF16), out_adapt).T,
        ]
    )
    adapt = adapt.reshape(3, groups, per_dev_d, rank).transpose(1, 0, 2, 3).reshape(groups, -1, rank)
    expand = expand.reshape(2, groups, rank // groups, d_rows).transpose(1, 0, 2, 3).reshape(groups, -1, d_rows)
    expand = jnp.pad(expand, ((0, 0), (0, 0), (0, rank - d_rows)))
    small_gains = jnp.pad(
        gains[:, :d_rows].reshape(8, groups, per_dev_d).transpose(1, 0, 2), ((0, 0), (0, 8), (0, rank - per_dev_d))
    )
    small = jnp.concatenate([adapt, small_gains, expand], axis=1).astype(BF16)
    n_adapt = 3 * per_dev_d
    per_seq = rank // groups // n_seq
    own_adapt, own_expand = finish_small(topo, 8, small, n_adapt + 16, per_seq)
    grad_ga, grad_ua, grad_qa = own_adapt[:n_adapt].reshape(3, per_dev_d, rank)
    grad_gain_attn = own_adapt[n_adapt, :per_dev_d]
    grad_gain_mlp = own_adapt[n_adapt + 1, :per_dev_d]
    own_expand = own_expand[..., :d_rows].reshape(n_seq, 2, per_seq, d_rows).transpose(1, 2, 0, 3).reshape(2, per_seq, width)
    grad_de, grad_oe = own_expand[0], own_expand[1]
    grad_wk, grad_wv = grad_wkv[:, :HD], grad_wkv[:, HD:]
    grad_ka = dot_t(grad_wk.astype(BF16), key_expand)
    grad_va = dot_t(grad_wv.astype(BF16), value_expand)
    grad_ke, grad_ve = grad_kve[:, :HD], grad_kve[:, HD:]
    return (
        result_rows[None, None], grad_rows[None, None],
        grad_gain_attn, grad_gain_mlp,
        grad_wq, grad_wk, grad_wv, grad_wo, grad_wg, grad_wu, grad_wd,
        grad_qa, grad_qe, grad_ka, grad_ke, grad_va, grad_ve, grad_oa, grad_oe,
        grad_ga, grad_ge, grad_ua, grad_ue, grad_da, grad_de,
    )


def solution(mesh):
    topo = Topo(mesh.shape["dp"], mesh.shape["seq"])
    both = ("dp", "seq")
    in_specs = (
        P(None, "dp", "seq", None), P(None, "dp", "seq"), P(None, "dp", "seq", None),
        P(), P(), P(None, "dp"), P(), P(), P("dp", None), P(None, "dp"), P(None, "dp"), P("dp", None),
        P(), P(None, "dp"), P(), P(), P(), P(), P("dp", None), P(),
        P(), P(None, "dp"), P(), P(None, "dp"), P("dp", None), P(),
    )
    out_specs = (
        P(None, "dp", "seq", None), P(None, "dp", "seq", None), P(both), P(both),
        P("seq", "dp"), P(both, None), P(both, None), P("dp", "seq"), P("seq", "dp"), P("seq", "dp"), P("dp", "seq"),
        P(both, None), P("seq", "dp"), P(both, None), P(both, None), P(both, None), P(both, None),
        P("dp", "seq"), P(both, None), P(both, None), P("seq", "dp"), P(both, None), P("seq", "dp"),
        P("dp", "seq"), P(both, None),
    )
    return jax.shard_map(
        lambda *args: local(topo, *args), mesh=mesh, in_specs=in_specs, out_specs=out_specs, check_vma=False
    )
```

```python
import itertools
import math

import jax
import jax.numpy as jnp
from jax import lax
from jax.experimental import pallas as pl
from jax.experimental.pallas import tpu as pltpu
from jax.sharding import PartitionSpec as P

HD = 256
EPSILON = 1e-06
ROTARY_BASE = 10000.0
MASKED = -1e30

MESH = pl.DeviceIdType.MESH
BF16 = jnp.bfloat16
F32 = jnp.float32


class Topo:
    def __init__(self, n_dp, n_seq):
        self.n_dp, self.n_seq = n_dp, n_seq
        self.size = {"c": 2, "x": n_dp // 2, "b": n_seq // 4, "l": 2, "h": 2}

    def here(self):
        dp, seq = lax.axis_index("dp"), lax.axis_index("seq")
        nb = self.size["b"]
        outer = lax.div(seq, nb)
        return {
            "c": lax.rem(dp, 2),
            "x": lax.div(dp, 2),
            "b": lax.rem(seq, nb),
            "l": lax.rem(outer, 2),
            "h": lax.div(outer, 2),
        }

    def moved(self, at, dims, offsets, sign=1):
        new = dict(at)
        for dim, offset in zip(dims, offsets):
            n = self.size[dim]
            if not (isinstance(offset, int) and offset == 0):
                new[dim] = lax.rem(at[dim] + (offset if sign > 0 else n - offset), n)
        return new

    def seq_of(self, at):
        return (at["h"] * 2 + at["l"]) * self.size["b"] + at["b"]

    def device(self, at):
        return (at["x"] * 2 + at["c"], self.seq_of(at))

    def index(self, at, group):
        dp, seq = self.device(at)
        if group == "all":
            return dp * self.n_seq + seq
        if group == "half":
            nb = self.size["b"]
            return dp * (2 * nb) + at["l"] * nb + at["b"]
        if group == "dp":
            return dp
        if group == "seq":
            return seq
        if group == "quad":
            return at["l"] * self.size["b"] + at["b"]
        raise ValueError(group)

    def group_size(self, group):
        nb = self.size["b"]
        return {
            "all": self.n_dp * self.n_seq,
            "half": self.n_dp * 2 * nb,
            "dp": self.n_dp,
            "seq": self.n_seq,
            "quad": 2 * nb,
        }[group]


GROUP_DIMS = {"all": "cxblh", "half": "cxbl", "dp": "cx", "seq": "blh", "quad": "bl"}


def remote(src, dst, send_sem, recv_sem, device):
    return pltpu.make_async_remote_copy(
        src_ref=src,
        dst_ref=dst,
        send_sem=send_sem,
        recv_sem=recv_sem,
        device_id=device,
        device_id_type=MESH,
    )


def peers_of(topo, group):
    return {((dim, d),) for dim in GROUP_DIMS[group] for d in range(1, topo.size[dim])}


def digits(key, sizes):
    k = 0
    for o, s in zip(key, sizes):
        k = k * s + o
    return k


def arrived(topo, at, ref, send_sem, recv_sem):
    remote(ref, ref, send_sem, recv_sem, topo.device(at)).wait_recv()


class Gather:
    def __init__(self, topo, group, x, parts, beyond=None, need=None, keep=True):
        self.topo, self.group, self.parts, self.beyond = topo, group, parts, beyond
        self.keep = keep and not beyond
        self.slots = "half" if beyond else group
        self.need = need or (lambda dims, key: 0)
        self.inputs = [x]
        rows, cols = x.shape
        n = topo.group_size(group)
        self.outputs = [jax.ShapeDtypeStruct((topo.group_size(self.slots), rows, cols), x.dtype)]
        self.in_specs = [pl.BlockSpec(memory_space=pltpu.VMEM)]
        self.out_specs = [pl.BlockSpec(memory_space=pl.ANY)]
        self.scratch = [
            pltpu.SemaphoreType.DMA((len(parts), n)),
            pltpu.SemaphoreType.DMA((len(parts), n)),
            pltpu.SemaphoreType.DMA(()),
        ]

    def peers(self):
        return peers_of(self.topo, self.group)

    def keeps(self, order, key):
        return not self.beyond or key[order.index(self.beyond)] != 0

    def work(self):
        work = []
        for part, (row, rows, order) in enumerate(self.parts):
            for key in itertools.product(*[range(self.topo.size[dim]) for dim in order]):
                if not any(key) or self.keeps(order, key):
                    hops = sum(1 for o in key if o)
                    last = max([i for i, o in enumerate(key) if o], default=-1)
                    work.append((hops, self.need(order, key), last, part, key))
        work.sort()
        return [(w[3], w[4]) for w in work]

    def steps(self, at, ins, outs, scratch):
        topo = self.topo
        (x_ref,), (out_ref,) = ins, outs
        send_sem, recv_sem, own_sem = scratch
        size_of = lambda order: [topo.size[dim] for dim in order]

        def copy(part, key, stage, d):
            row, rows, order = self.parts[part]
            slot = topo.index(topo.moved(at, order, key, -1), self.slots)
            new_key = tuple(d if i == stage else o for i, o in enumerate(key))
            place = out_ref.at[slot, pl.ds(row, rows)]
            k = digits(new_key, size_of(order))
            target = topo.device(topo.moved(at, [order[stage]], [d]))
            source = place if any(key) else x_ref.at[pl.ds(row, rows)]
            return remote(source, place, send_sem.at[part, k], recv_sem.at[part, k], target)

        def own():
            return pltpu.make_async_copy(x_ref, out_ref.at[topo.index(at, self.slots)], own_sem)

        sent, steps = [], []
        for n, (part, key) in enumerate(self.work()):
            row, rows, order = self.parts[part]
            last = max([i for i, o in enumerate(key) if o], default=-1)
            sends = []
            for stage in range(last + 1, len(order)):
                for d in range(1, topo.size[order[stage]]):
                    new_key = tuple(d if i == stage else o for i, o in enumerate(key))
                    if self.keeps(order, new_key):
                        sends.append((self.need(order, new_key), stage, d))
            sends = [(part, key, stage, d) for _, stage, d in sorted(sends)]
            sent += sends

            def step(n=n, part=part, key=key, sends=sends):
                row, rows, order = self.parts[part]
                if n == 0 and self.keep:
                    own().start()
                if any(key):
                    slot = topo.index(topo.moved(at, order, key, -1), self.slots)
                    k = digits(key, size_of(order))
                    arrived(topo, at, out_ref.at[slot, pl.ds(row, rows)], send_sem.at[part, k], recv_sem.at[part, k])
                for send in sends:
                    copy(*send).start()

            steps.append(step)

        def end():
            for send in sent:
                copy(*send).wait_send()
            if self.keep:
                own().wait()

        return steps, [end]


TILE = 512


class Reduce:
    def __init__(self, topo, group, shape, dtype, parts):
        self.topo, self.group, self.parts, self.dtype = topo, group, parts, dtype
        n, rows, cols = shape
        assert n == topo.group_size(group), (n, group)
        self.tile = math.gcd(cols, TILE)

    def peers(self):
        return peers_of(self.topo, self.group)

    def stages(self, part):
        sizes = self.sizes(part)
        return [(max(s - 1, 1), math.prod(sizes[k + 1 :])) for k, s in enumerate(sizes)]

    def sizes(self, part):
        return [self.topo.size[dim] for dim in self.parts[part][2]]

    def jobs(self):
        jobs = []
        for part in range(len(self.parts)):
            sizes = self.sizes(part)
            keys = list(itertools.product(*[range(s) for s in sizes]))
            first = {k: min([i for i, o in enumerate(k) if o], default=len(sizes)) for k in keys}
            keys.sort(key=lambda k: (first[k], [0 if o else 1 for o in k]))
            jobs += [(first[key], rank, part, key) for rank, key in enumerate(keys)]
        jobs.sort()
        return [(first, part, key) for first, _, part, key in jobs]

    def block(self, at, part, key):
        return self.topo.index(self.topo.moved(at, self.parts[part][2], key), self.group)

    def target(self, at, part, key, stage):
        return self.topo.device(self.topo.moved(at, [self.parts[part][2][stage]], [key[stage]]))

    def place(self, part, key, stage):
        return key[stage] - 1, digits(key[stage + 1 :], self.sizes(part)[stage + 1 :])

    def terms(self, part, key, first):
        sizes = self.sizes(part)
        return [
            (stage, d - 1, digits(key[stage + 1 :], sizes[stage + 1 :]))
            for stage in range(first)
            for d in range(1, sizes[stage])
        ]


class VScatter(Reduce):
    def __init__(self, topo, group, shape, dtype, parts):
        super().__init__(topo, group, shape, dtype, parts)
        self.scratch = []
        for part, (row, nrows, order) in enumerate(parts):
            self.scratch.append(pltpu.VMEM((math.prod(self.sizes(part)[1:]), nrows, shape[2]), dtype))
            for m, rest in self.stages(part):
                self.scratch.append(pltpu.VMEM((m, rest, nrows, shape[2]), dtype))
                self.scratch.append(pltpu.SemaphoreType.DMA((m, rest)))
                self.scratch.append(pltpu.SemaphoreType.DMA((m, rest)))

    def steps(self, at, x_ref, out_ref, scratch):
        topo, tile = self.topo, self.tile
        scratch = list(scratch)
        bufs = []
        for part in range(len(self.parts)):
            acc = scratch.pop(0)
            bufs.append((acc, [tuple(scratch.pop(0) for _ in range(3)) for _ in self.sizes(part)]))
        jobs = self.jobs()

        def send(first, part, key):
            row, nrows, order = self.parts[part]
            acc, stages = bufs[part]
            buf, send_sem, recv_sem = stages[first]
            d, k = self.place(part, key, first)
            if first == 0:
                source = x_ref.at[self.block(at, part, key), pl.ds(row, nrows)]
            else:
                source = acc.at[digits(key[1:], self.sizes(part)[1:])]
            return remote(
                source, buf.at[d, k], send_sem.at[d, k], recv_sem.at[d, k], self.target(at, part, key, first)
            )

        def start():
            for job in jobs:
                if job[0] == 0:
                    send(*job).start()

        steps = [start]
        for job in jobs:
            if job[0] == 0:
                continue

            def step(job=job):
                first, part, key = job
                row, nrows, order = self.parts[part]
                acc, stages = bufs[part]
                terms = self.terms(part, key, first)
                for stage, d, k in terms:
                    buf, send_sem, recv_sem = stages[stage]
                    arrived(topo, at, buf.at[d, k], send_sem.at[d, k], recv_sem.at[d, k])
                block, kk = self.block(at, part, key), digits(key[1:], self.sizes(part)[1:])
                final = first == len(order)

                tiles = x_ref.shape[-1] // tile

                def add(n, _):
                    r0 = pl.multiple_of(lax.div(n, tiles) * 16, 16)
                    cols = pl.ds(pl.multiple_of(lax.rem(n, tiles) * tile, tile), tile)
                    r1 = pl.ds(pl.multiple_of(row + r0, 16), 16)
                    total = x_ref[block, r1, cols].astype(F32)
                    for stage, d, k in terms:
                        total = total + stages[stage][0][d, k, pl.ds(r0, 16), cols].astype(F32)
                    if final:
                        out_ref[r1, cols] = total.astype(out_ref.dtype)
                    else:
                        acc[kk, pl.ds(r0, 16), cols] = total.astype(acc.dtype)
                    return 0

                lax.fori_loop(0, nrows // 16 * tiles, add, 0)
                if not final:
                    send(*job).start()

            steps.append(step)

        def end():
            for job in jobs:
                if job[0] < len(self.parts[job[1]][2]):
                    send(*job).wait_send()

        return steps, [end]


class SlimScatter(Reduce):
    RING = 4

    def __init__(self, topo, group, shape, dtype, parts):
        super().__init__(topo, group, shape, dtype, parts)
        rows, cols = shape[1:]
        self.outputs = [jax.ShapeDtypeStruct((rows, cols), F32)]
        self.out_specs = [pl.BlockSpec(memory_space=pltpu.VMEM)]
        self.scratch = []
        self.most, self.cols = max(p[1] for p in parts), cols
        self.count = 1 + sum(topo.size[d] - 1 for d in GROUP_DIMS[group])
        for part, (row, nrows, order) in enumerate(parts):
            for m, rest in self.stages(part):
                self.outputs.append(jax.ShapeDtypeStruct((m, rest, nrows, cols), dtype))
                self.out_specs.append(pl.BlockSpec(memory_space=pl.ANY))
                self.scratch.append(pltpu.SemaphoreType.DMA((m, rest)))
                self.scratch.append(pltpu.SemaphoreType.DMA((m, rest)))

    def shared_scratch(self):
        return [
            pltpu.VMEM((2, self.count, self.most, self.cols), self.dtype),
            pltpu.SemaphoreType.DMA((2, self.count)),
            pltpu.VMEM((self.RING, self.most, self.cols), self.dtype),
        ]

    def steps(self, at, x_ref, outs, scratch, shared):
        topo, tile = self.topo, self.tile
        outs, scratch = list(outs), list(scratch)
        out_ref = outs.pop(0)
        stage_buf, stage_sem, ring = shared
        bufs = [
            [(outs.pop(0), scratch.pop(0), scratch.pop(0)) for _ in self.sizes(part)]
            for part in range(len(self.parts))
        ]
        jobs = self.jobs()
        later = [job for job in jobs if job[0] > 0]
        passed = [job for job in later if job[0] < len(self.parts[job[1]][2])]

        def own(part, key):
            row, nrows, order = self.parts[part]
            return x_ref.at[self.block(at, part, key), pl.ds(row, nrows)]

        def send(first, part, key, source=None):
            row, nrows, order = self.parts[part]
            buf, send_sem, recv_sem = bufs[part][first]
            d, k = self.place(part, key, first)
            if source is None:
                source = own(part, key) if first == 0 else ring.at[0, pl.ds(0, nrows)]
            return remote(
                source, buf.at[d, k], send_sem.at[d, k], recv_sem.at[d, k], self.target(at, part, key, first)
            )

        def loads(n):
            first, part, key = later[n]
            nrows = self.parts[part][1]
            sources = [own(part, key)] + [
                bufs[part][stage][0].at[d, k] for stage, d, k in self.terms(part, key, first)
            ]
            return [
                pltpu.make_async_copy(ref, stage_buf.at[n % 2, i, pl.ds(0, nrows)], stage_sem.at[n % 2, i])
                for i, ref in enumerate(sources)
            ]

        def fetch(n):
            first, part, key = later[n]
            for stage, d, k in self.terms(part, key, first):
                buf, send_sem, recv_sem = bufs[part][stage]
                arrived(topo, at, buf.at[d, k], send_sem.at[d, k], recv_sem.at[d, k])
            for cp in loads(n):
                cp.start()

        def start():
            for job in jobs:
                if job[0] == 0:
                    send(*job).start()

        steps = [start, lambda: fetch(0)]
        for n in range(len(later)):

            def step(n=n):
                first, part, key = later[n]
                row, nrows, order = self.parts[part]
                copies = loads(n)
                for cp in copies:
                    cp.wait()
                final = first == len(order)
                if not final:
                    sent = passed.index(later[n])
                    if sent >= self.RING:
                        send(*passed[sent - self.RING]).wait_send()

                tiles = self.cols // tile

                def add(n_tile, _):
                    r0 = pl.multiple_of(lax.div(n_tile, tiles) * 16, 16)
                    cols = pl.ds(pl.multiple_of(lax.rem(n_tile, tiles) * tile, tile), tile)
                    total = stage_buf[n % 2, 0, pl.ds(r0, 16), cols].astype(F32)
                    for i in range(1, len(copies)):
                        total = total + stage_buf[n % 2, i, pl.ds(r0, 16), cols].astype(F32)
                    if final:
                        out_ref[pl.ds(pl.multiple_of(row + r0, 16), 16), cols] = total
                    else:
                        ring[sent % self.RING, pl.ds(r0, 16), cols] = total.astype(ring.dtype)
                    return 0

                lax.fori_loop(0, nrows // 16 * tiles, add, 0)
                if not final:
                    send(first, part, key, ring.at[sent % self.RING, pl.ds(0, nrows)]).start()
                if n + 1 < len(later):
                    fetch(n + 1)

            steps.append(step)

        def end():
            for job in jobs:
                if job[0] == 0:
                    send(*job).wait_send()
            for job in passed[-self.RING :]:
                send(*job).wait_send()

        return steps, [end]


class Exchange:
    def __init__(self, topo, group, x, keep=True):
        self.topo, self.group, self.keep = topo, group, keep
        self.inputs = [x]
        n = x.shape[0]
        assert n == topo.group_size(group)
        self.outputs = [jax.ShapeDtypeStruct(x.shape, x.dtype)]
        self.in_specs = [pl.BlockSpec(memory_space=pl.ANY)]
        self.out_specs = [pl.BlockSpec(memory_space=pl.ANY)]
        self.scratch = [
            pltpu.SemaphoreType.DMA((n,)),
            pltpu.SemaphoreType.DMA((n,)),
            pltpu.SemaphoreType.DMA(()),
        ]

    def offsets(self):
        dims = GROUP_DIMS[self.group]
        return dims, [
            o for o in itertools.product(*[range(self.topo.size[d]) for d in dims]) if any(o)
        ]

    def peers(self):
        dims, offsets = self.offsets()
        return {tuple((dim, o) for dim, o in zip(dims, off) if o) for off in offsets}

    def steps(self, at, ins, outs, scratch):
        topo = self.topo
        (x_ref,), (out_ref,) = ins, outs
        send_sem, recv_sem, own_sem = scratch
        dims, offsets = self.offsets()
        me = topo.index(at, self.group)

        def own():
            return pltpu.make_async_copy(x_ref.at[me], out_ref.at[me], own_sem)

        def send(i):
            there = topo.moved(at, dims, offsets[i])
            source = x_ref.at[topo.index(there, self.group)]
            return remote(source, out_ref.at[me], send_sem.at[i], recv_sem.at[i], topo.device(there))

        def start():
            if self.keep:
                own().start()
            for i in range(len(offsets)):
                send(i).start()

        def wait(i):
            ref = out_ref.at[topo.index(topo.moved(at, dims, offsets[i], -1), self.group)]
            arrived(topo, at, ref, send_sem.at[i], recv_sem.at[i])

        def end():
            for i in range(len(offsets)):
                send(i).wait_send()
            if self.keep:
                own().wait()

        return [start] + [lambda i=i: wait(i) for i in range(len(offsets))], [end]


class Finish:
    def __init__(self, topo, x, y):
        self.topo = topo
        self.inputs = [x, y]
        self.outputs = [
            jax.ShapeDtypeStruct(x.shape, x.dtype),
            jax.ShapeDtypeStruct(y.shape, y.dtype),
        ]
        self.in_specs = [pl.BlockSpec(memory_space=pl.ANY)] * 2
        self.out_specs = [pl.BlockSpec(memory_space=pl.ANY)] * 2
        self.inner = Exchange(topo, "seq", y)
        self.scratch = self.inner.scratch + [pltpu.SemaphoreType.DMA(())] * 3

    def peers(self):
        return self.inner.peers()

    def route(self):
        topo = self.topo
        dp, seq = lax.axis_index("dp"), lax.axis_index("seq")
        n = seq * topo.n_dp + dp
        target = (lax.div(n, topo.n_seq), lax.rem(n, topo.n_seq))
        m = dp * topo.n_seq + seq
        source = (lax.rem(m, topo.n_dp), lax.div(m, topo.n_dp))
        stays = (target[0] == dp) & (target[1] == seq)
        return target, source, stays

    def greet(self, barrier):
        target, source, stays = self.route()

        @pl.when(jnp.logical_not(stays))
        def _():
            pl.semaphore_signal(barrier, inc=1, device_id=source, device_id_type=MESH)

        return jnp.where(stays, 0, 1)

    def steps(self, at, ins, outs, scratch):
        (x_ref, y_ref), (x_out, y_out) = ins, outs
        send_sem, recv_sem, own_sem = scratch[3:]
        target, source, stays = self.route()
        cp = remote(x_ref, x_out, send_sem, recv_sem, target)
        own = pltpu.make_async_copy(x_ref, x_out, own_sem)
        inner, ends = self.inner.steps(at, [y_ref], [y_out], scratch[:3])

        def start():
            pl.when(stays)(own.start)
            pl.when(jnp.logical_not(stays))(cp.start)

        def end():
            pl.when(stays)(own.wait)
            pl.when(jnp.logical_not(stays))(cp.wait)

        return [start] + inner, ends + [end]


def greet(topo, ops):
    at = topo.here()
    peers = sorted(set().union(*[op.peers() for op in ops]))
    barrier = pltpu.get_barrier_semaphore()
    for peer in peers:
        there = topo.device(topo.moved(at, [p[0] for p in peer], [p[1] for p in peer]))
        pl.semaphore_signal(barrier, inc=1, device_id=there, device_id_type=MESH)
    count = len(peers)
    for op in ops:
        if hasattr(op, "greet"):
            count = count + op.greet(barrier)
    pl.semaphore_wait(barrier, count)
    return at


class Steps:
    def __init__(self, steps):
        self.todo = steps[0] + steps[1]

    def run(self, count=1):
        for _ in range(count):
            if self.todo:
                self.todo.pop(0)()

    def finish(self):
        self.run(len(self.todo))


def run_slot(t, slots):
    def tree(low, high):
        if not any(slots[low:high]):
            return
        if high - low == 1:
            for step in slots[low]:
                step()
            return
        middle = (low + high) // 2
        left, right = any(slots[low:middle]), any(slots[middle:high])
        if left and right:
            lax.cond(t < middle, lambda: tree(low, middle), lambda: tree(middle, high))
        elif left:
            pl.when(t < middle)(lambda: tree(low, middle))
        else:
            pl.when(t >= middle)(lambda: tree(middle, high))

    tree(0, len(slots))


def communicate(topo, name, collective_id, *ops):
    n_in = [len(op.inputs) for op in ops]
    n_out = [len(op.outputs) for op in ops]
    n_scratch = [len(op.scratch) for op in ops]

    def kernel(*refs):
        refs = list(refs)
        take = lambda counts: [[refs.pop(0) for _ in range(k)] for k in counts]
        ins, outs, scratch = take(n_in), take(n_out), take(n_scratch)
        at = greet(topo, ops)
        running = [Steps(op.steps(at, i, o, s)) for op, i, o, s in zip(ops, ins, outs, scratch)]
        while any(r.todo for r in running):
            for r in running:
                r.run()

    results = pl.pallas_call(
        kernel,
        name=name,
        out_shape=[s for op in ops for s in op.outputs],
        in_specs=[s for op in ops for s in op.in_specs],
        out_specs=[s for op in ops for s in op.out_specs],
        scratch_shapes=[s for op in ops for s in op.scratch],
        compiler_params=pltpu.CompilerParams(
            collective_id=collective_id, has_side_effects=True, vmem_limit_bytes=58 << 20
        ),
    )(*[x for op in ops for x in op.inputs])
    results = list(results)
    return [[results.pop(0) for _ in range(k)] for k in n_out]


class Scatter(VScatter):
    def __init__(self, topo, group, x, parts):
        super().__init__(topo, group, x.shape, x.dtype, parts)
        self.inputs = [x]
        self.outputs = [jax.ShapeDtypeStruct(x.shape[1:], F32)]
        self.in_specs = [pl.BlockSpec(memory_space=pltpu.VMEM)]
        self.out_specs = [pl.BlockSpec(memory_space=pltpu.VMEM)]

    def steps(self, at, ins, outs, scratch):
        return super().steps(at, ins[0], outs[0], scratch)


def row_parts(rows, orders, weights, step=16):
    parts, row, total = [], 0, sum(weights)
    for i, (order, weight) in enumerate(zip(orders, weights)):
        n = rows - row if i == len(orders) - 1 else min(rows - row, int(round(rows * weight / total / step)) * step)
        if n:
            parts.append((row, n, order))
            row += n
    return parts


def matmul(left, right):
    return jnp.dot(left, right, preferred_element_type=jnp.float32)


def contract(form, left, right):
    return jnp.einsum(form, left, right, preferred_element_type=jnp.float32)


def rotary(positions, size):
    half_size = size // 2
    frequency = ROTARY_BASE ** (-(jnp.arange(half_size, dtype=jnp.float32) * 2.0) / size)
    angles = positions.astype(jnp.float32)[:, None] * frequency[None, :]
    return (jnp.cos(angles), jnp.sin(angles))


def rotate(values, cosine_table, sine_table):
    half_size = values.shape[-1] // 2
    first_half = values[..., :half_size]
    second_half = values[..., half_size:]
    return jnp.concatenate(
        [
            first_half * cosine_table - second_half * sine_table,
            second_half * cosine_table + first_half * sine_table,
        ],
        axis=-1,
    )


def normalize(values, gain_vector):
    inverse_rms = lax.rsqrt(jnp.mean(values * values, axis=-1, keepdims=True) + EPSILON)
    unit_rows = values * inverse_rms
    return (unit_rows * gain_vector, unit_rows, inverse_rms)


def norm_backward(grad_normed, unit_rows, inverse_rms, gain_vector):
    gain_term = jnp.sum(grad_normed * unit_rows, axis=0)
    grad_unit = grad_normed * gain_vector
    inner = jnp.mean(grad_unit * unit_rows, axis=-1, keepdims=True)
    return (gain_term, inverse_rms * (grad_unit - unit_rows * inner))


def dot_t(left, right):
    return lax.dot_general(left, right, (((1,), (1,)), ((), ())), preferred_element_type=F32)


def t_dot(left, right):
    return lax.dot_general(left, right, (((0,), (0,)), ((), ())), preferred_element_type=F32)


GELU_C = math.sqrt(2.0 / math.pi)


def gelu_parts(v):
    square = v * v
    t = jnp.tanh(GELU_C * (v + 0.044715 * v * square))
    half_up = 0.5 * (1.0 + t)
    slope = half_up + 0.5 * v * (1.0 - t * t) * (GELU_C * (1.0 + 3.0 * 0.044715 * square))
    return v * half_up, slope


def feed_forward(
    topo, collective_id, normed, grads, grads_half,
    w_gate, w_up, w_down, gate_adapt, gate_expand, up_adapt, up_expand, down_adapt, down_expand,
):
    rows, width = normed.shape
    quad = topo.group_size("quad")
    half = topo.group_size("half")
    units = w_gate.shape[1] // quad
    rank = gate_adapt.shape[1]
    ranks = rank // 2
    half_width = width // 2
    d_rows, r_rows = half_width // quad, ranks // quad
    per_chunk = 512 // rows
    tile = 512
    block = 256

    dims = "hxclb"
    keys = list(itertools.product(*[range(topo.size[d]) for d in dims]))
    chunks = [keys[i : i + per_chunk] for i in range(0, len(keys), per_chunk)]
    own = len(chunks) // 2
    chunk_of = {key: i for i, keys_of in enumerate(chunks) for key in keys_of}

    def need(order, key):
        at_dim = dict(zip(order, key))
        return chunk_of[tuple(at_dim.get(d, 0) for d in dims)]

    near = row_parts(rows, ("xlbc", "lbxc", "bxlc"), (1, 1, 1))
    both = jnp.concatenate([normed, grads], axis=0)
    far = row_parts(2 * rows, ("hxlbc", "hlbxc", "hbxlc"), (1, 1, 1))
    gather_n = Gather(topo, "half", normed, near, need=need, keep=False)
    gather_far = Gather(topo, "all", both, far, beyond="h", need=need)
    thirds = row_parts(2 * rows, ("cxbl", "cblx", "clxb"), (1, 1, 1))
    sum_both = SlimScatter(topo, "half", (half, 2 * rows, width), BF16, thirds)
    comm = [gather_n, gather_far, sum_both]

    inputs = [
        normed, both, grads_half, w_gate, w_up, w_down,
        gate_adapt, gate_expand, up_adapt, up_expand, down_adapt, down_expand,
    ]
    part = jax.ShapeDtypeStruct((half, 2 * rows, width), BF16)
    grad = jax.ShapeDtypeStruct((quad, d_rows + r_rows, units), BF16)
    any_spec = pl.BlockSpec(memory_space=pl.ANY)
    out_shape = [part, grad, grad, grad]
    out_specs = [any_spec] * 4
    scratch = [
        pltpu.VMEM((width, units), BF16), pltpu.VMEM((width, units), BF16), pltpu.VMEM((units, width), BF16),
        pltpu.VMEM((width, rank), BF16), pltpu.VMEM((rank, units), BF16),
        pltpu.VMEM((width, rank), BF16), pltpu.VMEM((rank, units), BF16),
        pltpu.VMEM((units, rank), BF16), pltpu.VMEM((rank, width), BF16),
        pltpu.VMEM((half_width + ranks, units), F32),
        pltpu.VMEM((half_width + ranks, units), F32),
        pltpu.VMEM((half_width + ranks, units), F32),
        pltpu.VMEM((3, tile, units), BF16),
        pltpu.VMEM((3, tile, ranks), BF16),
        pltpu.VMEM((2, tile, width), BF16), pltpu.VMEM((2, tile, width), BF16),
        pltpu.VMEM((tile, width), BF16), pltpu.VMEM((tile, width), BF16),
        pltpu.SemaphoreType.DMA((9,)),
        pltpu.SemaphoreType.DMA((2, 2, per_chunk)),
        pltpu.SemaphoreType.DMA((2, per_chunk)),
        pltpu.SemaphoreType.DMA((3,)),
    ]
    n_own = len(scratch)
    shared = sum_both.shared_scratch()
    scratch = scratch + shared
    for op in comm:
        out_shape = out_shape + op.outputs
        out_specs = out_specs + op.out_specs
        scratch = scratch + op.scratch

    def kernel(*refs):
        refs = list(refs)
        (
            n_hbm, both_hbm, g_half, wg_hbm, wu_hbm, wd_hbm, ga_hbm, ge_hbm, ua_hbm, ue_hbm, da_hbm, de_hbm,
        ) = [refs.pop(0) for _ in inputs]
        part_hbm, dg_out, du_out, dd_out = [refs.pop(0) for _ in range(4)]
        op_outs = [[refs.pop(0) for _ in op.outputs] for op in comm]
        (
            wg, wu, wd, ga, ge, ua, ue, da, de, acc_g, acc_u, acc_d, acts, low_s, n_buf, g_buf, down_st, gn_st,
            w_sem, load_sem, store_sem, grad_sem,
        ) = [refs.pop(0) for _ in range(n_own)]
        shared_refs = [refs.pop(0) for _ in shared]
        op_scratch = [[refs.pop(0) for _ in op.scratch] for op in comm]
        mix_s, gg_s, gu_s = acts.at[0], acts.at[1], acts.at[2]
        at = topo.here()
        high = at["h"]
        member = topo.index(at, "quad")
        unit_at = pl.multiple_of(member * units, units)

        w_copies = [
            pltpu.make_async_copy(src, dst, w_sem.at[i])
            for i, (src, dst) in enumerate(
                (
                    (de_hbm, de),
                    (da_hbm.at[pl.ds(unit_at, units), :], da),
                    (wd_hbm.at[pl.ds(unit_at, units), :], wd),
                    (ga_hbm, ga),
                    (ge_hbm.at[:, pl.ds(unit_at, units)], ge),
                    (wg_hbm.at[:, pl.ds(unit_at, units)], wg),
                    (ua_hbm, ua),
                    (ue_hbm.at[:, pl.ds(unit_at, units)], ue),
                    (wu_hbm.at[:, pl.ds(unit_at, units)], wu),
                )
            )
        ]
        for cp in w_copies:
            cp.start()

        greet(topo, comm)
        gathers = (gather_n, gather_far)
        all_steps = [op.steps(at, [x], o, sc) for op, x, o, sc in zip(gathers, (n_hbm, both_hbm), op_outs, op_scratch)]
        ranked = []
        for g, (op, (steps_g, _)) in enumerate(zip(gathers, all_steps)):
            for i, (f, (p, k)) in enumerate(zip(steps_g, op.work())):
                when = NEAR_US * i / len(steps_g) - 20.0 if g == 0 else FAR_AT + i * FAR_US
                ranked.append((when if any(k) or g else -1e3, g, i, f, need(op.parts[p][2], k)))
        ranked.sort(key=lambda w: w[:3])
        steps = [(f, chunk) for _, _, _, f, chunk in ranked]
        when_of = [w[0] for w in ranked]
        started = len(gather_n.parts)
        for f, _ in steps[:started]:
            f()

        def upto(chunk, done):
            last = [i for i, (_, c) in enumerate(steps) if c <= chunk and i >= started]
            return max([done] + [i + 1 for i in last])

        acc_g[...] = jnp.zeros_like(acc_g)
        acc_u[...] = jnp.zeros_like(acc_u)
        acc_d[...] = jnp.zeros_like(acc_d)

        def merge_rows(weight, adapt, expand, total):
            def one(i, _):
                r = pl.ds(pl.multiple_of(i * block, block), block)
                weight[r, :] = (weight[r, :].astype(F32) + matmul(adapt[r, :], expand[...])).astype(BF16)
                return 0

            lax.fori_loop(0, total // block, one, 0)

        first_chunk = upto(0, started)
        ready = [started]

        def early(count):
            last = min(ready[0] + count, first_chunk)
            for f, _ in steps[ready[0] : last]:
                f()
            ready[0] = last

        for cp in w_copies[:3]:
            cp.wait()
        merge_rows(wd, da, de, units)
        early(int(EARLY))
        for cp in w_copies[3:6]:
            cp.wait()
        merge_rows(wg, ga, ge, width)
        early(int(EARLY))
        for cp in w_copies[6:]:
            cp.wait()
        merge_rows(wu, ua, ue, width)

        def key_of(c, i):
            k = c * per_chunk + i
            key = []
            for d in reversed(dims):
                key.append(lax.rem(k, topo.size[d]))
                k = lax.div(k, topo.size[d])
            return key[::-1]

        def chunk_copies(c, slot, other):
            copies = []
            for i in range(per_chunk):
                origin = topo.moved(at, dims, key_of(c, i), -1)
                r = pl.ds(i * rows, rows)
                in_half = topo.index(origin, "half")
                if other:
                    n_src = op_outs[1][0].at[in_half, pl.ds(0, rows)]
                    g_src = op_outs[1][0].at[in_half, pl.ds(rows, rows)]
                else:
                    n_src, g_src = op_outs[0][0].at[in_half], g_half.at[in_half]
                copies.append(pltpu.make_async_copy(n_src, n_buf.at[slot, r], load_sem.at[slot, 0, i]))
                copies.append(pltpu.make_async_copy(g_src, g_buf.at[slot, r], load_sem.at[slot, 1, i]))
            return copies

        def first_copies():
            copies = chunk_copies(0, 0, False)
            r = pl.ds(0, rows)
            copies[0] = pltpu.make_async_copy(n_hbm, n_buf.at[0, r], load_sem.at[0, 0, 0])
            return copies

        def store_copies(c):
            copies = []
            for i in range(per_chunk):
                slot = topo.index(topo.moved(at, dims, key_of(c, i), -1), "half")
                r = pl.ds(i * rows, rows)
                for k, source in enumerate((gn_st, down_st)):
                    place = part_hbm.at[slot, pl.ds(k * rows, rows)]
                    copies.append(pltpu.make_async_copy(source.at[r], place, store_sem.at[k, i]))
            return copies

        n_one, n_two, n_three = units // block, width // block, half_width // block
        scale = units / 1024
        kinds = {
            False: [("one", n_one, 1.9), ("two", n_two, 1.0 * scale), ("pre", 1, 2.0 * scale), ("three", n_three, 0.7 * scale)],
            True: [("one", n_one, 1.9), ("pre", 1, 2.0 * scale), ("three", n_three, 0.7 * scale)],
        }
        slots = {(other, kind): [[] for _ in range(own * n)] for other in (False, True) for kind, n, _ in kinds[other]}
        done = first_chunk
        for f, _ in steps[ready[0] : done]:
            f()
        clock = 0.0
        for c in range(len(chunks)):
            other = c >= own
            for kind, n, cost in kinds[other]:
                for i in range(n):
                    clock += cost
                    target = max(done, sum(1 for w in when_of if w <= clock))
                    if kind == "pre" and c + 1 < len(chunks):
                        target = upto(c + 1, target)
                    slots[other, kind][(c - own if other else c) * n + i] += [f for f, _ in steps[done:target]]
                    done = target
        sums, sums_end = sum_both.steps(at, part_hbm, op_outs[2], op_scratch[2], shared_refs)
        clock, summed = 0.0, 0
        for c in range(own):
            for kind, n, cost in kinds[True]:
                for i in range(n):
                    clock += cost
                    target = min(len(sums), 1 + int(max(clock - 3.0, 0.0) / SUM_US))
                    if kind != "pre":
                        slots[True, kind][c * n + i] += sums[summed:target]
                        summed = target

        for cp in first_copies():
            cp.start()
        low_cols = pl.ds(pl.multiple_of(high * ranks, ranks), ranks)
        half_at = high * half_width

        def chunk_loop(other):
            first = own if other else 0

            def body(k, _):
                c = first + k
                slot = lax.rem(c, 2)
                nb, gb = n_buf.at[slot], g_buf.at[slot]
                for cp in chunk_copies(c, slot, other):
                    cp.wait()
                low_s[0] = matmul(nb[...], ga[:, low_cols]).astype(BF16)
                low_s[1] = matmul(nb[...], ua[:, low_cols]).astype(BF16)
                low_s[2] = dot_t(gb[...], de[low_cols, :]).astype(BF16)

                def one(i, _):
                    cols = pl.ds(pl.multiple_of(i * block, block), block)
                    gate = matmul(nb[...], wg[:, cols])
                    up = matmul(nb[...], wu[:, cols])
                    act, slope = gelu_parts(gate)
                    gm = dot_t(gb[...], wd[cols, :])
                    mix_s[:, cols] = (act * up).astype(BF16)
                    gg_s[:, cols] = (gm * up * slope).astype(BF16)
                    gu_s[:, cols] = (gm * act).astype(BF16)
                    run_slot(k * n_one + i, slots[other, "one"])
                    return 0

                lax.fori_loop(0, n_one, one, 0)
                if not other:

                    @pl.when(c > 0)
                    def _():
                        for cp in store_copies(c - 1):
                            cp.wait()

                    def two(i, _):
                        cols = pl.ds(pl.multiple_of(i * block, block), block)
                        down_st[:, cols] = matmul(mix_s[...], wd[:, cols]).astype(BF16)
                        gn_st[:, cols] = (dot_t(gg_s[...], wg[cols, :]) + dot_t(gu_s[...], wu[cols, :])).astype(BF16)
                        run_slot(k * n_two + i, slots[other, "two"])
                        return 0

                    lax.fori_loop(0, n_two, two, 0)
                    for cp in store_copies(c):
                        cp.start()
                for i, (acc, grads_s) in enumerate(((acc_g, gg_s), (acc_u, gu_s), (acc_d, mix_s))):
                    acc[half_width:, :] += t_dot(low_s[i], grads_s[...])
                run_slot(k, slots[other, "pre"])
                if other:

                    @pl.when(c + 1 < len(chunks))
                    def _():
                        for cp in chunk_copies(c + 1, 1 - slot, True):
                            cp.start()

                else:

                    @pl.when(c + 1 < own)
                    def _():
                        for cp in chunk_copies(c + 1, 1 - slot, False):
                            cp.start()

                    @pl.when(c + 1 == own)
                    def _():
                        for cp in chunk_copies(c + 1, 1 - slot, True):
                            cp.start()

                def three(i, _):
                    r = pl.ds(pl.multiple_of(i * block, block), block)
                    cols = pl.ds(pl.multiple_of(half_at + i * block, block), block)
                    acc_g[r, :] += t_dot(nb[:, cols], gg_s[...])
                    acc_u[r, :] += t_dot(nb[:, cols], gu_s[...])
                    acc_d[r, :] += t_dot(gb[:, cols], mix_s[...])
                    run_slot(k * n_three + i, slots[other, "three"])
                    return 0

                lax.fori_loop(0, n_three, three, 0)
                return 0

            lax.fori_loop(0, own, body, 0)

        chunk_loop(False)
        for cp in store_copies(own - 1):
            cp.wait()
        chunk_loop(True)

        pending = []
        for q in range(quad):
            for k, (acc, out) in enumerate(((acc_g, dg_out), (acc_u, du_out), (acc_d, dd_out))):
                if len(pending) >= 3:
                    pending.pop(0).wait()
                acts[k, :d_rows, :] = acc[q * d_rows : (q + 1) * d_rows, :].astype(BF16)
                acts[k, d_rows : d_rows + r_rows, :] = acc[
                    half_width + q * r_rows : half_width + (q + 1) * r_rows, :
                ].astype(BF16)
                cp = pltpu.make_async_copy(acts.at[k, pl.ds(0, d_rows + r_rows)], out.at[q], grad_sem.at[k])
                cp.start()
                pending.append(cp)
        for f in steps[done:]:
            f[0]()
        for f in sums[summed:]:
            f()
        for cp in pending:
            cp.wait()
        for f in [f for _, end in all_steps for f in end] + sums_end:
            f()

    flops = 2 * rows * topo.n_dp * topo.n_seq * units * width * 9
    results = pl.pallas_call(
        kernel,
        name="feed_forward",
        out_shape=out_shape,
        in_specs=[any_spec] * len(inputs),
        out_specs=out_specs,
        scratch_shapes=scratch,
        compiler_params=pltpu.CompilerParams(
            collective_id=collective_id, has_side_effects=True, vmem_limit_bytes=60 << 20
        ),
        cost_estimate=pl.CostEstimate(flops=flops, bytes_accessed=1 << 27, transcendentals=0),
    )(*inputs)
    dg, du, dd = results[1:4]
    total = results[4 + len(gather_n.outputs) + len(gather_far.outputs)]
    return total[rows:], total[:rows], dg, du, dd


KV_STEPS = 3
EARLY = 8
NEAR_US = 45.0
FAR_AT = 5.0
FAR_US = 1.5
SUM_US = 2.0


def attention_back(
    topo, collective_id, grad_branch, grad_middle, query_rot, heads_out, key_value, log_total, own_segs, key_segs,
    normed_all, unit_attn, rms_attn, gain_attn, gain_mlp_term, cosine, sine, wo, wq, wk, wv,
    query_adapt, out_expand, key_adapt, value_adapt, dg, du, dd,
):
    groups, rows, width = normed_all.shape
    n_seq = topo.n_seq
    length = rows * n_seq
    head_cols = heads_out.shape[1]
    heads = head_cols // HD
    tokens = groups * rows
    rank = query_adapt.shape[1]
    scale = HD ** (-0.5)
    d_rows, r_rows = width // n_seq, rank // n_seq
    share_d, share_r = width // groups, rank // groups
    kv_d, kv_r = d_rows // groups, r_rows // groups
    kv_pad = -(-kv_r // 16) * 16
    kv_rows = kv_d + kv_pad + 16

    gather_g = Gather(topo, "dp", grad_branch, row_parts(rows, ("xc", "xc"), (1, 1)))
    gather_kv = Gather(topo, "dp", jax.ShapeDtypeStruct((rows, 2 * HD), BF16), [(0, rows, "xc")])
    swaps = [Exchange(topo, "quad", a, keep=False) for a in (dg, du, dd)]
    seq_parts = lambda n: row_parts(n, ("blh", "lbh"), (2, 1))
    w_shape = (n_seq, d_rows + r_rows, head_cols)
    sum_o = VScatter(topo, "seq", w_shape, BF16, seq_parts(d_rows + r_rows))
    sum_q = VScatter(topo, "seq", w_shape, BF16, seq_parts(d_rows + r_rows))
    sum_k = VScatter(topo, "seq", (n_seq, kv_rows, 2 * HD), BF16, seq_parts(kv_rows))
    kv_shape = (groups * n_seq, rows, 2 * HD)
    sum_kv = VScatter(topo, "all", kv_shape, BF16, row_parts(rows, ("cxblh", "cblxh"), (1, 1)))
    sum_n = VScatter(topo, "dp", (groups, rows, width), BF16, row_parts(rows, ("cx", "cx"), (1, 1)))

    inputs = [
        grad_branch, grad_middle, query_rot, heads_out, key_value, log_total, own_segs, key_segs,
        normed_all, unit_attn, rms_attn, gain_attn, gain_mlp_term, cosine, sine, wo, wq, wk, wv,
        query_adapt, out_expand, key_adapt, value_adapt, dg, du, dd,
    ]
    vmem, anywhere = pl.BlockSpec(memory_space=pltpu.VMEM), pl.BlockSpec(memory_space=pl.ANY)
    big = groups * n_seq > 32
    in_specs = [anywhere] + [vmem] * (len(inputs) - 4) + [anywhere] * 3
    if big:
        in_specs[4] = anywhere
    out_shape = [
        jax.ShapeDtypeStruct((rows, width), BF16),
        jax.ShapeDtypeStruct((d_rows + r_rows, head_cols), F32),
        jax.ShapeDtypeStruct((d_rows + r_rows, head_cols), F32),
        jax.ShapeDtypeStruct((kv_rows, 2 * HD), F32),
    ] + [op.outputs[0] for op in swaps]
    out_specs = [vmem] * 4 + [anywhere] * 3
    if big:
        sum_kv = SlimScatter(topo, "all", kv_shape, BF16, row_parts(rows, ("cxblh", "cblxh"), (1, 1)))
        out_shape = out_shape + [jax.ShapeDtypeStruct(kv_shape, BF16)] + sum_kv.outputs
        out_specs = out_specs + [anywhere] + sum_kv.out_specs
    scratch = [
        pltpu.VMEM((groups, rows, width), BF16),
        pltpu.VMEM((tokens, head_cols), BF16),
        pltpu.VMEM((tokens, head_cols), BF16),
        pltpu.VMEM(w_shape, BF16),
        pltpu.VMEM(w_shape, BF16),
        pltpu.VMEM((n_seq, kv_rows, 2 * HD), BF16),
        pltpu.VMEM((length, 2 * HD) if big else kv_shape, BF16),
        pltpu.VMEM((groups, rows, width), BF16),
        pltpu.VMEM((rows, 2 * HD), F32),
        pltpu.VMEM((rows, width), F32),
        pltpu.VMEM((rows, 2 * HD), BF16),
        pltpu.VMEM((groups, rows, 2 * HD), BF16),
        pltpu.SemaphoreType.DMA((n_seq,)),
    ]
    n_own = len(scratch)
    shared = sum_kv.shared_scratch() + [pltpu.VMEM((length, 2 * HD), BF16)] if big else []
    scratch = scratch + shared
    ops = [gather_g, gather_kv] + swaps + [sum_o, sum_q, sum_k, sum_kv, sum_n]
    for op in ops:
        scratch = scratch + op.scratch

    def kernel(*refs):
        refs = list(refs)
        (
            gb_hbm, gmid, qrot, hout, kv, lse, own_seg, key_seg, norm_all, unit, rms, gain, gain_term, cos, sin,
            wo_r, wq_r, wk_r, wv_r, qa, oe, ka, va, dg_r, du_r, dd_r,
        ) = [refs.pop(0) for _ in inputs]
        grad_rows, so_out, sq_out, sk_out, dg_o, du_o, dd_o = [refs.pop(0) for _ in range(7)]
        kv_outs = [refs.pop(0) for _ in out_shape[7:]]
        (
            ga, gh, gq, xo, xq, xk, xkv, xn, kv_sum, n_sum, gkv, gkv_all, load_sem,
        ) = [refs.pop(0) for _ in range(n_own)]
        shared_refs = [refs.pop(0) for _ in shared]
        op_scratch = [[refs.pop(0) for _ in op.scratch] for op in ops]
        dp = lax.axis_index("dp")
        at = greet(topo, ops)
        get_g = Steps(gather_g.steps(at, [gb_hbm], [ga], op_scratch[0]))
        get_g.run()
        moves = [
            Steps(op.steps(at, [r], [o], sc))
            for op, r, o, sc in zip(swaps, (dg_r, du_r, dd_r), (dg_o, du_o, dd_o), op_scratch[2:5])
        ]
        moves[0].run()
        get_g.finish()
        flat = lambda ref: ref[...].reshape(tokens, ref.shape[-1])

        gh[...] = dot_t(flat(ga), wo_r[...]).astype(BF16)

        for j in range(n_seq):
            part = t_dot(ga[:, :, j * d_rows : (j + 1) * d_rows].reshape(tokens, d_rows), hout[...])
            xo[j, :d_rows, :] = part.astype(BF16)
        low = dot_t(flat(ga), oe[...]).astype(BF16)
        part = t_dot(low, hout[...]).astype(BF16)
        for j in range(n_seq):
            xo[j, d_rows:, :] = part[j * r_rows : (j + 1) * r_rows, :]
        get_o = Steps(sum_o.steps(at, xo, so_out, op_scratch[5]))
        get_o.run()

        seq = lax.axis_index("seq")
        key_at = lax.broadcasted_iota(jnp.int32, (heads * rows, length), 1)
        row_at = lax.broadcasted_iota(jnp.int32, (heads * rows, length), 0)
        causal = key_at <= seq * rows + lax.rem(row_at, rows)
        for s in range(groups):
            r = slice(s * rows, (s + 1) * rows)
            stack = lambda ref: jnp.concatenate([ref[r, h * HD : (h + 1) * HD] for h in range(heads)], axis=0)
            q, d_o = stack(qrot), stack(gh)
            if big:
                one = shared_refs[3]
                cp = pltpu.make_async_copy(kv.at[pl.ds(s * length, length)], one, load_sem.at[0])
                cp.start()
                cp.wait()
            else:
                one = kv.at[pl.ds(s * length, length)]
            keys, values = one[:, :HD], one[:, HD:]
            mine = jnp.concatenate([own_seg[:, s : s + 1]] * heads, axis=0)
            allowed = causal & (mine == key_seg[s : s + 1, :])
            scores = jnp.where(allowed, dot_t(q, keys) * scale, MASKED)
            probs = jnp.exp(scores - lse[s])
            grad_probs = dot_t(d_o, values)
            delta = jnp.sum(probs * grad_probs, axis=-1, keepdims=True)
            grad_scores = (probs * (grad_probs - delta)).astype(BF16)
            d_q = matmul(grad_scores, keys) * scale
            d_k = (t_dot(grad_scores, q) * scale).astype(BF16)
            d_v = t_dot(probs.astype(BF16), d_o).astype(BF16)
            both = jnp.concatenate([d_k, d_v], axis=1)
            if big:
                xkv[...] = both
                copies = [
                    pltpu.make_async_copy(
                        xkv.at[pl.ds(j * rows, rows)], kv_outs[0].at[s * n_seq + j], load_sem.at[j]
                    )
                    for j in range(n_seq)
                ]
                for cp in copies:
                    cp.start()
                for cp in copies:
                    cp.wait()
            else:
                xkv[s * n_seq : (s + 1) * n_seq] = both.reshape(n_seq, rows, 2 * HD)
            for h in range(heads):
                gq[r, h * HD : (h + 1) * HD] = rotate(
                    d_q[h * rows : (h + 1) * rows], cos[...], -sin[...]
                ).astype(BF16)
            if s + 2 >= groups:
                get_o.run(4 if s + 2 == groups else 2)
        if big:
            get_kv = Steps(sum_kv.steps(at, kv_outs[0], kv_outs[1:], op_scratch[8], shared_refs[:3]))
        else:
            get_kv = Steps(sum_kv.steps(at, xkv, kv_sum, op_scratch[8]))
        get_kv.run()
        moves[1].run()
        for s in range(groups):
            xn[s] = dot_t(gq[s * rows : (s + 1) * rows, :], wq_r[...]).astype(BF16)
        get_n = Steps(sum_n.steps(at, xn, n_sum, op_scratch[9]))
        get_n.run()

        def poll():
            get_kv.run(1)

        for j in range(n_seq):
            part = t_dot(norm_all[:, :, j * d_rows : (j + 1) * d_rows].reshape(tokens, d_rows), gq[...])
            xq[j, :d_rows, :] = part.astype(BF16)
            poll()
        low = matmul(flat(norm_all), qa[...]).astype(BF16)
        part = t_dot(low, gq[...]).astype(BF16)
        for j in range(n_seq):
            xq[j, d_rows:, :] = part[j * r_rows : (j + 1) * r_rows, :]
        get_q = Steps(sum_q.steps(at, xq, sq_out, op_scratch[6]))
        get_q.run()
        get_n.run(2)
        while get_kv.todo:
            get_kv.run(KV_STEPS)
            get_o.run()
        get_n.finish()
        moves[2].run()

        total_kv = kv_outs[1] if big else kv_sum
        gk = rotate(total_kv[:, :HD], cos[...], -sin[...]).astype(BF16)
        gv = total_kv[:, HD:].astype(BF16)
        gkv[:, :HD] = gk
        gkv[:, HD:] = gv
        get_kv2 = Steps(gather_kv.steps(at, [gkv], [gkv_all], op_scratch[1]))
        get_kv2.run()
        grad_normed = n_sum[...] + dot_t(gk, wk_r[...]) + dot_t(gv, wv_r[...])
        u_rows = unit[...]
        gain_attn_term = jnp.sum(grad_normed * u_rows, axis=0, keepdims=True)
        grad_unit = grad_normed * gain[...]
        inner = jnp.mean(grad_unit * u_rows, axis=-1, keepdims=True)
        get_o.run(2)
        get_q.run(2)
        grad_rows[...] = (gmid[...] + rms[...] * (grad_unit - u_rows * inner)).astype(BF16)
        get_kv2.finish()
        get_q.run(2)
        mine = pl.ds(pl.multiple_of(dp * share_d, share_d), share_d)
        part_rows = norm_all[:, :, mine].reshape(tokens, share_d)
        low_k = matmul(flat(norm_all), ka[...]).astype(BF16)
        low_v = matmul(flat(norm_all), va[...]).astype(BF16)
        g_rows = flat(gkv_all)
        part = t_dot(part_rows, g_rows).astype(BF16)
        low = jnp.concatenate(
            [t_dot(low_k, g_rows[:, :HD]), t_dot(low_v, g_rows[:, HD:])], axis=1
        )
        zero_r = jnp.zeros((kv_pad - kv_r, 2 * HD), F32)
        terms = jnp.concatenate([gain_attn_term, gain_term[...], jnp.zeros((14, width), F32)], axis=0)
        zero_c = jnp.zeros((16, 2 * HD - d_rows), F32)
        for j in range(n_seq):
            xk[j, :kv_d, :] = part[j * kv_d : (j + 1) * kv_d, :]
            xk[j, kv_d : kv_d + kv_pad, :] = jnp.concatenate(
                [low[j * kv_r : (j + 1) * kv_r, :], zero_r], axis=0
            ).astype(BF16)
            xk[j, kv_d + kv_pad :, :] = jnp.concatenate(
                [terms[:, j * d_rows : (j + 1) * d_rows], zero_c], axis=1
            ).astype(BF16)
        get_k = Steps(sum_k.steps(at, xk, sk_out, op_scratch[7]))
        get_k.run()
        left = [get_o, get_q, get_k]
        while any(g.todo for g in left):
            for g in left:
                g.run()
        for move in moves:
            move.finish()

    results = pl.pallas_call(
        kernel,
        name="attention_back",
        out_shape=out_shape,
        in_specs=in_specs,
        out_specs=out_specs,
        scratch_shapes=scratch,
        compiler_params=pltpu.CompilerParams(
            collective_id=collective_id, has_side_effects=True, vmem_limit_bytes=60 << 20
        ),
    )(*inputs)
    return results[:7]


def unfold(d_rows, member, owns, dg, du, dd, gate_expand, up_expand, down_adapt):
    quad, total, units = dg.shape
    rank = gate_expand.shape[0]
    r_rows = total - d_rows

    def kernel(
        me, dg_own, du_own, dd_own, dg_ref, du_ref, dd_ref, ge_ref, ue_ref, da_ref,
        wg, eg, wu, eu, wd, ad, ga, ua, de, term_g, term_u, term_d,
    ):
        first = pl.program_id(0) == 0
        mine = pl.program_id(0) == me[0]
        for own, got, term in ((dg_own, dg_ref, term_g), (du_own, du_ref, term_u), (dd_own, dd_ref, term_d)):
            term[...] = jnp.where(mine, own[0], got[0])
        for src, w, e in ((term_g, wg, eg), (term_u, wu, eu)):
            w[...] = src[:d_rows, :].astype(F32)
            e[...] = src[d_rows:, :].astype(F32)
        both = term_d[...].astype(F32).T
        wd[...] = both[:, :d_rows]
        ad[...] = both[:, d_rows:]
        for out, term in (
            (ga, dot_t(term_g[:d_rows, :], ge_ref[...])),
            (ua, dot_t(term_u[:d_rows, :], ue_ref[...])),
            (de, matmul(term_d[:d_rows, :], da_ref[...])),
        ):
            out[...] = jnp.where(first, term, term + out[...])

    cols = lambda n: pl.BlockSpec((n, units), lambda q, me: (0, q))
    side = lambda n: pl.BlockSpec((units, n), lambda q, me: (q, 0))
    block = pl.BlockSpec((1, total, units), lambda q, me: (q, 0, 0))
    own = pl.BlockSpec((1, total, units), lambda q, me: (me[0], 0, 0))
    kept = pl.BlockSpec((d_rows, rank), lambda q, me: (0, 0))
    shape = lambda *s: jax.ShapeDtypeStruct(s, F32)
    all_units = quad * units
    return pl.pallas_call(
        kernel,
        name="unfold",
        grid_spec=pltpu.PrefetchScalarGridSpec(
            num_scalar_prefetch=1,
            grid=(quad,),
            in_specs=[own] * 3 + [block] * 3 + [cols(rank), cols(rank), side(rank)],
            out_specs=[cols(d_rows), cols(r_rows), cols(d_rows), cols(r_rows), side(d_rows), side(r_rows)] + [kept] * 3,
            scratch_shapes=[pltpu.VMEM((total, units), BF16)] * 3,
        ),
        out_shape=[
            shape(d_rows, all_units), shape(r_rows, all_units), shape(d_rows, all_units), shape(r_rows, all_units),
            shape(all_units, d_rows), shape(all_units, r_rows),
        ] + [shape(d_rows, rank)] * 3,
        compiler_params=pltpu.CompilerParams(vmem_limit_bytes=56 << 20),
    )(member, *owns, dg, du, dd, gate_expand, up_expand, down_adapt)


def finish_small(topo, collective_id, small, n_moved, per_seq):
    rows, rank = small.shape[1:]
    n_seq = topo.n_seq
    sums = VScatter(topo, "dp", small.shape, small.dtype, [(0, rows, "cx")])
    moved = jax.ShapeDtypeStruct((n_moved, rank), F32)
    spread = jax.ShapeDtypeStruct((n_seq, 2 * per_seq, rank), F32)
    last = Finish(topo, moved, spread)
    scratch = [pltpu.VMEM((rows, rank), F32), pltpu.VMEM(moved.shape, F32), pltpu.VMEM(spread.shape, F32)]

    def kernel(x_ref, moved_out, spread_out, total, moved_in, spread_in, *refs):
        at = greet(topo, [sums, last])
        Steps(sums.steps(at, x_ref, total, refs[: len(sums.scratch)])).finish()
        moved_in[...] = total[:n_moved, :]
        for j in range(n_seq):
            for k in range(2):
                first = n_moved + (k * n_seq + j) * per_seq
                spread_in[j, k * per_seq : (k + 1) * per_seq, :] = total[first : first + per_seq, :]
        refs = refs[len(sums.scratch) :]
        Steps(last.steps(at, [moved_in, spread_in], [moved_out, spread_out], refs)).finish()

    return pl.pallas_call(
        kernel,
        name="finish_small",
        out_shape=[moved, spread],
        in_specs=[pl.BlockSpec(memory_space=pltpu.VMEM)],
        out_specs=[pl.BlockSpec(memory_space=pl.ANY)] * 2,
        scratch_shapes=scratch + sums.scratch + last.scratch,
        compiler_params=pltpu.CompilerParams(
            collective_id=collective_id, has_side_effects=True, vmem_limit_bytes=32 << 20
        ),
    )(small)


def local(
    topo,
    tokens, segment_ids, out_grad, gain_attn, gain_mlp, w_query, w_key, w_value, w_out, w_gate, w_up, w_down,
    query_adapt, query_expand, key_adapt, key_expand, value_adapt, value_expand, out_adapt, out_expand,
    gate_adapt, gate_expand, up_adapt, up_expand, down_adapt, down_expand,
):
    rows, width = tokens.shape[2], tokens.shape[3]
    groups, n_seq = topo.n_dp, topo.n_seq
    length = rows * n_seq
    heads_dev = w_query.shape[1] // HD
    head_cols = heads_dev * HD
    rank = query_adapt.shape[1]
    scale_qk = HD ** (-0.5)
    quad = topo.group_size("quad")
    units = w_gate.shape[1] // quad
    seq = lax.axis_index("seq")
    dp = lax.axis_index("dp")

    def merged(weight, adapt, expand):
        return (weight.astype(F32) + matmul(adapt, expand)).astype(BF16)

    wq = merged(w_query, query_adapt, query_expand)
    wk = merged(w_key, key_adapt, key_expand)
    wv = merged(w_value, value_adapt, value_expand)
    wo = merged(w_out, out_adapt, out_expand)
    token_rows = tokens[0, 0].astype(F32)
    grad_rows_in = out_grad[0, 0]
    normed, unit_attn, rms_attn = normalize(token_rows, gain_attn)
    normed_attn = normed.astype(BF16)
    positions = seq * rows + jnp.arange(rows, dtype=jnp.int32)
    cosine_table, sine_table = rotary(positions, HD)
    cosine_heads, sine_heads = cosine_table[:, None, :], sine_table[:, None, :]
    key_rot = rotate(matmul(normed_attn, wk), cosine_table, sine_table).astype(BF16)
    value_rows = matmul(normed_attn, wv).astype(BF16)
    key_value = jnp.concatenate([key_rot, value_rows], axis=1)
    seg_rows = jnp.zeros((16, rows), F32).at[0].set(segment_ids[0, 0].astype(F32))

    zyx, xzy = "lhbxc", "xlhbc"
    (normed_all,), (kv_all,), (seg_all,) = communicate(
        topo, "gather_attention", 0,
        Gather(topo, "dp", normed_attn, row_parts(rows, ("xc", "xc"), (1, 1))),
        Gather(topo, "all", key_value, row_parts(rows, (zyx, xzy), (7, 4))),
        Gather(topo, "all", seg_rows, [(0, 16, zyx)]),
    )
    kv_all = kv_all.reshape(groups, length, 2 * HD)
    keys_all, values_all = kv_all[..., :HD], kv_all[..., HD:]
    segments = seg_all[:, 0, :].reshape(groups, length)
    own_segments = lax.dynamic_slice_in_dim(segments, seq * rows, rows, 1)
    key_positions = jnp.arange(length, dtype=jnp.int32)
    causal = (key_positions[None, :] <= positions[:, None])[None, :, :]
    allowed = (causal & (own_segments[:, :, None] == segments[:, None, :]))[:, None, :, :]

    queries = matmul(normed_all.reshape(groups * rows, width), wq)
    query_rot = rotate(queries.reshape(groups, rows, heads_dev, HD), cosine_heads, sine_heads).astype(BF16)
    scores = jnp.where(allowed, contract("sthd,sjd->shtj", query_rot, keys_all) * scale_qk, MASKED)
    row_top = jnp.max(scores, axis=-1, keepdims=True)
    log_total = row_top + jnp.log(jnp.sum(jnp.exp(scores - row_top), axis=-1, keepdims=True))
    prob_low = jnp.exp(scores - log_total).astype(BF16)
    heads_out = (
        contract("shtj,sjd->sthd", prob_low, values_all).reshape(groups * rows, head_cols).astype(BF16)
    )
    out_part = matmul(heads_out, wo).astype(BF16).reshape(groups, rows, width)
    (out_sum,), (grad_half,) = communicate(
        topo, "sum_attention", 1,
        Scatter(topo, "dp", out_part, row_parts(rows, ("cx", "cx"), (1, 1))),
        Gather(topo, "half", grad_rows_in, row_parts(rows, ("xlbc", "lbxc", "bxlc"), (1, 1, 1))),
    )
    middle = token_rows + out_sum
    normed, unit_mlp, rms_mlp = normalize(middle, gain_mlp)
    normed_mlp = normed.astype(BF16)
    down_sum, gn_sum, dg, du, dd = feed_forward(
        topo, 2, normed_mlp, grad_rows_in, grad_half,
        w_gate, w_up, w_down, gate_adapt, gate_expand, up_adapt, up_expand, down_adapt, down_expand,
    )
    result_rows = (middle + down_sum).astype(BF16)
    gain_mlp_term, grad_from_mlp = norm_backward(gn_sum, unit_mlp, rms_mlp, gain_mlp)
    grad_middle = grad_rows_in.astype(F32) + grad_from_mlp
    grad_branch_attn = grad_middle.astype(BF16)
    my_kv_ranks = lambda a: lax.dynamic_slice_in_dim(a, dp * (rank // groups), rank // groups, 1)
    owns = (dg, du, dd)
    grad_rows, so, sq, sk, dg, du, dd = attention_back(
        topo, 4, grad_branch_attn, grad_middle,
        query_rot.reshape(groups * rows, head_cols), heads_out, kv_all.reshape(groups * length, 2 * HD),
        log_total.reshape(groups, heads_dev * rows, 1), own_segments.T, segments,
        normed_all, unit_attn, rms_attn, gain_attn[None], gain_mlp_term[None], cosine_table, sine_table,
        wo, wq, wk, wv, query_adapt, out_expand, my_kv_ranks(key_adapt), my_kv_ranks(value_adapt), dg, du, dd,
    )
    d_rows, r_rows = width // n_seq, rank // n_seq
    per_dev_d, per_dev_r = d_rows // groups, r_rows // groups
    kv_pad = -(-per_dev_r // 16) * 16
    grad_wg, grad_ge, grad_wu, grad_ue, grad_wd, grad_da, part_ga, part_ua, part_de = unfold(
        d_rows, lax.rem(seq, topo.group_size("quad")).reshape(1), owns, dg, du, dd, gate_expand, up_expand, down_adapt
    )
    grad_wq, grad_qe = sq[:d_rows], sq[d_rows:]
    grad_wo, grad_oa = so[:d_rows].T, so[d_rows:].T
    grad_wkv, grad_kve = sk[:per_dev_d], sk[per_dev_d : per_dev_d + per_dev_r]
    gains = jnp.pad(sk[per_dev_d + kv_pad : per_dev_d + kv_pad + 2, :d_rows], ((0, 6), (0, 0)))

    adapt = jnp.stack(
        [
            part_ga,
            part_ua,
            dot_t(grad_wq.astype(BF16), query_expand),
        ]
    )
    expand = jnp.stack(
        [
            part_de.T,
            matmul(so[:d_rows].astype(BF16), out_adapt).T,
        ]
    )
    adapt = adapt.reshape(3, groups, per_dev_d, rank).transpose(1, 0, 2, 3).reshape(groups, -1, rank)
    expand = expand.reshape(2, groups, rank // groups, d_rows).transpose(1, 0, 2, 3).reshape(groups, -1, d_rows)
    expand = jnp.pad(expand, ((0, 0), (0, 0), (0, rank - d_rows)))
    small_gains = jnp.pad(
        gains[:, :d_rows].reshape(8, groups, per_dev_d).transpose(1, 0, 2), ((0, 0), (0, 8), (0, rank - per_dev_d))
    )
    small = jnp.concatenate([adapt, small_gains, expand], axis=1).astype(BF16)
    n_adapt = 3 * per_dev_d
    per_seq = rank // groups // n_seq
    own_adapt, own_expand = finish_small(topo, 8, small, n_adapt + 16, per_seq)
    grad_ga, grad_ua, grad_qa = own_adapt[:n_adapt].reshape(3, per_dev_d, rank)
    grad_gain_attn = own_adapt[n_adapt, :per_dev_d]
    grad_gain_mlp = own_adapt[n_adapt + 1, :per_dev_d]
    own_expand = own_expand[..., :d_rows].reshape(n_seq, 2, per_seq, d_rows).transpose(1, 2, 0, 3).reshape(2, per_seq, width)
    grad_de, grad_oe = own_expand[0], own_expand[1]
    grad_wk, grad_wv = grad_wkv[:, :HD], grad_wkv[:, HD:]
    grad_ka = dot_t(grad_wk.astype(BF16), key_expand)
    grad_va = dot_t(grad_wv.astype(BF16), value_expand)
    grad_ke, grad_ve = grad_kve[:, :HD], grad_kve[:, HD:]
    return (
        result_rows[None, None], grad_rows[None, None],
        grad_gain_attn, grad_gain_mlp,
        grad_wq, grad_wk, grad_wv, grad_wo, grad_wg, grad_wu, grad_wd,
        grad_qa, grad_qe, grad_ka, grad_ke, grad_va, grad_ve, grad_oa, grad_oe,
        grad_ga, grad_ge, grad_ua, grad_ue, grad_da, grad_de,
    )


def solution(mesh):
    topo = Topo(mesh.shape["dp"], mesh.shape["seq"])
    both = ("dp", "seq")
    in_specs = (
        P(None, "dp", "seq", None), P(None, "dp", "seq"), P(None, "dp", "seq", None),
        P(), P(), P(None, "dp"), P(), P(), P("dp", None), P(None, "dp"), P(None, "dp"), P("dp", None),
        P(), P(None, "dp"), P(), P(), P(), P(), P("dp", None), P(),
        P(), P(None, "dp"), P(), P(None, "dp"), P("dp", None), P(),
    )
    out_specs = (
        P(None, "dp", "seq", None), P(None, "dp", "seq", None), P(both), P(both),
        P("seq", "dp"), P(both, None), P(both, None), P("dp", "seq"), P("seq", "dp"), P("seq", "dp"), P("dp", "seq"),
        P(both, None), P("seq", "dp"), P(both, None), P(both, None), P(both, None), P(both, None),
        P("dp", "seq"), P(both, None), P(both, None), P("seq", "dp"), P(both, None), P("seq", "dp"),
        P("dp", "seq"), P(both, None),
    )
    return jax.shard_map(
        lambda *args: local(topo, *args), mesh=mesh, in_specs=in_specs, out_specs=out_specs, check_vma=False
    )
```
